32 devices in a mesh: grp: 4 (over x, core), mem: 4 (over z), pair: 2 (over y).
Axes of the slice: x: 2, y: 2, z: 4, core: 2. Of those that a mesh axis runs over, the one named last changes fastest.
Arguments:
- voltages: bfloat16 [1024, 2, 71680], P(('grp', 'mem'), 'pair'), may hold values from -6 to 6
- gain_table: float32 [64, 2, 1024], P(None, None, 'mem'), may hold values from -4.2 to 4.2
- gain_index: int32 [1024, 2], replicated, may hold values from 0 to 63
- cylinder_map: int32 [1024], replicated, may hold values from 0 to 1023, each once
- delays: int32 [32, 1024], replicated, may hold values from 0 to 31
- chan_map: int32 [1024], replicated, may hold values from 0 to 1023, each once
Outputs:
- dedispersed: float32 [2, 512, 32, 32], P('pair', ('grp', 'mem'))
The draws below stay inside these ranges and needn't reach their ends.
Inputs may be any that keep to these rules, and one draw needn't show every extreme that they name: `cylinder_map`: each of 0 to 1023 appears once. `chan_map`: each of 0 to 1023 appears once.
All inputs are finite; a program needn't handle non-finite values.
Results may differ from the reference program's by a relative error of at most 0.011.
Values may be sent and summed in bfloat16 or wider, within the bound.
A program may use at most 128 MiB of HBM per device.

```python
import math
import jax
import jax.numpy as jnp
from jax import lax

NFFT = 2048
CHANS = 1024
TAPS = 4
CYL = 4
NS = 256
POLS = 2
FEEDS = 1024
BEAMS = 1024
TIMES = 32
SAMPLES = 71680
TRIALS = 32
GAIN_ROWS = 64


def touch_ends(result, key, low, top_value):
    longest = result.shape.index(max(result.shape))
    spots = []
    for shift in (0, 1):
        where = [jax.random.randint(jax.random.fold_in(key, axis), (), 0, length) for axis, length in enumerate(result.shape)]
        where[longest] = (where[longest] + shift) % result.shape[longest]
        spots.append(tuple(where))
    return result.at[spots[0]].set(low).at[spots[1]].set(top_value)


def level_of(key, shape, cuts, low, largest):
    gain = 1.0
    for dim, shards_of in cuts:
        heights = jax.random.uniform(jax.random.fold_in(jax.random.fold_in(key, 6), dim), (shards_of,), jnp.float32, low / len(cuts), largest / len(cuts))
        gain = gain * jnp.repeat(jnp.exp(heights), shape[dim] // shards_of).reshape((-1,) + (1,) * (len(shape) - 1 - dim))
    return gain


def noise(stream_key, dims, scale, limit, split=(), held_as=jnp.bfloat16):
    factor_of = level_of(stream_key, dims, split, -0.22, 0.18) if split else 1.0
    entries = jax.random.normal(stream_key, dims, jnp.float32) * scale * factor_of
    return jnp.minimum(jnp.maximum(entries, -limit), limit).astype(held_as)


def setup_inputs(seed: int = 0) -> dict:
    seeds = jax.random.split(jax.random.key(seed), 7)
    voltages = noise(seeds[0], (FEEDS, POLS, SAMPLES), 1.0, 6.0, ((0, 16), (1, 2)))
    gain_table = noise(seeds[1], (GAIN_ROWS, 2, CHANS), 0.7, 4.2, ((2, 4),), jnp.float32)
    gain_index = touch_ends(jax.random.randint(seeds[2], (FEEDS, POLS), 0, GAIN_ROWS), jax.random.fold_in(seeds[2], 1), 0, GAIN_ROWS - 1).astype(jnp.int32)
    cylinder_map = jax.random.permutation(seeds[3], FEEDS).astype(jnp.int32)
    delays = touch_ends(jax.random.randint(seeds[4], (TRIALS, CHANS), 0, TIMES), jax.random.fold_in(seeds[4], 1), 0, TIMES - 1).astype(jnp.int32)
    chan_map = jax.random.permutation(seeds[5], CHANS).astype(jnp.int32)
    return {"voltages": voltages, "gain_table": gain_table, "gain_index": gain_index, "cylinder_map": cylinder_map, "delays": delays, "chan_map": chan_map}


HIGHEST_PRECISION = lax.Precision.HIGHEST

def pfb_window(tap_count, length):
    offsets = jnp.arange(tap_count * length, dtype=jnp.float32) + 0.5
    shaped = jnp.sinc((offsets - tap_count * length / 2.0) / length)
    taper_term = 0.5 - 0.5 * jnp.cos(offsets * (2.0 * math.pi / (tap_count * length)))
    return (shaped * taper_term).reshape(tap_count, length)

def channel_table(length, start_col, columns):
    samples = jnp.arange(length, dtype=jnp.int32)[:, None]
    channels = start_col + jnp.arange(columns, dtype=jnp.int32)[None, :]
    turns_int = samples * channels % length
    angles = turns_int.astype(jnp.float32) * (2.0 * math.pi / length)
    return (jnp.cos(angles).astype(jnp.bfloat16), (-jnp.sin(angles)).astype(jnp.bfloat16))

def frame_signal(volt_rows, window):
    leading = volt_rows.shape[0]
    frames = volt_rows.reshape(leading, TIMES + TAPS - 1, NFFT).astype(jnp.float32)
    framed = frames[:, 0:TIMES] * window[0]
    for tap_index in range(1, TAPS):
        framed = framed + frames[:, tap_index:tap_index + TIMES] * window[tap_index]
    return framed.astype(jnp.bfloat16).reshape(leading * TIMES, NFFT)

def beam_table(length):
    samples = jnp.arange(length, dtype=jnp.int32).reshape(length, 1, 1)
    beam_index = jnp.arange(length, dtype=jnp.int32).reshape(length // 2, 2).T.reshape(1, 2, length // 2)
    turns_int = samples * beam_index % length
    angles = turns_int.astype(jnp.float32) * (2.0 * math.pi / length)
    cosine = jnp.cos(angles).astype(jnp.bfloat16)
    sine_part = jnp.sin(angles).astype(jnp.bfloat16)
    first_row = jnp.stack([cosine, -sine_part], axis=1)
    second_row = jnp.stack([sine_part, cosine], axis=1)
    return jnp.stack([first_row, second_row], axis=1)

def beam_power(ns_real, ns_imag, feed_total):
    cylinders = ns_real.shape[1]
    indices = jnp.arange(cylinders, dtype=jnp.int32)
    turns_int = indices[:, None] * indices[None, :] % cylinders
    angles = turns_int.astype(jnp.float32) * (2.0 * math.pi / cylinders)
    cosine = jnp.cos(angles)
    sine_table = jnp.sin(angles)
    beam_real = jnp.einsum('ec,lchq->lehq', cosine, ns_real, precision=HIGHEST_PRECISION) + jnp.einsum('ec,lchq->lehq', sine_table, ns_imag, precision=HIGHEST_PRECISION)
    beam_imag = jnp.einsum('ec,lchq->lehq', cosine, ns_imag, precision=HIGHEST_PRECISION) - jnp.einsum('ec,lchq->lehq', sine_table, ns_real, precision=HIGHEST_PRECISION)
    return (beam_real * beam_real + beam_imag * beam_imag) * (1.0 / feed_total)

def time_tables(length):
    indices = jnp.arange(length, dtype=jnp.int32)
    turns_int = indices[:, None] * indices[None, :] % length
    angles = turns_int.astype(jnp.float32) * (2.0 * math.pi / length)
    return (jnp.cos(angles), jnp.sin(angles))

def dedisperse(intensity, delays, chan_map):
    values = intensity.astype(jnp.float32)
    centred = values - lax.optimization_barrier(jnp.mean(values, axis=1, keepdims=True))
    cosine, sine_table = time_tables(TIMES)
    spec_real = jnp.einsum('btc,tk->bkc', centred, cosine, precision=HIGHEST_PRECISION).astype(jnp.bfloat16)
    spec_imag = (-jnp.einsum('btc,tk->bkc', centred, sine_table, precision=HIGHEST_PRECISION)).astype(jnp.bfloat16)
    trial_delay = jnp.take(delays, chan_map, axis=1)
    wave_index = jnp.arange(TIMES, dtype=jnp.int32)
    turns_int = wave_index[:, None, None] * trial_delay[None] % TIMES
    angles = turns_int.astype(jnp.float32) * (2.0 * math.pi / TIMES)
    phase_real = jnp.cos(angles).astype(jnp.bfloat16).astype(jnp.float32)
    phase_imag = (-jnp.sin(angles)).astype(jnp.bfloat16).astype(jnp.float32)
    spec_real = spec_real.astype(jnp.float32)
    spec_imag = spec_imag.astype(jnp.float32)
    trial_real = jnp.einsum('bkc,kjc->bkj', spec_real, phase_real, precision=HIGHEST_PRECISION) - jnp.einsum('bkc,kjc->bkj', spec_imag, phase_imag, precision=HIGHEST_PRECISION)
    trial_imag = jnp.einsum('bkc,kjc->bkj', spec_real, phase_imag, precision=HIGHEST_PRECISION) + jnp.einsum('bkc,kjc->bkj', spec_imag, phase_real, precision=HIGHEST_PRECISION)
    scale_out = 1.0 / (TIMES * math.sqrt(CHANS))
    series = jnp.einsum('bkj,kt->bjt', trial_real, cosine, precision=HIGHEST_PRECISION) - jnp.einsum('bkj,kt->bjt', trial_imag, sine_table, precision=HIGHEST_PRECISION)
    return series * scale_out

def reference(voltages, gain_table, gain_index, cylinder_map, delays, chan_map):
    window = pfb_window(TAPS, NFFT)
    cos_table, sin_table = channel_table(NFFT, 0, CHANS)
    scale_dft = 1.0 / math.sqrt(NFFT)
    group_size = 32
    grouped = voltages.reshape(FEEDS // group_size, group_size * POLS, SAMPLES)

    def channelize(volt_rows):
        framed = frame_signal(volt_rows, window)
        real_part = jnp.dot(framed, cos_table, preferred_element_type=jnp.float32) * scale_dft
        imag_part = jnp.dot(framed, sin_table, preferred_element_type=jnp.float32) * scale_dft
        stacked = jnp.stack([real_part, imag_part], axis=0).astype(jnp.bfloat16)
        return stacked.reshape(2, group_size * POLS, TIMES, CHANS)
    spectra = lax.map(channelize, grouped)
    spectra = jnp.moveaxis(spectra, 1, 0).reshape(2, FEEDS, POLS, TIMES, CHANS)
    ordered = jnp.take(spectra, cylinder_map, axis=1)
    ordered = jnp.moveaxis(ordered, 3, 0)
    gain_rows = jnp.take(gain_index, cylinder_map, axis=0)
    gain_values = jnp.take(gain_table, gain_rows, axis=0)
    gain_real = gain_values[:, :, 0]
    gain_imag = gain_values[:, :, 1]
    ns_table = beam_table(NS).astype(jnp.float32)

    def form_beams(time_slab):
        volt_real = time_slab[0].astype(jnp.float32)
        volt_imag = time_slab[1].astype(jnp.float32)
        cal_real = volt_real * gain_real - volt_imag * gain_imag
        cal_imag = volt_real * gain_imag + volt_imag * gain_real
        cal_grid = lax.optimization_barrier(jnp.stack([cal_real, cal_imag], axis=0).astype(jnp.bfloat16))
        cal_grid = cal_grid.astype(jnp.float32).reshape(2, CYL, NS, POLS, CHANS)
        ns_beams = jnp.einsum('rcnpl,nrsah->spachl', cal_grid, ns_table, precision=HIGHEST_PRECISION)
        half_beams = NS // 2
        powers = beam_power(ns_beams[0].reshape(POLS * 2, CYL, half_beams, CHANS), ns_beams[1].reshape(POLS * 2, CYL, half_beams, CHANS), FEEDS)
        powers = powers.reshape(POLS, 2, CYL, half_beams, CHANS)
        return (powers[0] + powers[1]).astype(jnp.bfloat16)
    intensity = lax.map(form_beams, ordered)
    intensity = jnp.transpose(intensity, (1, 2, 3, 0, 4)).reshape(BEAMS, TIMES, CHANS)
    series = dedisperse(intensity, delays, chan_map)
    return series.reshape(2, BEAMS // 2, TRIALS, TIMES)
```

```python
import functools
import math

import jax
import jax.numpy as jnp
from jax import lax
from jax.experimental import pallas as pl
from jax.experimental.pallas import tpu as pltpu
from jax.sharding import PartitionSpec as P

NFFT = 2048
CHANS = 1024
TAPS = 4
CYL = 4
NS = 256
FEEDS = 1024
BEAMS = 1024
TIMES = 32
TRIALS = 32
PEERS = ("grp", "mem")
LANES = 128


def pfb_window(tap_count, length):
    offsets = jnp.arange(tap_count * length, dtype=jnp.float32) + 0.5
    shaped = jnp.sinc((offsets - tap_count * length / 2.0) / length)
    taper_term = 0.5 - 0.5 * jnp.cos(offsets * (2.0 * math.pi / (tap_count * length)))
    return (shaped * taper_term).reshape(tap_count, length)


def turn(index, length):
    angles = (index % length).astype(jnp.float32) * (2.0 * math.pi / length)
    return lax.optimization_barrier((jnp.cos(angles), jnp.sin(angles)))


def times(a, b):
    return (a[0] * b[0] - a[1] * b[1], a[0] * b[1] + a[1] * b[0])


def channel_table(chan_of, quarter):
    chan = chan_of[None, :]
    high = turn(jnp.arange(16, dtype=jnp.int32)[:, None] * 128 * chan, NFFT)
    mid = turn(jnp.arange(16, dtype=jnp.int32)[:, None] * 8 * chan, NFFT)
    low = turn(jnp.arange(8, dtype=jnp.int32)[:, None] * chan + quarter[None, :] * (NFFT // 4), NFFT)
    upper = times([p[:, None, :] for p in high], [p[None, :, :] for p in mid])
    upper = lax.optimization_barrier(tuple(p.reshape(NFFT // 8, 1, -1) for p in upper))
    table = upper[0] * low[0][None] - upper[1] * low[1][None]
    return table.astype(jnp.bfloat16).reshape(NFFT, -1)


def beam_weights(cylinder_map):
    slots = jnp.arange(FEEDS, dtype=jnp.int32)
    hit = cylinder_map[:, None] == slots[None, :]
    slot_of = jnp.sum(jnp.where(hit, slots[:, None], 0), axis=0)
    cyl, pos = slot_of // NS, slot_of % NS
    e = jnp.arange(CYL, dtype=jnp.int32).reshape(CYL, 1, 1)
    hh = jnp.arange(16, dtype=jnp.int32).reshape(1, 16, 1)
    upper = turn(16 * pos * hh + (NS // CYL) * e * cyl, NS)
    a = jnp.arange(2, dtype=jnp.int32).reshape(2, 1, 1)
    hl = jnp.arange(8, dtype=jnp.int32).reshape(1, 8, 1)
    lower = turn(pos * (2 * hl + a), NS)
    real, imag = times(
        [p[None, :, :, None, :] for p in upper], [p[:, None, None, :, :] for p in lower]
    )
    return jnp.concatenate(
        [p.astype(jnp.bfloat16).reshape(BEAMS, FEEDS) for p in (real, imag)], axis=1
    )


BEAM_VMEM = 40
DFT_VMEM = 40
CHUNKS = (8, 20, 4)


def dft_kernel(frames, feeds, window_ref, volt_ref, table_ref, out_ref, framed_ref):
    @pl.when(pl.program_id(0) == 0)
    def _():
        for t in range(frames):
            total = volt_ref[:, t * NFFT : (t + 1) * NFFT].astype(jnp.float32) * window_ref[0:1, :]
            for j in range(1, TAPS):
                tap = volt_ref[:, (t + j) * NFFT : (t + j + 1) * NFFT].astype(jnp.float32)
                total = total + tap * window_ref[j : j + 1, :]
            framed_ref[t * feeds : (t + 1) * feeds, :] = total.astype(jnp.bfloat16)

    part = jnp.dot(framed_ref[...], table_ref[...], preferred_element_type=jnp.float32)
    part = (part * (1.0 / math.sqrt(NFFT))).astype(jnp.bfloat16)
    for i in range(out_ref.shape[0]):
        out_ref[i] = part[:, i * LANES : (i + 1) * LANES].reshape(frames, feeds, LANES)


def dft_stage(voltages, window, table, start, frames, peers):
    feeds = voltages.shape[0]
    length = (frames + TAPS - 1) * NFFT
    volt = lax.slice_in_dim(voltages, start * NFFT, start * NFFT + length, axis=2)
    volt = volt.reshape(feeds, length)
    width = table.shape[1] // peers
    if width != LANES:
        view = volt.reshape(feeds, frames + TAPS - 1, NFFT).astype(jnp.float32)
        framed = view[:, 0:frames] * window[0]
        for j in range(1, TAPS):
            framed = framed + view[:, j : j + frames] * window[j]
        rows = jnp.swapaxes(framed.astype(jnp.bfloat16), 0, 1).reshape(frames * feeds, NFFT)
        part = jnp.dot(rows, table, preferred_element_type=jnp.float32) * (1.0 / math.sqrt(NFFT))
        part = part.astype(jnp.bfloat16).reshape(frames, feeds, peers, width)
        return jnp.moveaxis(part, 2, 0)
    step = 4
    return pl.pallas_call(
        functools.partial(dft_kernel, frames, feeds),
        grid=(peers // step,),
        out_shape=jax.ShapeDtypeStruct((peers, frames, feeds, width), jnp.bfloat16),
        in_specs=[
            pl.BlockSpec((TAPS, NFFT), lambda i: (0, 0)),
            pl.BlockSpec((feeds, length), lambda i: (0, 0)),
            pl.BlockSpec((NFFT, step * width), lambda i: (0, i)),
        ],
        out_specs=pl.BlockSpec((step, frames, feeds, width), lambda i: (i, 0, 0, 0)),
        scratch_shapes=[pltpu.VMEM((frames * feeds, NFFT), jnp.bfloat16)],
        compiler_params=pltpu.CompilerParams(
            dimension_semantics=("arbitrary",), vmem_limit_bytes=DFT_VMEM * 1024 * 1024
        ),
    )(window, volt, table)


HIT = (TIMES - 1) / (TIMES * TIMES)
MISS = -1.0 / (TIMES * TIMES)


def beam_kernel(start, frames, chans, r_ref, ga_ref, gb_ref, w_ref, e_ref, *rest):
    acc_ref = rest[0] if len(rest) == 6 else None
    out_ref, even_ref, odd_ref, t_ref, p_ref = rest[-5:]
    width = 2 * chans
    lane = lax.broadcasted_iota(jnp.int32, (FEEDS, width), 1)
    sign = jnp.where(lane < chans, 1.0, -1.0)
    low = lax.broadcasted_iota(jnp.int32, (BEAMS, width), 1) < chans

    def calibrate(pair, x_ref):
        for u in range(2):
            i = 2 * pair + u
            volt = r_ref[:, i].reshape(FEEDS, width).astype(jnp.float32)
            cal = volt * ga_ref[...] + pltpu.roll(volt, chans, 1) * gb_ref[...]
            turned = pltpu.roll(cal, chans, 1) * sign
            cols = slice(u * width, (u + 1) * width)
            x_ref[0:FEEDS, cols] = cal.astype(jnp.bfloat16)
            x_ref[FEEDS : 2 * FEEDS, cols] = turned.astype(jnp.bfloat16)
            hit = e_ref[...] == start + i
            rows = pl.ds(pl.multiple_of(i * chans, chans), chans)
            t_ref[rows, :] = jnp.where(hit, HIT, MISS).astype(jnp.bfloat16)

    def form(pair, x_ref):
        beams = jnp.dot(w_ref[...], x_ref[...], preferred_element_type=jnp.float32)
        squares = beams * beams
        one, two = squares[:, :width], squares[:, width:]
        first = one + pltpu.roll(one, chans, 1)
        second = two + pltpu.roll(two, chans, 1)
        power = jnp.where(low, first, second) * (1.0 / FEEDS)
        p_ref[:, pl.ds(pl.multiple_of(pair * width, width), width)] = power.astype(jnp.bfloat16)

    pairs = frames // 2
    calibrate(0, even_ref)

    def body(k, carry):
        form(2 * k, even_ref)
        calibrate(2 * k + 1, odd_ref)
        form(2 * k + 1, odd_ref)
        calibrate(jnp.minimum(2 * k + 2, pairs - 1), even_ref)
        return carry

    lax.fori_loop(0, pairs // 2, body, 0)
    if pairs % 2:
        form(pairs - 1, even_ref)
    part = jnp.dot(p_ref[...], t_ref[...], preferred_element_type=jnp.float32)
    if acc_ref is not None:
        part = part + acc_ref[...]
    out_ref[...] = part.astype(out_ref.dtype)


def beam_stage(received, gains, weights, shift, start, acc):
    _, frames, _, width = received.shape
    chans = width // 2
    last = start + frames == TIMES
    held = jnp.bfloat16 if last else jnp.float32
    if width != LANES:
        volt = jnp.moveaxis(received, 1, 0).reshape(frames, FEEDS, 2, chans).astype(jnp.float32)
        ga, gb = (g.reshape(FEEDS, 2, chans) for g in gains)
        cal = (volt * ga + volt[:, :, ::-1] * gb).astype(jnp.bfloat16)
        turned = jnp.stack([cal[:, :, 1], -cal[:, :, 0]], axis=2)
        both = jnp.concatenate([cal, turned], axis=1)
        beams = jnp.einsum("bf,tfrc->btrc", weights, both, preferred_element_type=jnp.float32)
        power = jnp.sum(beams * beams, axis=2) * (1.0 / FEEDS)
        power = power.astype(jnp.bfloat16).reshape(BEAMS, frames * chans)
        frame = start + jnp.arange(frames, dtype=jnp.int32)[:, None, None]
        spread = jnp.where(shift[None] == frame, HIT, MISS).astype(jnp.bfloat16)
        spread = spread.reshape(frames * chans, -1)
        part = jnp.dot(power, spread, preferred_element_type=jnp.float32)
        return (part if acc is None else part + acc).astype(held)
    series = TRIALS * TIMES
    operands = (received, *gains, weights, shift) + (() if acc is None else (acc,))
    return pl.pallas_call(
        functools.partial(beam_kernel, start, frames, chans),
        out_shape=jax.ShapeDtypeStruct((BEAMS, series), held),
        in_specs=[pl.BlockSpec(memory_space=pltpu.VMEM)] * len(operands),
        out_specs=pl.BlockSpec(memory_space=pltpu.VMEM),
        scratch_shapes=[
            pltpu.VMEM((2 * FEEDS, 2 * width), jnp.bfloat16),
            pltpu.VMEM((2 * FEEDS, 2 * width), jnp.bfloat16),
            pltpu.VMEM((frames * chans, series), jnp.bfloat16),
            pltpu.VMEM((BEAMS, frames * chans), jnp.bfloat16),
        ],
        compiler_params=pltpu.CompilerParams(vmem_limit_bytes=BEAM_VMEM * 1024 * 1024),
    )(*operands)


def local(voltages, gain_table, gain_index, cylinder_map, delays, chan_map):
    feeds = voltages.shape[0]
    grp_count, mem_count = lax.axis_size("grp"), lax.axis_size("mem")
    peers = grp_count * mem_count
    chans = CHANS // peers
    grp, mem = lax.axis_index("grp"), lax.axis_index("mem")

    window = pfb_window(TAPS, NFFT)
    peer = jnp.arange(peers, dtype=jnp.int32)
    base = peer % mem_count * (CHANS // mem_count) + peer // mem_count * chans
    chan_of = base[:, None, None] + jnp.arange(chans, dtype=jnp.int32)[None, None, :]
    quarter = jnp.arange(2, dtype=jnp.int32)[None, :, None]
    chan_of, quarter = (
        jnp.broadcast_to(v, (peers, 2, chans)).reshape(-1) for v in (chan_of, quarter)
    )
    table = channel_table(chan_of, quarter)

    table = lax.optimization_barrier(table)
    starts = [sum(CHUNKS[:i]) for i in range(len(CHUNKS))]

    def exchange(spectra):
        return lax.all_to_all(spectra, PEERS, split_axis=0, concat_axis=0, tiled=True)

    spectra = [
        dft_stage(voltages, window, table, start, frames, peers)
        for start, frames in zip(starts, CHUNKS)
    ]
    received = [exchange(block) for block in spectra[:-1]]

    pairs = lax.axis_size("pair")
    cores = 2 if grp_count % 2 == 0 else 1
    owned = BEAMS // (pairs * peers)
    weights = beam_weights(cylinder_map)
    weights = weights.reshape(pairs, grp_count // cores, cores, mem_count * owned, 2 * FEEDS)
    weights = jnp.moveaxis(weights, 2, 0).reshape(BEAMS, 2 * FEEDS)
    gain_here = lax.dynamic_slice_in_dim(gain_table, grp * chans, chans, 2)
    gain_rows = gain_index[:, lax.axis_index("pair")]
    pick = gain_rows[:, None] == jnp.arange(gain_table.shape[0], dtype=jnp.int32)[None, :]
    gain_values = jnp.dot(
        pick.astype(jnp.float32),
        gain_here.reshape(gain_table.shape[0], 2 * chans),
        precision=lax.Precision.HIGHEST,
    )
    gain_real, gain_imag = gain_values[:, :chans], gain_values[:, chans:]
    gains = (
        jnp.concatenate([gain_real, gain_real], axis=1),
        jnp.concatenate([-gain_imag, gain_imag], axis=1),
    )

    first = mem * (CHANS // mem_count) + grp * chans
    freq = lax.dynamic_slice_in_dim(chan_map, first, chans, 0)
    column = jnp.arange(CHANS, dtype=jnp.int32)[:, None] == freq[None, :]
    delay = jnp.dot(
        delays.astype(jnp.bfloat16), column.astype(jnp.bfloat16), preferred_element_type=jnp.float32
    ).astype(jnp.int32)
    frame = jnp.arange(TIMES, dtype=jnp.int32)[None, None, :]
    shift = ((frame - delay.T[:, :, None]) % TIMES).reshape(chans, TRIALS * TIMES)

    part = None
    for i, start in enumerate(starts):
        if i == len(starts) - 1:
            last, part = lax.optimization_barrier((spectra[-1], held))
            received.append(exchange(last))
            part = beam_stage(received[i - 1], gains, weights, shift, starts[i - 1], part)
        if i == len(starts) - 2:
            held = part
            continue
        part = beam_stage(received[i], gains, weights, shift, start, part)

    series = TRIALS * TIMES
    groups = [[x * cores + c for c in range(cores)] for x in range(grp_count // cores)]
    part = part.reshape(cores, BEAMS // cores, series)
    part = lax.all_to_all(
        part, "grp", split_axis=0, concat_axis=0, axis_index_groups=groups, tiled=True
    )
    part = jnp.sum(part.astype(jnp.float32), axis=0).astype(jnp.bfloat16)
    part = part.reshape(pairs * peers // cores, owned, series)
    groups = [
        [
            (p * grp_count + x * cores + c) * mem_count + m
            for p in range(pairs)
            for x in range(grp_count // cores)
            for m in range(mem_count)
        ]
        for c in range(cores)
    ]
    part = lax.all_to_all(
        part, ("pair",) + PEERS, split_axis=0, concat_axis=0, axis_index_groups=groups, tiled=True
    )
    series = jnp.sum(part.astype(jnp.float32), axis=0)
    return series.reshape(1, owned, TRIALS, TIMES)

GROUP = 4
STEP = 2
FUSED_VMEM = 62


def fused_kernel(
    sizes, window_ref, ga_ref, gb_ref, shift_ref, volt_hbm, table_hbm, weights_hbm, out_ref,
    volt_ref, table_ref, w_ref, framed_ref, send_ref, recv_ref, x_ref, psend_ref, precv_ref,
    t_ref, lhs_ref, acc_ref, zsend_ref, zrecv_ref,
    head_sem, volt_sem, table_sem, w_sem, send_sem, recv_sem, own_sem,
    psend_sem, precv_sem, pown_sem, zsend_sem, zrecv_sem,
):
    grp_count, mem_count, pairs, cores = sizes
    peers = grp_count * mem_count
    chips = peers // cores
    feeds = volt_hbm.shape[0]
    chans = LANES // 2
    width = LANES
    chunks = TIMES // GROUP
    steps = GROUP // STEP
    grp, mem, pair = (lax.axis_index(n) for n in ("grp", "mem", "pair"))
    me = grp * mem_count + mem
    across = pair * grp_count + grp
    MESH = pl.DeviceIdType.MESH

    def load(src, dst, sem):
        return pltpu.make_async_copy(src, dst, sem)

    head = (TAPS - 1) * NFFT
    load(volt_hbm.at[:, 0:head], volt_ref.at[:, 0:head], head_sem).start()

    def volt_copy(k):
        cols = pl.ds(pl.multiple_of(head + k * (GROUP * NFFT), NFFT), GROUP * NFFT)
        return load(volt_hbm.at[:, cols], volt_ref.at[:, cols], volt_sem.at[k])

    def table_copy(chip):
        cols = pl.ds(pl.multiple_of(chip * (cores * width), cores * width), cores * width)
        return load(table_hbm.at[:, cols], table_ref.at[chip], table_sem.at[chip])

    volt_copy(0).start()
    for chip in range(chips):
        table_copy(chip).start()
    for k in range(1, chunks):
        volt_copy(k).start()
    load(weights_hbm, w_ref, w_sem).start()

    barrier = pltpu.get_barrier_semaphore()
    met = 0
    for dg in range(grp_count):
        for dm in range(mem_count):
            for dp in range(pairs):
                if (dg, dm, dp) == (0, 0, 0) or (dm != 0 and dp != 0):
                    continue
                there = {
                    "grp": (grp + dg) % grp_count,
                    "mem": (mem + dm) % mem_count,
                    "pair": (pair + dp) % pairs,
                }
                pl.semaphore_signal(barrier, inc=1, device_id=there, device_id_type=MESH)
                met += 1
    pl.semaphore_wait(barrier, met)

    acc_ref[...] = jnp.zeros_like(acc_ref)
    load(volt_hbm.at[:, 0:head], volt_ref.at[:, 0:head], head_sem).wait()

    def main_copy(q, g, m):
        peer = g * mem_count + m
        return pltpu.make_async_remote_copy(
            src_ref=send_ref.at[q, peer],
            dst_ref=recv_ref.at[q, me],
            send_sem=send_sem.at[q],
            recv_sem=recv_sem.at[q],
            device_id={"grp": g, "mem": m},
            device_id_type=MESH,
        )

    def own_copy(q):
        return load(send_ref.at[q, me], recv_ref.at[q, me], own_sem.at[q])

    x_here = grp // cores

    def dft(k):
        volt_copy(k).wait()
        for t in range(GROUP):
            def tap(j):
                at = pl.multiple_of((k * GROUP + t + j) * NFFT, NFFT)
                return volt_ref[:, pl.ds(at, NFFT)].astype(jnp.float32) * window_ref[j : j + 1, :]

            total = tap(0)
            for j in range(1, TAPS):
                total = total + tap(j)
            framed_ref[t * feeds : (t + 1) * feeds, :] = total.astype(jnp.bfloat16)

        def tile(s, carry):
            h = s // 2
            far = (mem + 2) % 4 * ((3 - h) // 3) + (3 - mem) * (h % 3 % 2)
            near = (mem + 1 - 2 * (mem % 2)) * (h % 3 // 2) + mem * (h // 3)
            m = far + near
            x = (x_here + s + 1) % 2
            chip = x * mem_count + m

            @pl.when(k == 0)
            def _():
                table_copy(chip).wait()

            part = jnp.dot(framed_ref[...], table_ref[chip], preferred_element_type=jnp.float32)
            part = (part * (1.0 / math.sqrt(NFFT))).astype(jnp.bfloat16)
            for c in range(cores):
                g = x * cores + c
                peer = g * mem_count + m
                for u in range(steps):
                    q = k * steps + u
                    rows = part[u * STEP * feeds : (u + 1) * STEP * feeds, c * width : (c + 1) * width]
                    send_ref[q, peer] = rows.reshape(STEP, feeds, width)

                @pl.when(peer != me)
                def _():
                    for u in range(steps):
                        main_copy(k * steps + u, g, m).start()

                @pl.when(peer == me)
                def _():
                    for u in range(steps):
                        own_copy(k * steps + u).start()

            return carry

        lax.fori_loop(0, chips, tile, 0)

    lane = lax.broadcasted_iota(jnp.int32, (FEEDS, width), 1)
    sign = jnp.where(lane < chans, 1.0, -1.0)
    low = lax.broadcasted_iota(jnp.int32, (BEAMS, width), 1) < chans
    rows_each = BEAMS // (pairs * grp_count)

    def arrived(q):
        others = recv_ref.at[q, pl.ds(0, peers - 1)]
        return load(others, others, recv_sem.at[q])

    def left(q):
        others = send_ref.at[q, pl.ds(0, peers - 1)]
        return load(others, others, send_sem.at[q])

    def power_copy(q, p, g):
        d = p * grp_count + g
        block = pl.ds(pl.multiple_of(d * rows_each, rows_each), rows_each)
        return pltpu.make_async_remote_copy(
            src_ref=psend_ref.at[q, block],
            dst_ref=precv_ref.at[q, across],
            send_sem=psend_sem.at[q],
            recv_sem=precv_sem.at[q],
            device_id={"pair": p, "grp": g},
            device_id_type=MESH,
        )

    def power_own(q):
        block = pl.ds(pl.multiple_of(across * rows_each, rows_each), rows_each)
        return load(psend_ref.at[q, block], precv_ref.at[q, across], pown_sem.at[q])

    others_count = pairs * grp_count - 1

    def power_arrived(q):
        others = precv_ref.at[q, pl.ds(0, others_count)]
        return load(others, others, precv_sem.at[q])

    def power_left(q):
        others = psend_ref.at[q, pl.ds(0, others_count * rows_each)]
        return load(others, others, psend_sem.at[q])

    def beams(q):
        arrived(q).wait()
        own_copy(q).wait()
        for u in range(STEP):
            volt = recv_ref[q, :, u].reshape(FEEDS, width).astype(jnp.float32)
            cal = volt * ga_ref[...] + pltpu.roll(volt, chans, 1) * gb_ref[...]
            turned = pltpu.roll(cal, chans, 1) * sign
            cols = slice(u * width, (u + 1) * width)
            x_ref[0:FEEDS, cols] = cal.astype(jnp.bfloat16)
            x_ref[FEEDS : 2 * FEEDS, cols] = turned.astype(jnp.bfloat16)
        formed = jnp.dot(w_ref[...], x_ref[...], preferred_element_type=jnp.float32)
        squares = formed * formed
        one, two = squares[:, :width], squares[:, width:]
        first = one + pltpu.roll(one, chans, 1)
        second = two + pltpu.roll(two, chans, 1)
        power = jnp.where(low, first, second) * (1.0 / FEEDS)
        psend_ref[q] = power.astype(jnp.bfloat16)
        for dp in range(pairs - 1, -1, -1):
            for dg in range(grp_count - 1, -1, -1):
                if dp == 0 and dg == 0:
                    power_own(q).start()
                else:
                    power_copy(q, (pair + dp) % pairs, (grp + dg) % grp_count).start()

    def dedisperse(q):
        for s in range(grp_count):
            for u in range(STEP):
                hit = shift_ref[s * chans : (s + 1) * chans, :] == q * STEP + u
                at = (s * STEP + u) * chans
                t_ref[at : at + chans, :] = jnp.where(hit, HIT, MISS).astype(jnp.bfloat16)
        power_arrived(q).wait()
        power_own(q).wait()
        for s in range(grp_count):
            both = precv_ref[q, s].astype(jnp.float32)
            for p in range(1, pairs):
                both = both + precv_ref[q, p * grp_count + s].astype(jnp.float32)
            lhs_ref[:, s * width : (s + 1) * width] = both.astype(jnp.bfloat16)
        acc_ref[...] += jnp.dot(lhs_ref[...], t_ref[...], preferred_element_type=jnp.float32)

    load(weights_hbm, w_ref, w_sem).wait()

    def body(i, carry):
        @pl.when(i < chunks)
        def _():
            dft(i)

        @pl.when(i >= 3)
        def _():
            lax.fori_loop(0, steps, lambda u, c: (dedisperse((i - 3) * steps + u), c)[1], 0)

        @pl.when(jnp.logical_and(i >= 2, i < chunks + 2))
        def _():
            lax.fori_loop(0, steps, lambda u, c: (beams((i - 2) * steps + u), c)[1], 0)

        return carry

    lax.fori_loop(0, chunks + 3, body, 0)

    owned = rows_each // mem_count
    zsend_ref[...] = acc_ref[...].astype(jnp.bfloat16)

    def z_copy(d):
        m = (mem + d) % mem_count
        return pltpu.make_async_remote_copy(
            src_ref=zsend_ref.at[pl.ds(pl.multiple_of(m * owned, owned), owned)],
            dst_ref=zrecv_ref.at[d - 1],
            send_sem=zsend_sem.at[d - 1],
            recv_sem=zrecv_sem.at[d - 1],
            device_id={"mem": m},
            device_id_type=MESH,
        )

    for d in range(1, mem_count):
        z_copy(d).start()

    def drain(q, carry):
        left(q).wait()
        power_left(q).wait()
        return carry

    lax.fori_loop(0, chunks * steps, drain, 0)
    total = acc_ref[pl.ds(pl.multiple_of(mem * owned, owned), owned), :]
    for d in range(1, mem_count):
        z_copy(d).wait()
        total = total + zrecv_ref[d - 1].astype(jnp.float32)
    out_ref[...] = total


def fused_stage(sizes, window, gains, shift, voltages, table, weights):
    grp_count, mem_count, pairs, cores = sizes
    peers = grp_count * mem_count
    chips = peers // cores
    feeds, samples = voltages.shape
    series = TRIALS * TIMES
    count = TIMES // STEP
    groups = pairs * grp_count
    rows_each = BEAMS // groups
    owned = rows_each // mem_count
    bf16, f32 = jnp.bfloat16, jnp.float32
    dma = pltpu.SemaphoreType.DMA
    vmem = pl.BlockSpec(memory_space=pltpu.VMEM)
    hbm = pl.BlockSpec(memory_space=pl.ANY)
    return pl.pallas_call(
        functools.partial(fused_kernel, sizes),
        out_shape=jax.ShapeDtypeStruct((owned, series), f32),
        in_specs=[vmem] * 4 + [hbm] * 3,
        out_specs=vmem,
        scratch_shapes=[
            pltpu.VMEM((feeds, samples), bf16),
            pltpu.VMEM((chips, NFFT, cores * LANES), bf16),
            pltpu.VMEM((BEAMS, 2 * FEEDS), bf16),
            pltpu.VMEM((GROUP * feeds, NFFT), bf16),
            pltpu.VMEM((count, peers, STEP, feeds, LANES), bf16),
            pltpu.VMEM((count, peers, STEP, feeds, LANES), bf16),
            pltpu.VMEM((2 * FEEDS, STEP * LANES), bf16),
            pltpu.VMEM((count, BEAMS, LANES), bf16),
            pltpu.VMEM((count, groups, rows_each, LANES), bf16),
            pltpu.VMEM((grp_count * LANES, series), bf16),
            pltpu.VMEM((rows_each, grp_count * LANES), bf16),
            pltpu.VMEM((rows_each, series), f32),
            pltpu.VMEM((rows_each, series), bf16),
            pltpu.VMEM((mem_count - 1, owned, series), bf16),
            dma,
            dma((TIMES // GROUP,)),
            dma((chips,)),
            dma,
            dma((count,)),
            dma((count,)),
            dma((count,)),
            dma((count,)),
            dma((count,)),
            dma((count,)),
            dma((mem_count - 1,)),
            dma((mem_count - 1,)),
        ],
        compiler_params=pltpu.CompilerParams(
            collective_id=0, has_side_effects=True, vmem_limit_bytes=FUSED_VMEM * 1024 * 1024
        ),
    )(window, *gains, shift, voltages, table, weights)


def local_fused(voltages, gain_table, gain_index, cylinder_map, delays, chan_map):
    feeds = voltages.shape[0]
    grp_count, mem_count = lax.axis_size("grp"), lax.axis_size("mem")
    pairs, cores = lax.axis_size("pair"), 2
    peers = grp_count * mem_count
    chans = CHANS // peers
    grp, mem = lax.axis_index("grp"), lax.axis_index("mem")
    window = pfb_window(TAPS, NFFT)

    peer = jnp.arange(peers, dtype=jnp.int32)
    peer_grp = peer // (mem_count * cores) * cores + peer % cores
    peer_mem = peer // cores % mem_count
    base = peer_mem * (CHANS // mem_count) + peer_grp * chans
    chan_of = base[:, None, None] + jnp.arange(chans, dtype=jnp.int32)[None, None, :]
    quarter = jnp.arange(2, dtype=jnp.int32)[None, :, None]
    chan_of, quarter = (
        jnp.broadcast_to(v, (peers, 2, chans)).reshape(-1) for v in (chan_of, quarter)
    )
    table = channel_table(chan_of, quarter)
    weights = beam_weights(cylinder_map)

    gain_here = lax.dynamic_slice_in_dim(gain_table, grp * chans, chans, 2)
    gain_rows = gain_index[:, lax.axis_index("pair")]
    pick = gain_rows[:, None] == jnp.arange(gain_table.shape[0], dtype=jnp.int32)[None, :]
    gain_values = jnp.dot(
        pick.astype(jnp.float32),
        gain_here.reshape(gain_table.shape[0], 2 * chans),
        precision=lax.Precision.HIGHEST,
    )
    gain_real, gain_imag = gain_values[:, :chans], gain_values[:, chans:]
    gains = (
        jnp.concatenate([gain_real, gain_real], axis=1),
        jnp.concatenate([-gain_imag, gain_imag], axis=1),
    )

    held = CHANS // mem_count
    freq = lax.dynamic_slice_in_dim(chan_map, mem * held, held, 0)
    column = jnp.arange(CHANS, dtype=jnp.int32)[:, None] == freq[None, :]
    delay = jnp.dot(
        delays.astype(jnp.bfloat16), column.astype(jnp.bfloat16), preferred_element_type=jnp.float32
    ).astype(jnp.int32)
    frame = jnp.arange(TIMES, dtype=jnp.int32)[None, None, :]
    shift = ((frame - delay.T[:, :, None]) % TIMES).reshape(held, TRIALS * TIMES)

    sizes = (grp_count, mem_count, pairs, cores)
    series = fused_stage(
        sizes, window, gains, shift, voltages.reshape(feeds, voltages.shape[2]), table, weights
    )
    return series.reshape(1, -1, TRIALS, TIMES)


def solution(mesh):
    shape = (mesh.shape["grp"], mesh.shape["mem"], mesh.shape["pair"])
    return jax.shard_map(
        local_fused if shape == (4, 4, 2) else local,
        mesh=mesh,
        in_specs=(P(PEERS, "pair", None), P(None, None, "mem"), P(), P(), P(), P()),
        out_specs=P("pair", PEERS, None, None),
        check_vma=False,
    )
```

```python
import functools
import math

import jax
import jax.numpy as jnp
from jax import lax
from jax.experimental import pallas as pl
from jax.experimental.pallas import tpu as pltpu
from jax.sharding import PartitionSpec as P

NFFT = 2048
CHANS = 1024
TAPS = 4
CYL = 4
NS = 256
FEEDS = 1024
BEAMS = 1024
TIMES = 32
TRIALS = 32
PEERS = ("grp", "mem")
LANES = 128


def pfb_window(tap_count, length):
    offsets = jnp.arange(tap_count * length, dtype=jnp.float32) + 0.5
    shaped = jnp.sinc((offsets - tap_count * length / 2.0) / length)
    taper_term = 0.5 - 0.5 * jnp.cos(offsets * (2.0 * math.pi / (tap_count * length)))
    return (shaped * taper_term).reshape(tap_count, length)


def turn(index, length):
    angles = (index % length).astype(jnp.float32) * (2.0 * math.pi / length)
    return lax.optimization_barrier((jnp.cos(angles), jnp.sin(angles)))


def times(a, b):
    return (a[0] * b[0] - a[1] * b[1], a[0] * b[1] + a[1] * b[0])


def channel_table(chan_of, quarter):
    chan = chan_of[None, :]
    high = turn(jnp.arange(16, dtype=jnp.int32)[:, None] * 128 * chan, NFFT)
    mid = turn(jnp.arange(16, dtype=jnp.int32)[:, None] * 8 * chan, NFFT)
    low = turn(jnp.arange(8, dtype=jnp.int32)[:, None] * chan + quarter[None, :] * (NFFT // 4), NFFT)
    upper = times([p[:, None, :] for p in high], [p[None, :, :] for p in mid])
    upper = lax.optimization_barrier(tuple(p.reshape(NFFT // 8, 1, -1) for p in upper))
    table = upper[0] * low[0][None] - upper[1] * low[1][None]
    return table.astype(jnp.bfloat16).reshape(NFFT, -1)


def beam_weights(cylinder_map):
    slots = jnp.arange(FEEDS, dtype=jnp.int32)
    hit = cylinder_map[:, None] == slots[None, :]
    slot_of = jnp.sum(jnp.where(hit, slots[:, None], 0), axis=0)
    cyl, pos = slot_of // NS, slot_of % NS
    e = jnp.arange(CYL, dtype=jnp.int32).reshape(CYL, 1, 1)
    hh = jnp.arange(16, dtype=jnp.int32).reshape(1, 16, 1)
    upper = turn(16 * pos * hh + (NS // CYL) * e * cyl, NS)
    a = jnp.arange(2, dtype=jnp.int32).reshape(2, 1, 1)
    hl = jnp.arange(8, dtype=jnp.int32).reshape(1, 8, 1)
    lower = turn(pos * (2 * hl + a), NS)
    real, imag = times(
        [p[None, :, :, None, :] for p in upper], [p[:, None, None, :, :] for p in lower]
    )
    return jnp.concatenate(
        [p.astype(jnp.bfloat16).reshape(BEAMS, FEEDS) for p in (real, imag)], axis=1
    )


BEAM_VMEM = 40
DFT_VMEM = 40
CHUNKS = (8, 20, 4)


def dft_kernel(frames, feeds, window_ref, volt_ref, table_ref, out_ref, framed_ref):
    @pl.when(pl.program_id(0) == 0)
    def _():
        for t in range(frames):
            total = volt_ref[:, t * NFFT : (t + 1) * NFFT].astype(jnp.float32) * window_ref[0:1, :]
            for j in range(1, TAPS):
                tap = volt_ref[:, (t + j) * NFFT : (t + j + 1) * NFFT].astype(jnp.float32)
                total = total + tap * window_ref[j : j + 1, :]
            framed_ref[t * feeds : (t + 1) * feeds, :] = total.astype(jnp.bfloat16)

    part = jnp.dot(framed_ref[...], table_ref[...], preferred_element_type=jnp.float32)
    part = (part * (1.0 / math.sqrt(NFFT))).astype(jnp.bfloat16)
    for i in range(out_ref.shape[0]):
        out_ref[i] = part[:, i * LANES : (i + 1) * LANES].reshape(frames, feeds, LANES)


def dft_stage(voltages, window, table, start, frames, peers):
    feeds = voltages.shape[0]
    length = (frames + TAPS - 1) * NFFT
    volt = lax.slice_in_dim(voltages, start * NFFT, start * NFFT + length, axis=2)
    volt = volt.reshape(feeds, length)
    width = table.shape[1] // peers
    if width != LANES:
        view = volt.reshape(feeds, frames + TAPS - 1, NFFT).astype(jnp.float32)
        framed = view[:, 0:frames] * window[0]
        for j in range(1, TAPS):
            framed = framed + view[:, j : j + frames] * window[j]
        rows = jnp.swapaxes(framed.astype(jnp.bfloat16), 0, 1).reshape(frames * feeds, NFFT)
        part = jnp.dot(rows, table, preferred_element_type=jnp.float32) * (1.0 / math.sqrt(NFFT))
        part = part.astype(jnp.bfloat16).reshape(frames, feeds, peers, width)
        return jnp.moveaxis(part, 2, 0)
    step = 4
    return pl.pallas_call(
        functools.partial(dft_kernel, frames, feeds),
        grid=(peers // step,),
        out_shape=jax.ShapeDtypeStruct((peers, frames, feeds, width), jnp.bfloat16),
        in_specs=[
            pl.BlockSpec((TAPS, NFFT), lambda i: (0, 0)),
            pl.BlockSpec((feeds, length), lambda i: (0, 0)),
            pl.BlockSpec((NFFT, step * width), lambda i: (0, i)),
        ],
        out_specs=pl.BlockSpec((step, frames, feeds, width), lambda i: (i, 0, 0, 0)),
        scratch_shapes=[pltpu.VMEM((frames * feeds, NFFT), jnp.bfloat16)],
        compiler_params=pltpu.CompilerParams(
            dimension_semantics=("arbitrary",), vmem_limit_bytes=DFT_VMEM * 1024 * 1024
        ),
    )(window, volt, table)


HIT = (TIMES - 1) / (TIMES * TIMES)
MISS = -1.0 / (TIMES * TIMES)


def beam_kernel(start, frames, chans, r_ref, ga_ref, gb_ref, w_ref, e_ref, *rest):
    acc_ref = rest[0] if len(rest) == 6 else None
    out_ref, even_ref, odd_ref, t_ref, p_ref = rest[-5:]
    width = 2 * chans
    lane = lax.broadcasted_iota(jnp.int32, (FEEDS, width), 1)
    sign = jnp.where(lane < chans, 1.0, -1.0)
    low = lax.broadcasted_iota(jnp.int32, (BEAMS, width), 1) < chans

    def calibrate(pair, x_ref):
        for u in range(2):
            i = 2 * pair + u
            volt = r_ref[:, i].reshape(FEEDS, width).astype(jnp.float32)
            cal = volt * ga_ref[...] + pltpu.roll(volt, chans, 1) * gb_ref[...]
            turned = pltpu.roll(cal, chans, 1) * sign
            cols = slice(u * width, (u + 1) * width)
            x_ref[0:FEEDS, cols] = cal.astype(jnp.bfloat16)
            x_ref[FEEDS : 2 * FEEDS, cols] = turned.astype(jnp.bfloat16)
            hit = e_ref[...] == start + i
            rows = pl.ds(pl.multiple_of(i * chans, chans), chans)
            t_ref[rows, :] = jnp.where(hit, HIT, MISS).astype(jnp.bfloat16)

    def form(pair, x_ref):
        beams = jnp.dot(w_ref[...], x_ref[...], preferred_element_type=jnp.float32)
        squares = beams * beams
        one, two = squares[:, :width], squares[:, width:]
        first = one + pltpu.roll(one, chans, 1)
        second = two + pltpu.roll(two, chans, 1)
        power = jnp.where(low, first, second) * (1.0 / FEEDS)
        p_ref[:, pl.ds(pl.multiple_of(pair * width, width), width)] = power.astype(jnp.bfloat16)

    pairs = frames // 2
    calibrate(0, even_ref)

    def body(k, carry):
        form(2 * k, even_ref)
        calibrate(2 * k + 1, odd_ref)
        form(2 * k + 1, odd_ref)
        calibrate(jnp.minimum(2 * k + 2, pairs - 1), even_ref)
        return carry

    lax.fori_loop(0, pairs // 2, body, 0)
    if pairs % 2:
        form(pairs - 1, even_ref)
    part = jnp.dot(p_ref[...], t_ref[...], preferred_element_type=jnp.float32)
    if acc_ref is not None:
        part = part + acc_ref[...]
    out_ref[...] = part.astype(out_ref.dtype)


def beam_stage(received, gains, weights, shift, start, acc):
    _, frames, _, width = received.shape
    chans = width // 2
    last = start + frames == TIMES
    held = jnp.bfloat16 if last else jnp.float32
    if width != LANES:
        volt = jnp.moveaxis(received, 1, 0).reshape(frames, FEEDS, 2, chans).astype(jnp.float32)
        ga, gb = (g.reshape(FEEDS, 2, chans) for g in gains)
        cal = (volt * ga + volt[:, :, ::-1] * gb).astype(jnp.bfloat16)
        turned = jnp.stack([cal[:, :, 1], -cal[:, :, 0]], axis=2)
        both = jnp.concatenate([cal, turned], axis=1)
        beams = jnp.einsum("bf,tfrc->btrc", weights, both, preferred_element_type=jnp.float32)
        power = jnp.sum(beams * beams, axis=2) * (1.0 / FEEDS)
        power = power.astype(jnp.bfloat16).reshape(BEAMS, frames * chans)
        frame = start + jnp.arange(frames, dtype=jnp.int32)[:, None, None]
        spread = jnp.where(shift[None] == frame, HIT, MISS).astype(jnp.bfloat16)
        spread = spread.reshape(frames * chans, -1)
        part = jnp.dot(power, spread, preferred_element_type=jnp.float32)
        return (part if acc is None else part + acc).astype(held)
    series = TRIALS * TIMES
    operands = (received, *gains, weights, shift) + (() if acc is None else (acc,))
    return pl.pallas_call(
        functools.partial(beam_kernel, start, frames, chans),
        out_shape=jax.ShapeDtypeStruct((BEAMS, series), held),
        in_specs=[pl.BlockSpec(memory_space=pltpu.VMEM)] * len(operands),
        out_specs=pl.BlockSpec(memory_space=pltpu.VMEM),
        scratch_shapes=[
            pltpu.VMEM((2 * FEEDS, 2 * width), jnp.bfloat16),
            pltpu.VMEM((2 * FEEDS, 2 * width), jnp.bfloat16),
            pltpu.VMEM((frames * chans, series), jnp.bfloat16),
            pltpu.VMEM((BEAMS, frames * chans), jnp.bfloat16),
        ],
        compiler_params=pltpu.CompilerParams(vmem_limit_bytes=BEAM_VMEM * 1024 * 1024),
    )(*operands)


def local(voltages, gain_table, gain_index, cylinder_map, delays, chan_map):
    feeds = voltages.shape[0]
    grp_count, mem_count = lax.axis_size("grp"), lax.axis_size("mem")
    peers = grp_count * mem_count
    chans = CHANS // peers
    grp, mem = lax.axis_index("grp"), lax.axis_index("mem")

    window = pfb_window(TAPS, NFFT)
    peer = jnp.arange(peers, dtype=jnp.int32)
    base = peer % mem_count * (CHANS // mem_count) + peer // mem_count * chans
    chan_of = base[:, None, None] + jnp.arange(chans, dtype=jnp.int32)[None, None, :]
    quarter = jnp.arange(2, dtype=jnp.int32)[None, :, None]
    chan_of, quarter = (
        jnp.broadcast_to(v, (peers, 2, chans)).reshape(-1) for v in (chan_of, quarter)
    )
    table = channel_table(chan_of, quarter)

    table = lax.optimization_barrier(table)
    starts = [sum(CHUNKS[:i]) for i in range(len(CHUNKS))]

    def exchange(spectra):
        return lax.all_to_all(spectra, PEERS, split_axis=0, concat_axis=0, tiled=True)

    spectra = [
        dft_stage(voltages, window, table, start, frames, peers)
        for start, frames in zip(starts, CHUNKS)
    ]
    received = [exchange(block) for block in spectra[:-1]]

    pairs = lax.axis_size("pair")
    cores = 2 if grp_count % 2 == 0 else 1
    owned = BEAMS // (pairs * peers)
    weights = beam_weights(cylinder_map)
    weights = weights.reshape(pairs, grp_count // cores, cores, mem_count * owned, 2 * FEEDS)
    weights = jnp.moveaxis(weights, 2, 0).reshape(BEAMS, 2 * FEEDS)
    gain_here = lax.dynamic_slice_in_dim(gain_table, grp * chans, chans, 2)
    gain_rows = gain_index[:, lax.axis_index("pair")]
    pick = gain_rows[:, None] == jnp.arange(gain_table.shape[0], dtype=jnp.int32)[None, :]
    gain_values = jnp.dot(
        pick.astype(jnp.float32),
        gain_here.reshape(gain_table.shape[0], 2 * chans),
        precision=lax.Precision.HIGHEST,
    )
    gain_real, gain_imag = gain_values[:, :chans], gain_values[:, chans:]
    gains = (
        jnp.concatenate([gain_real, gain_real], axis=1),
        jnp.concatenate([-gain_imag, gain_imag], axis=1),
    )

    first = mem * (CHANS // mem_count) + grp * chans
    freq = lax.dynamic_slice_in_dim(chan_map, first, chans, 0)
    column = jnp.arange(CHANS, dtype=jnp.int32)[:, None] == freq[None, :]
    delay = jnp.dot(
        delays.astype(jnp.bfloat16), column.astype(jnp.bfloat16), preferred_element_type=jnp.float32
    ).astype(jnp.int32)
    frame = jnp.arange(TIMES, dtype=jnp.int32)[None, None, :]
    shift = ((frame - delay.T[:, :, None]) % TIMES).reshape(chans, TRIALS * TIMES)

    part = None
    for i, start in enumerate(starts):
        if i == len(starts) - 1:
            last, part = lax.optimization_barrier((spectra[-1], held))
            received.append(exchange(last))
            part = beam_stage(received[i - 1], gains, weights, shift, starts[i - 1], part)
        if i == len(starts) - 2:
            held = part
            continue
        part = beam_stage(received[i], gains, weights, shift, start, part)

    series = TRIALS * TIMES
    groups = [[x * cores + c for c in range(cores)] for x in range(grp_count // cores)]
    part = part.reshape(cores, BEAMS // cores, series)
    part = lax.all_to_all(
        part, "grp", split_axis=0, concat_axis=0, axis_index_groups=groups, tiled=True
    )
    part = jnp.sum(part.astype(jnp.float32), axis=0).astype(jnp.bfloat16)
    part = part.reshape(pairs * peers // cores, owned, series)
    groups = [
        [
            (p * grp_count + x * cores + c) * mem_count + m
            for p in range(pairs)
            for x in range(grp_count // cores)
            for m in range(mem_count)
        ]
        for c in range(cores)
    ]
    part = lax.all_to_all(
        part, ("pair",) + PEERS, split_axis=0, concat_axis=0, axis_index_groups=groups, tiled=True
    )
    series = jnp.sum(part.astype(jnp.float32), axis=0)
    return series.reshape(1, owned, TRIALS, TIMES)

GROUP = 4
STEP = 2
FUSED_VMEM = 62


def wave(index, length):
    angles = (index & (length - 1)).astype(jnp.float32) * (2.0 * math.pi / length)
    return jnp.cos(angles), jnp.sin(angles)


def iota(shape, axis):
    return lax.broadcasted_iota(jnp.int32, shape, axis)


def fill_window(window_ref):
    shape = (TAPS, NFFT)
    offsets = (iota(shape, 0) * NFFT + iota(shape, 1)).astype(jnp.float32) + 0.5
    arg = (offsets - TAPS * NFFT / 2.0) / NFFT * math.pi
    taper = 0.5 - 0.5 * jnp.cos(offsets * (2.0 * math.pi / (TAPS * NFFT)))
    window_ref[...] = jnp.sin(arg) / arg * taper


def fill_waves(wave_ref, cores, chans):
    shape = (8, cores * LANES)
    lane = iota(shape, 1)
    chan = lane // LANES * chans + lane % chans
    quarter = lane % LANES // chans * (NFFT // 4)
    start = wave(iota(shape, 0) * chan + quarter, NFFT)
    wave_ref[0, 0:8, :], wave_ref[1, 0:8, :] = start
    step = 8
    while step < NFFT:
        turn_real, turn_imag = (v[None] for v in wave(chan * step, NFFT))
        real, imag = (wave_ref[r, 0:step, :].reshape(step // 8, *shape) for r in range(2))
        rows = slice(step, 2 * step)
        wave_ref[0, rows, :] = (real * turn_real - imag * turn_imag).reshape(step, shape[1])
        wave_ref[1, rows, :] = (real * turn_imag + imag * turn_real).reshape(step, shape[1])
        step *= 2


def fill_table(table_ref, wave_ref, chip, first):
    period = NFFT // LANES
    shape = (period, table_ref.shape[2])
    turn_real, turn_imag = (v[None] for v in wave(iota(shape, 0) * (first // LANES), period))
    block = 256

    def part(i, carry):
        rows = pl.ds(pl.multiple_of(i * block, block), block)
        real, imag = (wave_ref[r, rows, :].reshape(block // period, *shape) for r in range(2))
        filled = (real * turn_real - imag * turn_imag).reshape(block, shape[1])
        table_ref[chip, rows, :] = filled.astype(jnp.bfloat16)
        return carry

    lax.fori_loop(0, NFFT // block, part, 0)


def fill_gains(gains_ref, gain_table_ref, gain_index_ref, grp, pair):
    rows, _, held = gain_table_ref.shape
    chans = LANES // 2
    low = iota((rows, held), 1) < chans

    def twice(values):
        values = pltpu.roll(values, (held - grp * chans) % held, 1)
        return jnp.where(low, values, pltpu.roll(values, chans, 1))[:, :LANES]

    real = twice(gain_table_ref[:, 0, :])
    imag = twice(gain_table_ref[:, 1, :])
    imag = jnp.where(low[:, :LANES], -imag, imag)
    left = jnp.concatenate([real, imag], axis=1)
    index = gain_index_ref[pl.ds(pair, 1), :]
    pick = jnp.where(iota((rows, index.shape[1]), 0) == index, 1.0, 0.0).astype(jnp.bfloat16)
    total = None
    for _ in range(3):
        term = left.astype(jnp.bfloat16)
        left = left - term.astype(jnp.float32)
        picked = lax.dot_general(
            pick, term, (((0,), (0,)), ((), ())), preferred_element_type=jnp.float32
        )
        total = picked if total is None else total + picked
    gains_ref[...] = total


def fill_shift(shift_ref, delays_ref, chan_map_ref, mem):
    held, series = shift_ref.shape
    freq = chan_map_ref[:, pl.ds(pl.multiple_of(mem * held, held), held)]
    column = jnp.where(iota((CHANS, held), 0) == freq, 1.0, 0.0).astype(jnp.bfloat16)
    known = delays_ref[...].astype(jnp.float32).astype(jnp.bfloat16)
    delay = jnp.dot(known, column, preferred_element_type=jnp.float32).astype(jnp.bfloat16)
    shape = (TRIALS, series)
    spread = jnp.where(iota(shape, 1) // TIMES == iota(shape, 0), 1.0, 0.0).astype(jnp.bfloat16)
    late = lax.dot_general(
        delay, spread, (((0,), (0,)), ((), ())), preferred_element_type=jnp.float32
    )
    shift = (iota((held, series), 1) % TIMES).astype(jnp.float32) - late
    shift_ref[...] = jnp.where(shift < 0.0, shift + TIMES, shift)


def fill_weights(w_ref, hit_ref, upper_ref, cylinder_ref):
    block = 128

    def mark(i, carry):
        at = pl.multiple_of(i * block, block)
        hit = iota((block, FEEDS), 0) + at == cylinder_ref[...]
        hit_ref[pl.ds(at, block), :] = jnp.where(hit, 1.0, 0.0).astype(jnp.bfloat16)
        return carry

    lax.fori_loop(0, FEEDS // block, mark, 0)
    shape = (8, FEEDS)
    row, slot = iota(shape, 0), iota(shape, 1)
    digit = jnp.where(row == 0, slot // NS, jnp.where(row == 1, slot % NS // 16, slot % 16))
    digit = digit.astype(jnp.float32).astype(jnp.bfloat16)
    found = lax.dot_general(
        digit, hit_ref[...], (((1,), (1,)), ((), ())), preferred_element_type=jnp.float32
    )
    cyl = found[0:1].astype(jnp.int32)
    pos = (found[1:2] * 16.0 + found[2:3]).astype(jnp.int32)
    shape = (CYL * 16, FEEDS)
    row = iota(shape, 0)
    upper = wave(16 * pos * (row % 16) + (NS // CYL) * cyl * (row // 16), NS)
    upper_ref[0], upper_ref[1] = upper
    shape = (8, FEEDS)
    lower = [wave(pos * (2 * iota(shape, 0) + a), NS) for a in range(2)]

    def pack(i, carry):
        for a in range(2):
            parts = [[], []]
            for v in range(2):
                at = pl.ds(i * 2 + v, 1)
                real, imag = times((upper_ref[0, at, :], upper_ref[1, at, :]), lower[a])
                parts[0].append(real)
                parts[1].append(imag)
            rows = pl.ds(pl.multiple_of(a * (BEAMS // 2) + i * 16, 16), 16)
            for r in range(2):
                both = jnp.concatenate(parts[r], axis=0).astype(jnp.bfloat16)
                w_ref[rows, r * FEEDS : (r + 1) * FEEDS] = both
        return carry

    lax.fori_loop(0, CYL * 16 // 2, pack, 0)


def fused_kernel(
    sizes, gain_table_ref, gain_index_ref, cylinder_ref, delays_ref, chan_map_ref, volt_hbm, out_ref,
    volt_ref, table_ref, w_ref, framed_ref, send_ref, recv_ref, x_ref, psend_ref, precv_ref,
    t_ref, lhs_ref, acc_ref, zsend_ref, zrecv_ref,
    window_ref, wave_ref, gains_ref, shift_ref, hit_ref, upper_ref,
    head_sem, volt_sem, send_sem, recv_sem, own_sem,
    psend_sem, precv_sem, pown_sem, zsend_sem, zrecv_sem,
):
    grp_count, mem_count, pairs, cores = sizes
    peers = grp_count * mem_count
    chips = peers // cores
    feeds = volt_hbm.shape[0]
    chans = LANES // 2
    width = LANES
    chunks = TIMES // GROUP
    steps = GROUP // STEP
    grp, mem, pair = (lax.axis_index(n) for n in ("grp", "mem", "pair"))
    me = grp * mem_count + mem
    across = pair * grp_count + grp
    MESH = pl.DeviceIdType.MESH

    def load(src, dst, sem):
        return pltpu.make_async_copy(src, dst, sem)

    head = (TAPS - 1) * NFFT
    load(volt_hbm.at[:, 0:head], volt_ref.at[:, 0:head], head_sem).start()

    def volt_copy(k):
        cols = pl.ds(pl.multiple_of(head + k * (GROUP * NFFT), NFFT), GROUP * NFFT)
        return load(volt_hbm.at[:, cols], volt_ref.at[:, cols], volt_sem.at[k])

    for k in range(chunks):
        volt_copy(k).start()

    barrier = pltpu.get_barrier_semaphore()
    met = 0
    for dg in range(grp_count):
        for dm in range(mem_count):
            for dp in range(pairs):
                if (dg, dm, dp) == (0, 0, 0) or (dm != 0 and dp != 0):
                    continue
                there = {
                    "grp": (grp + dg) % grp_count,
                    "mem": (mem + dm) % mem_count,
                    "pair": (pair + dp) % pairs,
                }
                pl.semaphore_signal(barrier, inc=1, device_id=there, device_id_type=MESH)
                met += 1
    acc_ref[...] = jnp.zeros_like(acc_ref)
    fill_window(window_ref)
    fill_waves(wave_ref, cores, chans)
    pl.semaphore_wait(barrier, met)
    load(volt_hbm.at[:, 0:head], volt_ref.at[:, 0:head], head_sem).wait()

    def main_copy(q, g, m):
        peer = g * mem_count + m
        return pltpu.make_async_remote_copy(
            src_ref=send_ref.at[q, peer],
            dst_ref=recv_ref.at[q, me],
            send_sem=send_sem.at[q],
            recv_sem=recv_sem.at[q],
            device_id={"grp": g, "mem": m},
            device_id_type=MESH,
        )

    def own_copy(q):
        return load(send_ref.at[q, me], recv_ref.at[q, me], own_sem.at[q])

    x_here = grp // cores

    def dft(k):
        volt_copy(k).wait()
        for t in range(GROUP):
            def tap(j):
                at = pl.multiple_of((k * GROUP + t + j) * NFFT, NFFT)
                return volt_ref[:, pl.ds(at, NFFT)].astype(jnp.float32) * window_ref[j : j + 1, :]

            total = tap(0)
            for j in range(1, TAPS):
                total = total + tap(j)
            framed_ref[t * feeds : (t + 1) * feeds, :] = total.astype(jnp.bfloat16)

        def tile(s, carry):
            h = s // 2
            far = (mem + 2) % 4 * ((3 - h) // 3) + (3 - mem) * (h % 3 % 2)
            near = (mem + 1 - 2 * (mem % 2)) * (h % 3 // 2) + mem * (h // 3)
            m = far + near
            x = (x_here + s + 1) % 2
            chip = x * mem_count + m

            @pl.when(k == 0)
            def _():
                first = m * (CHANS // mem_count) + x * (cores * chans)
                fill_table(table_ref, wave_ref, chip, first)

            part = jnp.dot(framed_ref[...], table_ref[chip], preferred_element_type=jnp.float32)
            part = (part * (1.0 / math.sqrt(NFFT))).astype(jnp.bfloat16)
            for c in range(cores):
                g = x * cores + c
                peer = g * mem_count + m
                for u in range(steps):
                    q = k * steps + u
                    rows = part[u * STEP * feeds : (u + 1) * STEP * feeds, c * width : (c + 1) * width]
                    send_ref[q, peer] = rows.reshape(STEP, feeds, width)

                @pl.when(peer != me)
                def _():
                    for u in range(steps):
                        main_copy(k * steps + u, g, m).start()

                @pl.when(peer == me)
                def _():
                    for u in range(steps):
                        own_copy(k * steps + u).start()

            return carry

        lax.fori_loop(0, chips, tile, 0)

    lane = lax.broadcasted_iota(jnp.int32, (FEEDS, width), 1)
    sign = jnp.where(lane < chans, 1.0, -1.0)
    low = lax.broadcasted_iota(jnp.int32, (BEAMS, width), 1) < chans
    rows_each = BEAMS // (pairs * grp_count)

    def arrived(q):
        others = recv_ref.at[q, pl.ds(0, peers - 1)]
        return load(others, others, recv_sem.at[q])

    def left(q):
        others = send_ref.at[q, pl.ds(0, peers - 1)]
        return load(others, others, send_sem.at[q])

    def power_copy(q, p, g):
        d = p * grp_count + g
        block = pl.ds(pl.multiple_of(d * rows_each, rows_each), rows_each)
        return pltpu.make_async_remote_copy(
            src_ref=psend_ref.at[q, block],
            dst_ref=precv_ref.at[q, across],
            send_sem=psend_sem.at[q],
            recv_sem=precv_sem.at[q],
            device_id={"pair": p, "grp": g},
            device_id_type=MESH,
        )

    def power_own(q):
        block = pl.ds(pl.multiple_of(across * rows_each, rows_each), rows_each)
        return load(psend_ref.at[q, block], precv_ref.at[q, across], pown_sem.at[q])

    others_count = pairs * grp_count - 1

    def power_arrived(q):
        others = precv_ref.at[q, pl.ds(0, others_count)]
        return load(others, others, precv_sem.at[q])

    def power_left(q):
        others = psend_ref.at[q, pl.ds(0, others_count * rows_each)]
        return load(others, others, psend_sem.at[q])

    def beams(q):
        arrived(q).wait()
        own_copy(q).wait()
        for u in range(STEP):
            volt = recv_ref[q, :, u].reshape(FEEDS, width).astype(jnp.float32)
            cal = volt * gains_ref[:, :width] + pltpu.roll(volt, chans, 1) * gains_ref[:, width:]
            turned = pltpu.roll(cal, chans, 1) * sign
            cols = slice(u * width, (u + 1) * width)
            x_ref[0:FEEDS, cols] = cal.astype(jnp.bfloat16)
            x_ref[FEEDS : 2 * FEEDS, cols] = turned.astype(jnp.bfloat16)
        formed = jnp.dot(w_ref[...], x_ref[...], preferred_element_type=jnp.float32)
        squares = formed * formed
        one, two = squares[:, :width], squares[:, width:]
        first = one + pltpu.roll(one, chans, 1)
        second = two + pltpu.roll(two, chans, 1)
        power = jnp.where(low, first, second) * (1.0 / FEEDS)
        psend_ref[q] = power.astype(jnp.bfloat16)
        for dp in range(pairs - 1, -1, -1):
            for dg in range(grp_count - 1, -1, -1):
                if dp == 0 and dg == 0:
                    power_own(q).start()
                else:
                    power_copy(q, (pair + dp) % pairs, (grp + dg) % grp_count).start()

    def dedisperse(q):
        for s in range(grp_count):
            for u in range(STEP):
                frame = (q * STEP + u).astype(jnp.float32)
                hit = shift_ref[s * chans : (s + 1) * chans, :] == frame
                at = (s * STEP + u) * chans
                t_ref[at : at + chans, :] = jnp.where(hit, HIT, MISS).astype(jnp.bfloat16)
        power_arrived(q).wait()
        power_own(q).wait()
        for s in range(grp_count):
            both = precv_ref[q, s].astype(jnp.float32)
            for p in range(1, pairs):
                both = both + precv_ref[q, p * grp_count + s].astype(jnp.float32)
            lhs_ref[:, s * width : (s + 1) * width] = both.astype(jnp.bfloat16)
        acc_ref[...] += jnp.dot(lhs_ref[...], t_ref[...], preferred_element_type=jnp.float32)

    def body(i, carry):
        @pl.when(i < chunks)
        def _():
            dft(i)

        @pl.when(i == 1)
        def _():
            fill_gains(gains_ref, gain_table_ref, gain_index_ref, grp, pair)
            fill_shift(shift_ref, delays_ref, chan_map_ref, mem)
            fill_weights(w_ref, hit_ref, upper_ref, cylinder_ref)

        @pl.when(i >= 3)
        def _():
            lax.fori_loop(0, steps, lambda u, c: (dedisperse((i - 3) * steps + u), c)[1], 0)

        @pl.when(jnp.logical_and(i >= 2, i < chunks + 2))
        def _():
            lax.fori_loop(0, steps, lambda u, c: (beams((i - 2) * steps + u), c)[1], 0)

        return carry

    lax.fori_loop(0, chunks + 3, body, 0)

    owned = rows_each // mem_count
    zsend_ref[...] = acc_ref[...].astype(jnp.bfloat16)

    def z_copy(d):
        m = (mem + d) % mem_count
        return pltpu.make_async_remote_copy(
            src_ref=zsend_ref.at[pl.ds(pl.multiple_of(m * owned, owned), owned)],
            dst_ref=zrecv_ref.at[d - 1],
            send_sem=zsend_sem.at[d - 1],
            recv_sem=zrecv_sem.at[d - 1],
            device_id={"mem": m},
            device_id_type=MESH,
        )

    for d in range(1, mem_count):
        z_copy(d).start()

    def drain(q, carry):
        left(q).wait()
        power_left(q).wait()
        return carry

    lax.fori_loop(0, chunks * steps, drain, 0)
    total = acc_ref[pl.ds(pl.multiple_of(mem * owned, owned), owned), :]
    for d in range(1, mem_count):
        z_copy(d).wait()
        total = total + zrecv_ref[d - 1].astype(jnp.float32)
    out_ref[...] = total


def fused_stage(sizes, gain_table, gain_index, cylinder_map, delays, chan_map, voltages):
    grp_count, mem_count, pairs, cores = sizes
    peers = grp_count * mem_count
    chips = peers // cores
    feeds, samples = voltages.shape
    series = TRIALS * TIMES
    count = TIMES // STEP
    groups = pairs * grp_count
    rows_each = BEAMS // groups
    owned = rows_each // mem_count
    bf16, f32 = jnp.bfloat16, jnp.float32
    dma = pltpu.SemaphoreType.DMA
    vmem = pl.BlockSpec(memory_space=pltpu.VMEM)
    return pl.pallas_call(
        functools.partial(fused_kernel, sizes),
        out_shape=jax.ShapeDtypeStruct((owned, series), f32),
        in_specs=[vmem] * 5 + [pl.BlockSpec(memory_space=pl.ANY)],
        out_specs=vmem,
        scratch_shapes=[
            pltpu.VMEM((feeds, samples), bf16),
            pltpu.VMEM((chips, NFFT, cores * LANES), bf16),
            pltpu.VMEM((BEAMS, 2 * FEEDS), bf16),
            pltpu.VMEM((GROUP * feeds, NFFT), bf16),
            pltpu.VMEM((count, peers, STEP, feeds, LANES), bf16),
            pltpu.VMEM((count, peers, STEP, feeds, LANES), bf16),
            pltpu.VMEM((2 * FEEDS, STEP * LANES), bf16),
            pltpu.VMEM((count, BEAMS, LANES), bf16),
            pltpu.VMEM((count, groups, rows_each, LANES), bf16),
            pltpu.VMEM((grp_count * LANES, series), bf16),
            pltpu.VMEM((rows_each, grp_count * LANES), bf16),
            pltpu.VMEM((rows_each, series), f32),
            pltpu.VMEM((rows_each, series), bf16),
            pltpu.VMEM((mem_count - 1, owned, series), bf16),
            pltpu.VMEM((TAPS, NFFT), f32),
            pltpu.VMEM((2, NFFT, cores * LANES), f32),
            pltpu.VMEM((FEEDS, 2 * LANES), f32),
            pltpu.VMEM((CHANS // mem_count, series), f32),
            pltpu.VMEM((FEEDS, FEEDS), bf16),
            pltpu.VMEM((2, CYL * 16, FEEDS), f32),
            dma,
            dma((TIMES // GROUP,)),
            dma((count,)),
            dma((count,)),
            dma((count,)),
            dma((count,)),
            dma((count,)),
            dma((count,)),
            dma((mem_count - 1,)),
            dma((mem_count - 1,)),
        ],
        compiler_params=pltpu.CompilerParams(
            collective_id=0, has_side_effects=True, vmem_limit_bytes=FUSED_VMEM * 1024 * 1024
        ),
    )(gain_table, gain_index, cylinder_map, delays, chan_map, voltages)


def local_fused(voltages, gain_table, gain_index, cylinder_map, delays, chan_map):
    feeds, _, samples = voltages.shape
    sizes = (lax.axis_size("grp"), lax.axis_size("mem"), lax.axis_size("pair"), 2)
    series = fused_stage(
        sizes,
        gain_table,
        gain_index.T,
        cylinder_map.reshape(1, FEEDS),
        delays,
        chan_map.reshape(1, CHANS),
        voltages.reshape(feeds, samples),
    )
    return series.reshape(1, -1, TRIALS, TIMES)


def solution(mesh):
    shape = (mesh.shape["grp"], mesh.shape["mem"], mesh.shape["pair"])
    return jax.shard_map(
        local_fused if shape == (4, 4, 2) else local,
        mesh=mesh,
        in_specs=(P(PEERS, "pair", None), P(None, None, "mem"), P(), P(), P(), P()),
        out_specs=P("pair", PEERS, None, None),
        check_vma=False,
    )
```

```python
import functools
import math

import jax
import jax.numpy as jnp
from jax import lax
from jax.experimental import pallas as pl
from jax.experimental.pallas import tpu as pltpu
from jax.sharding import PartitionSpec as P

NFFT = 2048
CHANS = 1024
TAPS = 4
CYL = 4
NS = 256
FEEDS = 1024
BEAMS = 1024
TIMES = 32
TRIALS = 32
PEERS = ("grp", "mem")
LANES = 128


def pfb_window(tap_count, length):
    offsets = jnp.arange(tap_count * length, dtype=jnp.float32) + 0.5
    shaped = jnp.sinc((offsets - tap_count * length / 2.0) / length)
    taper_term = 0.5 - 0.5 * jnp.cos(offsets * (2.0 * math.pi / (tap_count * length)))
    return (shaped * taper_term).reshape(tap_count, length)


def turn(index, length):
    angles = (index % length).astype(jnp.float32) * (2.0 * math.pi / length)
    return lax.optimization_barrier((jnp.cos(angles), jnp.sin(angles)))


def times(a, b):
    return (a[0] * b[0] - a[1] * b[1], a[0] * b[1] + a[1] * b[0])


def channel_table(chan_of, quarter):
    chan = chan_of[None, :]
    high = turn(jnp.arange(16, dtype=jnp.int32)[:, None] * 128 * chan, NFFT)
    mid = turn(jnp.arange(16, dtype=jnp.int32)[:, None] * 8 * chan, NFFT)
    low = turn(jnp.arange(8, dtype=jnp.int32)[:, None] * chan + quarter[None, :] * (NFFT // 4), NFFT)
    upper = times([p[:, None, :] for p in high], [p[None, :, :] for p in mid])
    upper = lax.optimization_barrier(tuple(p.reshape(NFFT // 8, 1, -1) for p in upper))
    table = upper[0] * low[0][None] - upper[1] * low[1][None]
    return table.astype(jnp.bfloat16).reshape(NFFT, -1)


def beam_weights(cylinder_map):
    slots = jnp.arange(FEEDS, dtype=jnp.int32)
    hit = cylinder_map[:, None] == slots[None, :]
    slot_of = jnp.sum(jnp.where(hit, slots[:, None], 0), axis=0)
    cyl, pos = slot_of // NS, slot_of % NS
    e = jnp.arange(CYL, dtype=jnp.int32).reshape(CYL, 1, 1)
    hh = jnp.arange(16, dtype=jnp.int32).reshape(1, 16, 1)
    upper = turn(16 * pos * hh + (NS // CYL) * e * cyl, NS)
    a = jnp.arange(2, dtype=jnp.int32).reshape(2, 1, 1)
    hl = jnp.arange(8, dtype=jnp.int32).reshape(1, 8, 1)
    lower = turn(pos * (2 * hl + a), NS)
    real, imag = times(
        [p[None, :, :, None, :] for p in upper], [p[:, None, None, :, :] for p in lower]
    )
    return jnp.concatenate(
        [p.astype(jnp.bfloat16).reshape(BEAMS, FEEDS) for p in (real, imag)], axis=1
    )


BEAM_VMEM = 40
DFT_VMEM = 40
CHUNKS = (8, 20, 4)


def dft_kernel(frames, feeds, window_ref, volt_ref, table_ref, out_ref, framed_ref):
    @pl.when(pl.program_id(0) == 0)
    def _():
        for t in range(frames):
            total = volt_ref[:, t * NFFT : (t + 1) * NFFT].astype(jnp.float32) * window_ref[0:1, :]
            for j in range(1, TAPS):
                tap = volt_ref[:, (t + j) * NFFT : (t + j + 1) * NFFT].astype(jnp.float32)
                total = total + tap * window_ref[j : j + 1, :]
            framed_ref[t * feeds : (t + 1) * feeds, :] = total.astype(jnp.bfloat16)

    part = jnp.dot(framed_ref[...], table_ref[...], preferred_element_type=jnp.float32)
    part = (part * (1.0 / math.sqrt(NFFT))).astype(jnp.bfloat16)
    for i in range(out_ref.shape[0]):
        out_ref[i] = part[:, i * LANES : (i + 1) * LANES].reshape(frames, feeds, LANES)


def dft_stage(voltages, window, table, start, frames, peers):
    feeds = voltages.shape[0]
    length = (frames + TAPS - 1) * NFFT
    volt = lax.slice_in_dim(voltages, start * NFFT, start * NFFT + length, axis=2)
    volt = volt.reshape(feeds, length)
    width = table.shape[1] // peers
    if width != LANES:
        view = volt.reshape(feeds, frames + TAPS - 1, NFFT).astype(jnp.float32)
        framed = view[:, 0:frames] * window[0]
        for j in range(1, TAPS):
            framed = framed + view[:, j : j + frames] * window[j]
        rows = jnp.swapaxes(framed.astype(jnp.bfloat16), 0, 1).reshape(frames * feeds, NFFT)
        part = jnp.dot(rows, table, preferred_element_type=jnp.float32) * (1.0 / math.sqrt(NFFT))
        part = part.astype(jnp.bfloat16).reshape(frames, feeds, peers, width)
        return jnp.moveaxis(part, 2, 0)
    step = 4
    return pl.pallas_call(
        functools.partial(dft_kernel, frames, feeds),
        grid=(peers // step,),
        out_shape=jax.ShapeDtypeStruct((peers, frames, feeds, width), jnp.bfloat16),
        in_specs=[
            pl.BlockSpec((TAPS, NFFT), lambda i: (0, 0)),
            pl.BlockSpec((feeds, length), lambda i: (0, 0)),
            pl.BlockSpec((NFFT, step * width), lambda i: (0, i)),
        ],
        out_specs=pl.BlockSpec((step, frames, feeds, width), lambda i: (i, 0, 0, 0)),
        scratch_shapes=[pltpu.VMEM((frames * feeds, NFFT), jnp.bfloat16)],
        compiler_params=pltpu.CompilerParams(
            dimension_semantics=("arbitrary",), vmem_limit_bytes=DFT_VMEM * 1024 * 1024
        ),
    )(window, volt, table)


HIT = (TIMES - 1) / (TIMES * TIMES)
MISS = -1.0 / (TIMES * TIMES)


def beam_kernel(start, frames, chans, r_ref, ga_ref, gb_ref, w_ref, e_ref, *rest):
    acc_ref = rest[0] if len(rest) == 6 else None
    out_ref, even_ref, odd_ref, t_ref, p_ref = rest[-5:]
    width = 2 * chans
    lane = lax.broadcasted_iota(jnp.int32, (FEEDS, width), 1)
    sign = jnp.where(lane < chans, 1.0, -1.0)
    low = lax.broadcasted_iota(jnp.int32, (BEAMS, width), 1) < chans

    def calibrate(pair, x_ref):
        for u in range(2):
            i = 2 * pair + u
            volt = r_ref[:, i].reshape(FEEDS, width).astype(jnp.float32)
            cal = volt * ga_ref[...] + pltpu.roll(volt, chans, 1) * gb_ref[...]
            turned = pltpu.roll(cal, chans, 1) * sign
            cols = slice(u * width, (u + 1) * width)
            x_ref[0:FEEDS, cols] = cal.astype(jnp.bfloat16)
            x_ref[FEEDS : 2 * FEEDS, cols] = turned.astype(jnp.bfloat16)
            hit = e_ref[...] == start + i
            rows = pl.ds(pl.multiple_of(i * chans, chans), chans)
            t_ref[rows, :] = jnp.where(hit, HIT, MISS).astype(jnp.bfloat16)

    def form(pair, x_ref):
        beams = jnp.dot(w_ref[...], x_ref[...], preferred_element_type=jnp.float32)
        squares = beams * beams
        one, two = squares[:, :width], squares[:, width:]
        first = one + pltpu.roll(one, chans, 1)
        second = two + pltpu.roll(two, chans, 1)
        power = jnp.where(low, first, second) * (1.0 / FEEDS)
        p_ref[:, pl.ds(pl.multiple_of(pair * width, width), width)] = power.astype(jnp.bfloat16)

    pairs = frames // 2
    calibrate(0, even_ref)

    def body(k, carry):
        form(2 * k, even_ref)
        calibrate(2 * k + 1, odd_ref)
        form(2 * k + 1, odd_ref)
        calibrate(jnp.minimum(2 * k + 2, pairs - 1), even_ref)
        return carry

    lax.fori_loop(0, pairs // 2, body, 0)
    if pairs % 2:
        form(pairs - 1, even_ref)
    part = jnp.dot(p_ref[...], t_ref[...], preferred_element_type=jnp.float32)
    if acc_ref is not None:
        part = part + acc_ref[...]
    out_ref[...] = part.astype(out_ref.dtype)


def beam_stage(received, gains, weights, shift, start, acc):
    _, frames, _, width = received.shape
    chans = width // 2
    last = start + frames == TIMES
    held = jnp.bfloat16 if last else jnp.float32
    if width != LANES:
        volt = jnp.moveaxis(received, 1, 0).reshape(frames, FEEDS, 2, chans).astype(jnp.float32)
        ga, gb = (g.reshape(FEEDS, 2, chans) for g in gains)
        cal = (volt * ga + volt[:, :, ::-1] * gb).astype(jnp.bfloat16)
        turned = jnp.stack([cal[:, :, 1], -cal[:, :, 0]], axis=2)
        both = jnp.concatenate([cal, turned], axis=1)
        beams = jnp.einsum("bf,tfrc->btrc", weights, both, preferred_element_type=jnp.float32)
        power = jnp.sum(beams * beams, axis=2) * (1.0 / FEEDS)
        power = power.astype(jnp.bfloat16).reshape(BEAMS, frames * chans)
        frame = start + jnp.arange(frames, dtype=jnp.int32)[:, None, None]
        spread = jnp.where(shift[None] == frame, HIT, MISS).astype(jnp.bfloat16)
        spread = spread.reshape(frames * chans, -1)
        part = jnp.dot(power, spread, preferred_element_type=jnp.float32)
        return (part if acc is None else part + acc).astype(held)
    series = TRIALS * TIMES
    operands = (received, *gains, weights, shift) + (() if acc is None else (acc,))
    return pl.pallas_call(
        functools.partial(beam_kernel, start, frames, chans),
        out_shape=jax.ShapeDtypeStruct((BEAMS, series), held),
        in_specs=[pl.BlockSpec(memory_space=pltpu.VMEM)] * len(operands),
        out_specs=pl.BlockSpec(memory_space=pltpu.VMEM),
        scratch_shapes=[
            pltpu.VMEM((2 * FEEDS, 2 * width), jnp.bfloat16),
            pltpu.VMEM((2 * FEEDS, 2 * width), jnp.bfloat16),
            pltpu.VMEM((frames * chans, series), jnp.bfloat16),
            pltpu.VMEM((BEAMS, frames * chans), jnp.bfloat16),
        ],
        compiler_params=pltpu.CompilerParams(vmem_limit_bytes=BEAM_VMEM * 1024 * 1024),
    )(*operands)


def local(voltages, gain_table, gain_index, cylinder_map, delays, chan_map):
    feeds = voltages.shape[0]
    grp_count, mem_count = lax.axis_size("grp"), lax.axis_size("mem")
    peers = grp_count * mem_count
    chans = CHANS // peers
    grp, mem = lax.axis_index("grp"), lax.axis_index("mem")

    window = pfb_window(TAPS, NFFT)
    peer = jnp.arange(peers, dtype=jnp.int32)
    base = peer % mem_count * (CHANS // mem_count) + peer // mem_count * chans
    chan_of = base[:, None, None] + jnp.arange(chans, dtype=jnp.int32)[None, None, :]
    quarter = jnp.arange(2, dtype=jnp.int32)[None, :, None]
    chan_of, quarter = (
        jnp.broadcast_to(v, (peers, 2, chans)).reshape(-1) for v in (chan_of, quarter)
    )
    table = channel_table(chan_of, quarter)

    table = lax.optimization_barrier(table)
    starts = [sum(CHUNKS[:i]) for i in range(len(CHUNKS))]

    def exchange(spectra):
        return lax.all_to_all(spectra, PEERS, split_axis=0, concat_axis=0, tiled=True)

    spectra = [
        dft_stage(voltages, window, table, start, frames, peers)
        for start, frames in zip(starts, CHUNKS)
    ]
    received = [exchange(block) for block in spectra[:-1]]

    pairs = lax.axis_size("pair")
    cores = 2 if grp_count % 2 == 0 else 1
    owned = BEAMS // (pairs * peers)
    weights = beam_weights(cylinder_map)
    weights = weights.reshape(pairs, grp_count // cores, cores, mem_count * owned, 2 * FEEDS)
    weights = jnp.moveaxis(weights, 2, 0).reshape(BEAMS, 2 * FEEDS)
    gain_here = lax.dynamic_slice_in_dim(gain_table, grp * chans, chans, 2)
    gain_rows = gain_index[:, lax.axis_index("pair")]
    pick = gain_rows[:, None] == jnp.arange(gain_table.shape[0], dtype=jnp.int32)[None, :]
    gain_values = jnp.dot(
        pick.astype(jnp.float32),
        gain_here.reshape(gain_table.shape[0], 2 * chans),
        precision=lax.Precision.HIGHEST,
    )
    gain_real, gain_imag = gain_values[:, :chans], gain_values[:, chans:]
    gains = (
        jnp.concatenate([gain_real, gain_real], axis=1),
        jnp.concatenate([-gain_imag, gain_imag], axis=1),
    )

    first = mem * (CHANS // mem_count) + grp * chans
    freq = lax.dynamic_slice_in_dim(chan_map, first, chans, 0)
    column = jnp.arange(CHANS, dtype=jnp.int32)[:, None] == freq[None, :]
    delay = jnp.dot(
        delays.astype(jnp.bfloat16), column.astype(jnp.bfloat16), preferred_element_type=jnp.float32
    ).astype(jnp.int32)
    frame = jnp.arange(TIMES, dtype=jnp.int32)[None, None, :]
    shift = ((frame - delay.T[:, :, None]) % TIMES).reshape(chans, TRIALS * TIMES)

    part = None
    for i, start in enumerate(starts):
        if i == len(starts) - 1:
            last, part = lax.optimization_barrier((spectra[-1], held))
            received.append(exchange(last))
            part = beam_stage(received[i - 1], gains, weights, shift, starts[i - 1], part)
        if i == len(starts) - 2:
            held = part
            continue
        part = beam_stage(received[i], gains, weights, shift, start, part)

    series = TRIALS * TIMES
    groups = [[x * cores + c for c in range(cores)] for x in range(grp_count // cores)]
    part = part.reshape(cores, BEAMS // cores, series)
    part = lax.all_to_all(
        part, "grp", split_axis=0, concat_axis=0, axis_index_groups=groups, tiled=True
    )
    part = jnp.sum(part.astype(jnp.float32), axis=0).astype(jnp.bfloat16)
    part = part.reshape(pairs * peers // cores, owned, series)
    groups = [
        [
            (p * grp_count + x * cores + c) * mem_count + m
            for p in range(pairs)
            for x in range(grp_count // cores)
            for m in range(mem_count)
        ]
        for c in range(cores)
    ]
    part = lax.all_to_all(
        part, ("pair",) + PEERS, split_axis=0, concat_axis=0, axis_index_groups=groups, tiled=True
    )
    series = jnp.sum(part.astype(jnp.float32), axis=0)
    return series.reshape(1, owned, TRIALS, TIMES)

GROUP = 4
STEP = 2
FUSED_VMEM = 62


def wave(index, length):
    angles = (index & (length - 1)).astype(jnp.float32) * (2.0 * math.pi / length)
    return jnp.cos(angles), jnp.sin(angles)


def iota(shape, axis):
    return lax.broadcasted_iota(jnp.int32, shape, axis)


def fill_window(window_ref):
    shape = (TAPS, NFFT)
    offsets = (iota(shape, 0) * NFFT + iota(shape, 1)).astype(jnp.float32) + 0.5
    arg = (offsets - TAPS * NFFT / 2.0) / NFFT * math.pi
    taper = 0.5 - 0.5 * jnp.cos(offsets * (2.0 * math.pi / (TAPS * NFFT)))
    window_ref[...] = jnp.sin(arg) / arg * taper


def fill_waves(wave_ref, cores, chans):
    shape = (8, cores * LANES)
    lane = iota(shape, 1)
    chan = lane // LANES * chans + lane % chans
    quarter = lane % LANES // chans * (NFFT // 4)
    start = wave(iota(shape, 0) * chan + quarter, NFFT)
    wave_ref[0, 0:8, :], wave_ref[1, 0:8, :] = start
    step = 8
    while step < NFFT:
        turn_real, turn_imag = (v[None] for v in wave(chan * step, NFFT))
        real, imag = (wave_ref[r, 0:step, :].reshape(step // 8, *shape) for r in range(2))
        rows = slice(step, 2 * step)
        wave_ref[0, rows, :] = (real * turn_real - imag * turn_imag).reshape(step, shape[1])
        wave_ref[1, rows, :] = (real * turn_imag + imag * turn_real).reshape(step, shape[1])
        step *= 2


def fill_table(table_ref, wave_ref, chip, first):
    period = NFFT // LANES
    shape = (period, table_ref.shape[2])
    turn_real, turn_imag = (v[None] for v in wave(iota(shape, 0) * (first // LANES), period))
    block = 256

    def part(i, carry):
        rows = pl.ds(pl.multiple_of(i * block, block), block)
        real, imag = (wave_ref[r, rows, :].reshape(block // period, *shape) for r in range(2))
        filled = (real * turn_real - imag * turn_imag).reshape(block, shape[1])
        table_ref[chip, rows, :] = filled.astype(jnp.bfloat16)
        return carry

    lax.fori_loop(0, NFFT // block, part, 0)


def fill_gains(gains_ref, gain_table_ref, gain_index_ref, grp, pair):
    rows, _, held = gain_table_ref.shape
    chans = LANES // 2
    low = iota((rows, held), 1) < chans

    def twice(values):
        values = pltpu.roll(values, (held - grp * chans) % held, 1)
        return jnp.where(low, values, pltpu.roll(values, chans, 1))[:, :LANES]

    real = twice(gain_table_ref[:, 0, :])
    imag = twice(gain_table_ref[:, 1, :])
    imag = jnp.where(low[:, :LANES], -imag, imag)
    left = jnp.concatenate([real, imag], axis=1)
    index = gain_index_ref[pl.ds(pair, 1), :]
    pick = jnp.where(iota((rows, index.shape[1]), 0) == index, 1.0, 0.0).astype(jnp.bfloat16)
    total = None
    for _ in range(3):
        term = left.astype(jnp.bfloat16)
        left = left - term.astype(jnp.float32)
        picked = lax.dot_general(
            pick, term, (((0,), (0,)), ((), ())), preferred_element_type=jnp.float32
        )
        total = picked if total is None else total + picked
    gains_ref[...] = total


def fill_shifts(shift_ref, final_ref, delays_ref, chan_map_ref, mem):
    held, series = shift_ref.shape
    known = delays_ref[...].astype(jnp.float32).astype(jnp.bfloat16)
    shape = (TRIALS, series)
    spread = jnp.where(iota(shape, 1) // TIMES == iota(shape, 0), 1.0, 0.0).astype(jnp.bfloat16)
    frame = (iota((held, series), 1) % TIMES).astype(jnp.float32)

    def some(m, carry):
        rows = pl.ds(pl.multiple_of(m * held, held), held)
        column = jnp.where(iota((CHANS, held), 0) == chan_map_ref[:, rows], 1.0, 0.0)
        delay = jnp.dot(known, column.astype(jnp.bfloat16), preferred_element_type=jnp.float32)
        late = lax.dot_general(
            delay.astype(jnp.bfloat16),
            spread,
            (((0,), (0,)), ((), ())),
            preferred_element_type=jnp.float32,
        )
        shift = frame - late
        shift = jnp.where(shift < 0.0, shift + TIMES, shift)
        hit = shift == float(TIMES - 1)
        final_ref[rows, :] = jnp.where(hit, HIT, MISS).astype(jnp.bfloat16)

        @pl.when(m == mem)
        def _():
            shift_ref[...] = shift

        return carry

    lax.fori_loop(0, CHANS // held, some, 0)


def fill_weights(w_ref, hit_ref, upper_ref, cylinder_ref):
    block = 128

    def mark(i, carry):
        at = pl.multiple_of(i * block, block)
        hit = iota((block, FEEDS), 0) + at == cylinder_ref[...]
        hit_ref[pl.ds(at, block), :] = jnp.where(hit, 1.0, 0.0).astype(jnp.bfloat16)
        return carry

    lax.fori_loop(0, FEEDS // block, mark, 0)
    shape = (8, FEEDS)
    row, slot = iota(shape, 0), iota(shape, 1)
    digit = jnp.where(row == 0, slot // NS, jnp.where(row == 1, slot % NS // 16, slot % 16))
    digit = digit.astype(jnp.float32).astype(jnp.bfloat16)
    found = lax.dot_general(
        digit, hit_ref[...], (((1,), (1,)), ((), ())), preferred_element_type=jnp.float32
    )
    cyl = found[0:1].astype(jnp.int32)
    pos = (found[1:2] * 16.0 + found[2:3]).astype(jnp.int32)
    shape = (CYL * 16, FEEDS)
    row = iota(shape, 0)
    upper = wave(16 * pos * (row % 16) + (NS // CYL) * cyl * (row // 16), NS)
    upper_ref[0], upper_ref[1] = upper
    shape = (8, FEEDS)
    lower = [wave(pos * (2 * iota(shape, 0) + a), NS) for a in range(2)]

    def pack(i, carry):
        for a in range(2):
            parts = [[], []]
            for v in range(2):
                at = pl.ds(i * 2 + v, 1)
                real, imag = times((upper_ref[0, at, :], upper_ref[1, at, :]), lower[a])
                parts[0].append(real)
                parts[1].append(imag)
            rows = pl.ds(pl.multiple_of(a * (BEAMS // 2) + i * 16, 16), 16)
            for r in range(2):
                both = jnp.concatenate(parts[r], axis=0).astype(jnp.bfloat16)
                w_ref[rows, r * FEEDS : (r + 1) * FEEDS] = both
        return carry

    lax.fori_loop(0, CYL * 16 // 2, pack, 0)


def fused_kernel(
    sizes, gain_table_ref, gain_index_ref, cylinder_ref, delays_ref, chan_map_ref, volt_hbm, out_ref,
    volt_ref, table_ref, w_ref, framed_ref, send_ref, recv_ref, x_ref, psend_ref, precv_ref,
    t_ref, lhs_ref, acc_ref, zsend_ref, zrecv_ref,
    window_ref, wave_ref, gains_ref, shift_ref, hit_ref, upper_ref, part_ref, parts_ref,
    head_sem, volt_sem, send_sem, recv_sem, own_sem,
    psend_sem, precv_sem, pown_sem, zsend_sem, zrecv_sem, lsend_sem, lrecv_sem,
):
    grp_count, mem_count, pairs, cores = sizes
    peers = grp_count * mem_count
    chips = peers // cores
    feeds = volt_hbm.shape[0]
    chans = LANES // 2
    width = LANES
    chunks = TIMES // GROUP
    steps = GROUP // STEP
    last = TIMES // STEP - 1
    grp, mem, pair = (lax.axis_index(n) for n in ("grp", "mem", "pair"))
    me = grp * mem_count + mem
    across = pair * grp_count + grp
    MESH = pl.DeviceIdType.MESH

    def load(src, dst, sem):
        return pltpu.make_async_copy(src, dst, sem)

    head = (TAPS - 1) * NFFT
    load(volt_hbm.at[:, 0:head], volt_ref.at[:, 0:head], head_sem).start()

    def volt_copy(k):
        cols = pl.ds(pl.multiple_of(head + k * (GROUP * NFFT), NFFT), GROUP * NFFT)
        return load(volt_hbm.at[:, cols], volt_ref.at[:, cols], volt_sem.at[k])

    for k in range(chunks):
        volt_copy(k).start()

    barrier = pltpu.get_barrier_semaphore()
    met = 0
    for dg in range(grp_count):
        for dm in range(mem_count):
            for dp in range(pairs):
                if (dg, dm, dp) == (0, 0, 0) or (dm != 0 and dp != 0):
                    continue
                there = {
                    "grp": (grp + dg) % grp_count,
                    "mem": (mem + dm) % mem_count,
                    "pair": (pair + dp) % pairs,
                }
                pl.semaphore_signal(barrier, inc=1, device_id=there, device_id_type=MESH)
                met += 1
    acc_ref[...] = jnp.zeros_like(acc_ref)
    fill_window(window_ref)
    fill_waves(wave_ref, cores, chans)
    load(volt_hbm.at[:, 0:head], volt_ref.at[:, 0:head], head_sem).wait()

    def spectra_copy(q, at, g, m):
        peer = g * mem_count + m
        return pltpu.make_async_remote_copy(
            src_ref=send_ref.at[(at[0], peer) + at[1:]],
            dst_ref=recv_ref.at[(at[0], me) + at[1:]],
            send_sem=send_sem.at[q],
            recv_sem=recv_sem.at[q],
            device_id={"grp": g, "mem": m},
            device_id_type=MESH,
        )

    def own_copy(q, at):
        own = (at[0], me) + at[1:]
        return load(send_ref.at[own], recv_ref.at[own], own_sem.at[q])

    def post(q, at, g, m):
        own = jnp.logical_and(g == grp, m == mem)

        @pl.when(jnp.logical_not(own))
        def _():
            spectra_copy(q, at, g, m).start()

        @pl.when(own)
        def _():
            own_copy(q, at).start()

    def place(s):
        h = s // 2
        far = (mem + 2) % 4 * ((3 - h) // 3) + (3 - mem) * (h % 3 % 2)
        near = (mem + 1 - 2 * (mem % 2)) * (h % 3 // 2) + mem * (h // 3)
        return (x_here + s + 1) % 2, far + near

    def post_all(q, at):
        def some(s, carry):
            x, m = place(s)
            for c in range(cores):
                post(q, at, x * cores + c, m)
            return carry

        lax.fori_loop(0, chips, some, 0)

    x_here = grp // cores

    def dft(k):
        volt_copy(k).wait()
        for t in range(GROUP):
            def tap(j):
                at = pl.multiple_of((k * GROUP + t + j) * NFFT, NFFT)
                return volt_ref[:, pl.ds(at, NFFT)].astype(jnp.float32) * window_ref[j : j + 1, :]

            total = tap(0)
            for j in range(1, TAPS):
                total = total + tap(j)
            framed_ref[t * feeds : (t + 1) * feeds, :] = total.astype(jnp.bfloat16)

        def tile(s, carry):
            x, m = place(s)
            chip = x * mem_count + m

            @pl.when(k == 0)
            def _():
                first = m * (CHANS // mem_count) + x * (cores * chans)
                fill_table(table_ref, wave_ref, chip, first)

            part = jnp.dot(framed_ref[...], table_ref[chip], preferred_element_type=jnp.float32)
            part = (part * (1.0 / math.sqrt(NFFT))).astype(jnp.bfloat16)
            for c in range(cores):
                peer = (x * cores + c) * mem_count + m
                for u in range(steps):
                    rows = part[u * STEP * feeds : (u + 1) * STEP * feeds, c * width : (c + 1) * width]
                    send_ref[k * steps + u, peer] = rows.reshape(STEP, feeds, width)

            @pl.when(jnp.logical_and(k == 0, s == 0))
            def _():
                pl.semaphore_wait(barrier, met)

            @pl.when(k == 0)
            def _():
                for c in range(cores):
                    for u in range(steps):
                        post(u, (u,), x * cores + c, m)

            return carry

        lax.fori_loop(0, chips, tile, 0)

        @pl.when(jnp.logical_and(k > 0, k < chunks - 1))
        def _():
            for u in range(steps):
                post_all(k * steps + u, (k * steps + u,))

        @pl.when(k == chunks - 1)
        def _():
            for u in range(steps - 1):
                post_all(k * steps + u, (k * steps + u,))
            for u in range(STEP):
                post_all(last + u, (last, u))

    lane = lax.broadcasted_iota(jnp.int32, (FEEDS, width), 1)
    sign = jnp.where(lane < chans, 1.0, -1.0)
    rows_each = BEAMS // (pairs * grp_count)
    half = BEAMS // pairs
    low = iota((half, width), 1) < chans
    owned = rows_each // mem_count

    def arrived(q, at):
        others = recv_ref.at[(at[0], pl.ds(0, peers - 1)) + at[1:]]
        return load(others, others, recv_sem.at[q])

    def left(q, at):
        others = send_ref.at[(at[0], pl.ds(0, peers - 1)) + at[1:]]
        return load(others, others, send_sem.at[q])

    others_count = pairs * grp_count - 1

    def power_copy(q, src, dst, p, g):
        return pltpu.make_async_remote_copy(
            src_ref=src,
            dst_ref=dst,
            send_sem=psend_sem.at[q],
            recv_sem=precv_sem.at[q],
            device_id={"pair": p, "grp": g},
            device_id_type=MESH,
        )

    def power_from(q, d, u, single):
        size = rows_each // 2 if single else rows_each
        at = u * (half if single else 0) + d * size
        return psend_ref.at[q, pl.ds(pl.multiple_of(at, size), size)]

    def power_to(q, src, u, single):
        size = rows_each // 2 if single else rows_each
        return precv_ref.at[q, src, pl.ds(u * size, size)]

    def power_own(q, u, single):
        src, dst = power_from(q, across, u, single), power_to(q, across, u, single)
        return load(src, dst, pown_sem.at[q + u])

    def power_arrived(q, u, single):
        others = power_to(q, pl.ds(0, others_count), u, single)
        return load(others, others, precv_sem.at[q + u])

    def power_left(q, u, single):
        others = power_to(q, pl.ds(0, others_count), u, single)
        return load(others, others, psend_sem.at[q + u])

    def calibrate(q, u, col):
        volt = recv_ref[q, :, u].reshape(FEEDS, width).astype(jnp.float32)
        cal = volt * gains_ref[:, :width] + pltpu.roll(volt, chans, 1) * gains_ref[:, width:]
        turned = pltpu.roll(cal, chans, 1) * sign
        x_ref[0:FEEDS, col : col + width] = cal.astype(jnp.bfloat16)
        x_ref[FEEDS : 2 * FEEDS, col : col + width] = turned.astype(jnp.bfloat16)

    def send_powers(q, u, p, single):
        for dg in range(grp_count - 1, -1, -1):
            g = (grp + dg) % grp_count
            here = jnp.logical_and(p == pair, g == grp)

            def go():
                src = power_from(q, p * grp_count + g, u, single)
                power_copy(q + u, src, power_to(q, across, u, single), p, g).start()

            if dg:
                go()
            else:
                pl.when(jnp.logical_not(here))(go)

                @pl.when(here)
                def _():
                    power_own(q, u, single).start()

    def beams(q):
        arrived(q, (q,)).wait()
        own_copy(q, (q,)).wait()
        for u in range(STEP):
            calibrate(q, u, u * width)

        def some(h, carry):
            p = (pair + 1 + h) % pairs
            rows = pl.ds(pl.multiple_of(p * half, half), half)
            formed = jnp.dot(w_ref[rows, :], x_ref[...], preferred_element_type=jnp.float32)
            squares = formed * formed
            one, two = squares[:, :width], squares[:, width:]
            first = one + pltpu.roll(one, chans, 1)
            second = two + pltpu.roll(two, chans, 1)
            power = jnp.where(low, first, second) * (1.0 / FEEDS)
            psend_ref[q, rows, :] = power.astype(jnp.bfloat16)
            send_powers(q, 0, p, False)
            return carry

        lax.fori_loop(0, pairs, some, 0)

    def beams_single(u):
        arrived(last + u, (last, u)).wait()
        own_copy(last + u, (last, u)).wait()
        calibrate(last, u, 0)

        def some(h, carry):
            p = (pair + 1 + h) % pairs
            rows = pl.ds(pl.multiple_of(p * half, half), half)
            formed = jnp.dot(
                w_ref[rows, :], x_ref[:, :width], preferred_element_type=jnp.float32
            )
            squares = formed * formed
            power = (squares + pltpu.roll(squares, chans, 1)) * (1.0 / FEEDS)
            power = power.reshape(grp_count, 2, rows_each // 2, width)
            lower = low[: rows_each // 2][None]
            power = jnp.where(lower, power[:, 0], power[:, 1]).reshape(half // 2, width)
            at = u * half + p * (half // 2)
            psend_ref[last, pl.ds(pl.multiple_of(at, half // 2), half // 2), :] = power.astype(
                jnp.bfloat16
            )
            send_powers(last, u, p, True)
            return carry

        lax.fori_loop(0, pairs, some, 0)

    def summed(q, s, rows):
        both = precv_ref[q, s, rows].astype(jnp.float32)
        for p in range(1, pairs):
            both = both + precv_ref[q, p * grp_count + s, rows].astype(jnp.float32)
        return both

    def dedisperse(q):
        for s in range(grp_count):
            for u in range(STEP):
                frame = (q * STEP + u).astype(jnp.float32)
                hit = shift_ref[s * chans : (s + 1) * chans, :] == frame
                at = (s * STEP + u) * chans
                t_ref[at : at + chans, :] = jnp.where(hit, HIT, MISS).astype(jnp.bfloat16)
        power_arrived(q, 0, False).wait()
        power_own(q, 0, False).wait()
        for s in range(grp_count):
            both = summed(q, s, slice(None))
            lhs_ref[:, s * width : (s + 1) * width] = both.astype(jnp.bfloat16)
        acc_ref[...] += jnp.dot(lhs_ref[...], t_ref[...], preferred_element_type=jnp.float32)

    def gather_single(u, into_ref):
        power_arrived(last, u, True).wait()
        power_own(last, u, True).wait()
        size = rows_each // 2
        lower = low[:size]
        for s in range(0, grp_count, 2):
            a, b = (summed(last, v, slice(u * size, (u + 1) * size)) for v in (s, s + 1))
            top = jnp.where(lower, a, pltpu.roll(b, chans, 1))
            bottom = jnp.where(lower, pltpu.roll(a, chans, 1), b)
            cols = slice(s * chans, (s + 2) * chans)
            into_ref[0:size, cols] = top.astype(jnp.bfloat16)
            into_ref[size : 2 * size, cols] = bottom.astype(jnp.bfloat16)

    def body(i, carry):
        @pl.when(i < chunks)
        def _():
            dft(i)

        @pl.when(i == 1)
        def _():
            fill_gains(gains_ref, gain_table_ref, gain_index_ref, grp, pair)
            fill_weights(w_ref, hit_ref, upper_ref, cylinder_ref)
            fill_shifts(shift_ref, hit_ref, delays_ref, chan_map_ref, mem)

        @pl.when(i >= 3)
        def _():
            lax.fori_loop(0, steps, lambda u, c: (dedisperse((i - 3) * steps + u), c)[1], 0)

        @pl.when(i >= 2)
        def _():
            count = jnp.minimum(steps, last - (i - 2) * steps)
            lax.fori_loop(0, count, lambda u, c: (beams((i - 2) * steps + u), c)[1], 0)

        return carry

    lax.fori_loop(0, chunks + 2, body, 0)
    beams_single(0)
    lax.fori_loop((chunks - 1) * steps, last, lambda q, c: (dedisperse(q), c)[1], 0)
    held = CHANS // mem_count
    hit = shift_ref[...] == float(TIMES - 2)
    t_ref[0:held, :] = jnp.where(hit, HIT, MISS).astype(jnp.bfloat16)
    gather_single(0, part_ref)
    acc_ref[...] += jnp.dot(part_ref[...], t_ref[0:held, :], preferred_element_type=jnp.float32)
    zsend_ref[...] = acc_ref[...].astype(jnp.bfloat16)

    def owned_rows(m):
        return pl.ds(pl.multiple_of(m * owned, owned), owned)

    def z_copy(d):
        m = (mem + d) % mem_count
        return pltpu.make_async_remote_copy(
            src_ref=zsend_ref.at[owned_rows(m)],
            dst_ref=zrecv_ref.at[d - 1],
            send_sem=zsend_sem.at[d - 1],
            recv_sem=zrecv_sem.at[d - 1],
            device_id={"mem": m},
            device_id_type=MESH,
        )

    def part_copy(d):
        m = (mem + d) % mem_count
        return pltpu.make_async_remote_copy(
            src_ref=part_ref.at[owned_rows(m)],
            dst_ref=parts_ref.at[mem],
            send_sem=lsend_sem.at[d - 1],
            recv_sem=lrecv_sem.at[d - 1],
            device_id={"mem": m},
            device_id_type=MESH,
        )

    order = sorted(range(1, mem_count), key=lambda d: abs(d - mem_count // 2))
    for d in order:
        z_copy(d).start()
    beams_single(1)

    def drain(q, carry):
        left(q, (q,)).wait()
        power_left(q, 0, False).wait()
        return carry

    lax.fori_loop(0, last, drain, 0)
    gather_single(1, part_ref)
    for d in order:
        part_copy(d).start()
    parts_ref[mem] = part_ref[owned_rows(mem), :]
    for u in range(STEP):
        left(last + u, (last, u)).wait()
        power_left(last, u, True).wait()
    total = acc_ref[owned_rows(mem), :]
    for d in order:
        z_copy(d).wait()
        total = total + zrecv_ref[d - 1].astype(jnp.float32)
    for d in order:
        part_copy(d).wait()
    for m in range(mem_count):
        total = total + jnp.dot(
            parts_ref[m], hit_ref[m * held : (m + 1) * held, :], preferred_element_type=jnp.float32
        )
    out_ref[...] = total


def fused_stage(sizes, gain_table, gain_index, cylinder_map, delays, chan_map, voltages):
    grp_count, mem_count, pairs, cores = sizes
    peers = grp_count * mem_count
    chips = peers // cores
    feeds, samples = voltages.shape
    series = TRIALS * TIMES
    count = TIMES // STEP
    groups = pairs * grp_count
    rows_each = BEAMS // groups
    owned = rows_each // mem_count
    bf16, f32 = jnp.bfloat16, jnp.float32
    dma = pltpu.SemaphoreType.DMA
    vmem = pl.BlockSpec(memory_space=pltpu.VMEM)
    return pl.pallas_call(
        functools.partial(fused_kernel, sizes),
        out_shape=jax.ShapeDtypeStruct((owned, series), f32),
        in_specs=[vmem] * 5 + [pl.BlockSpec(memory_space=pl.ANY)],
        out_specs=vmem,
        scratch_shapes=[
            pltpu.VMEM((feeds, samples), bf16),
            pltpu.VMEM((chips, NFFT, cores * LANES), bf16),
            pltpu.VMEM((BEAMS, 2 * FEEDS), bf16),
            pltpu.VMEM((GROUP * feeds, NFFT), bf16),
            pltpu.VMEM((count, peers, STEP, feeds, LANES), bf16),
            pltpu.VMEM((count, peers, STEP, feeds, LANES), bf16),
            pltpu.VMEM((2 * FEEDS, STEP * LANES), bf16),
            pltpu.VMEM((count, BEAMS, LANES), bf16),
            pltpu.VMEM((count, groups, rows_each, LANES), bf16),
            pltpu.VMEM((grp_count * LANES, series), bf16),
            pltpu.VMEM((rows_each, grp_count * LANES), bf16),
            pltpu.VMEM((rows_each, series), f32),
            pltpu.VMEM((rows_each, series), bf16),
            pltpu.VMEM((mem_count - 1, owned, series), bf16),
            pltpu.VMEM((TAPS, NFFT), f32),
            pltpu.VMEM((2, NFFT, cores * LANES), f32),
            pltpu.VMEM((FEEDS, 2 * LANES), f32),
            pltpu.VMEM((CHANS // mem_count, series), f32),
            pltpu.VMEM((FEEDS, FEEDS), bf16),
            pltpu.VMEM((2, CYL * 16, FEEDS), f32),
            pltpu.VMEM((rows_each, CHANS // mem_count), bf16),
            pltpu.VMEM((mem_count, owned, CHANS // mem_count), bf16),
            dma,
            dma((TIMES // GROUP,)),
            *[dma((count - 1 + STEP,))] * 6,
            *[dma((mem_count - 1,))] * 4,
        ],
        compiler_params=pltpu.CompilerParams(
            collective_id=0, has_side_effects=True, vmem_limit_bytes=FUSED_VMEM * 1024 * 1024
        ),
    )(gain_table, gain_index, cylinder_map, delays, chan_map, voltages)


def local_fused(voltages, gain_table, gain_index, cylinder_map, delays, chan_map):
    feeds, _, samples = voltages.shape
    sizes = (lax.axis_size("grp"), lax.axis_size("mem"), lax.axis_size("pair"), 2)
    series = fused_stage(
        sizes,
        gain_table,
        gain_index.T,
        cylinder_map.reshape(1, FEEDS),
        delays,
        chan_map.reshape(1, CHANS),
        voltages.reshape(feeds, samples),
    )
    return series.reshape(1, -1, TRIALS, TIMES)


def solution(mesh):
    shape = (mesh.shape["grp"], mesh.shape["mem"], mesh.shape["pair"])
    return jax.shard_map(
        local_fused if shape == (4, 4, 2) else local,
        mesh=mesh,
        in_specs=(P(PEERS, "pair", None), P(None, None, "mem"), P(), P(), P(), P()),
        out_specs=P("pair", PEERS, None, None),
        check_vma=False,
    )
```

```python
import functools
import math

import jax
import jax.numpy as jnp
from jax import lax
from jax.experimental import pallas as pl
from jax.experimental.pallas import tpu as pltpu
from jax.sharding import PartitionSpec as P

NFFT = 2048
CHANS = 1024
TAPS = 4
CYL = 4
NS = 256
FEEDS = 1024
BEAMS = 1024
TIMES = 32
TRIALS = 32
PEERS = ("grp", "mem")
LANES = 128


def pfb_window(tap_count, length):
    offsets = jnp.arange(tap_count * length, dtype=jnp.float32) + 0.5
    shaped = jnp.sinc((offsets - tap_count * length / 2.0) / length)
    taper_term = 0.5 - 0.5 * jnp.cos(offsets * (2.0 * math.pi / (tap_count * length)))
    return (shaped * taper_term).reshape(tap_count, length)


def turn(index, length):
    angles = (index % length).astype(jnp.float32) * (2.0 * math.pi / length)
    return lax.optimization_barrier((jnp.cos(angles), jnp.sin(angles)))


def times(a, b):
    return (a[0] * b[0] - a[1] * b[1], a[0] * b[1] + a[1] * b[0])


def channel_table(chan_of, quarter):
    chan = chan_of[None, :]
    high = turn(jnp.arange(16, dtype=jnp.int32)[:, None] * 128 * chan, NFFT)
    mid = turn(jnp.arange(16, dtype=jnp.int32)[:, None] * 8 * chan, NFFT)
    low = turn(jnp.arange(8, dtype=jnp.int32)[:, None] * chan + quarter[None, :] * (NFFT // 4), NFFT)
    upper = times([p[:, None, :] for p in high], [p[None, :, :] for p in mid])
    upper = lax.optimization_barrier(tuple(p.reshape(NFFT // 8, 1, -1) for p in upper))
    table = upper[0] * low[0][None] - upper[1] * low[1][None]
    return table.astype(jnp.bfloat16).reshape(NFFT, -1)


def beam_weights(cylinder_map):
    slots = jnp.arange(FEEDS, dtype=jnp.int32)
    hit = cylinder_map[:, None] == slots[None, :]
    slot_of = jnp.sum(jnp.where(hit, slots[:, None], 0), axis=0)
    cyl, pos = slot_of // NS, slot_of % NS
    e = jnp.arange(CYL, dtype=jnp.int32).reshape(CYL, 1, 1)
    hh = jnp.arange(16, dtype=jnp.int32).reshape(1, 16, 1)
    upper = turn(16 * pos * hh + (NS // CYL) * e * cyl, NS)
    a = jnp.arange(2, dtype=jnp.int32).reshape(2, 1, 1)
    hl = jnp.arange(8, dtype=jnp.int32).reshape(1, 8, 1)
    lower = turn(pos * (2 * hl + a), NS)
    real, imag = times(
        [p[None, :, :, None, :] for p in upper], [p[:, None, None, :, :] for p in lower]
    )
    return jnp.concatenate(
        [p.astype(jnp.bfloat16).reshape(BEAMS, FEEDS) for p in (real, imag)], axis=1
    )


BEAM_VMEM = 40
DFT_VMEM = 40
CHUNKS = (8, 20, 4)


def dft_kernel(frames, feeds, window_ref, volt_ref, table_ref, out_ref, framed_ref):
    @pl.when(pl.program_id(0) == 0)
    def _():
        for t in range(frames):
            total = volt_ref[:, t * NFFT : (t + 1) * NFFT].astype(jnp.float32) * window_ref[0:1, :]
            for j in range(1, TAPS):
                tap = volt_ref[:, (t + j) * NFFT : (t + j + 1) * NFFT].astype(jnp.float32)
                total = total + tap * window_ref[j : j + 1, :]
            framed_ref[t * feeds : (t + 1) * feeds, :] = total.astype(jnp.bfloat16)

    part = jnp.dot(framed_ref[...], table_ref[...], preferred_element_type=jnp.float32)
    part = (part * (1.0 / math.sqrt(NFFT))).astype(jnp.bfloat16)
    for i in range(out_ref.shape[0]):
        out_ref[i] = part[:, i * LANES : (i + 1) * LANES].reshape(frames, feeds, LANES)


def dft_stage(voltages, window, table, start, frames, peers):
    feeds = voltages.shape[0]
    length = (frames + TAPS - 1) * NFFT
    volt = lax.slice_in_dim(voltages, start * NFFT, start * NFFT + length, axis=2)
    volt = volt.reshape(feeds, length)
    width = table.shape[1] // peers
    if width != LANES:
        view = volt.reshape(feeds, frames + TAPS - 1, NFFT).astype(jnp.float32)
        framed = view[:, 0:frames] * window[0]
        for j in range(1, TAPS):
            framed = framed + view[:, j : j + frames] * window[j]
        rows = jnp.swapaxes(framed.astype(jnp.bfloat16), 0, 1).reshape(frames * feeds, NFFT)
        part = jnp.dot(rows, table, preferred_element_type=jnp.float32) * (1.0 / math.sqrt(NFFT))
        part = part.astype(jnp.bfloat16).reshape(frames, feeds, peers, width)
        return jnp.moveaxis(part, 2, 0)
    step = 4
    return pl.pallas_call(
        functools.partial(dft_kernel, frames, feeds),
        grid=(peers // step,),
        out_shape=jax.ShapeDtypeStruct((peers, frames, feeds, width), jnp.bfloat16),
        in_specs=[
            pl.BlockSpec((TAPS, NFFT), lambda i: (0, 0)),
            pl.BlockSpec((feeds, length), lambda i: (0, 0)),
            pl.BlockSpec((NFFT, step * width), lambda i: (0, i)),
        ],
        out_specs=pl.BlockSpec((step, frames, feeds, width), lambda i: (i, 0, 0, 0)),
        scratch_shapes=[pltpu.VMEM((frames * feeds, NFFT), jnp.bfloat16)],
        compiler_params=pltpu.CompilerParams(
            dimension_semantics=("arbitrary",), vmem_limit_bytes=DFT_VMEM * 1024 * 1024
        ),
    )(window, volt, table)


HIT = (TIMES - 1) / (TIMES * TIMES)
MISS = -1.0 / (TIMES * TIMES)


def beam_kernel(start, frames, chans, r_ref, ga_ref, gb_ref, w_ref, e_ref, *rest):
    acc_ref = rest[0] if len(rest) == 6 else None
    out_ref, even_ref, odd_ref, t_ref, p_ref = rest[-5:]
    width = 2 * chans
    lane = lax.broadcasted_iota(jnp.int32, (FEEDS, width), 1)
    sign = jnp.where(lane < chans, 1.0, -1.0)
    low = lax.broadcasted_iota(jnp.int32, (BEAMS, width), 1) < chans

    def calibrate(pair, x_ref):
        for u in range(2):
            i = 2 * pair + u
            volt = r_ref[:, i].reshape(FEEDS, width).astype(jnp.float32)
            cal = volt * ga_ref[...] + pltpu.roll(volt, chans, 1) * gb_ref[...]
            turned = pltpu.roll(cal, chans, 1) * sign
            cols = slice(u * width, (u + 1) * width)
            x_ref[0:FEEDS, cols] = cal.astype(jnp.bfloat16)
            x_ref[FEEDS : 2 * FEEDS, cols] = turned.astype(jnp.bfloat16)
            hit = e_ref[...] == start + i
            rows = pl.ds(pl.multiple_of(i * chans, chans), chans)
            t_ref[rows, :] = jnp.where(hit, HIT, MISS).astype(jnp.bfloat16)

    def form(pair, x_ref):
        beams = jnp.dot(w_ref[...], x_ref[...], preferred_element_type=jnp.float32)
        squares = beams * beams
        one, two = squares[:, :width], squares[:, width:]
        first = one + pltpu.roll(one, chans, 1)
        second = two + pltpu.roll(two, chans, 1)
        power = jnp.where(low, first, second) * (1.0 / FEEDS)
        p_ref[:, pl.ds(pl.multiple_of(pair * width, width), width)] = power.astype(jnp.bfloat16)

    pairs = frames // 2
    calibrate(0, even_ref)

    def body(k, carry):
        form(2 * k, even_ref)
        calibrate(2 * k + 1, odd_ref)
        form(2 * k + 1, odd_ref)
        calibrate(jnp.minimum(2 * k + 2, pairs - 1), even_ref)
        return carry

    lax.fori_loop(0, pairs // 2, body, 0)
    if pairs % 2:
        form(pairs - 1, even_ref)
    part = jnp.dot(p_ref[...], t_ref[...], preferred_element_type=jnp.float32)
    if acc_ref is not None:
        part = part + acc_ref[...]
    out_ref[...] = part.astype(out_ref.dtype)


def beam_stage(received, gains, weights, shift, start, acc):
    _, frames, _, width = received.shape
    chans = width // 2
    last = start + frames == TIMES
    held = jnp.bfloat16 if last else jnp.float32
    if width != LANES:
        volt = jnp.moveaxis(received, 1, 0).reshape(frames, FEEDS, 2, chans).astype(jnp.float32)
        ga, gb = (g.reshape(FEEDS, 2, chans) for g in gains)
        cal = (volt * ga + volt[:, :, ::-1] * gb).astype(jnp.bfloat16)
        turned = jnp.stack([cal[:, :, 1], -cal[:, :, 0]], axis=2)
        both = jnp.concatenate([cal, turned], axis=1)
        beams = jnp.einsum("bf,tfrc->btrc", weights, both, preferred_element_type=jnp.float32)
        power = jnp.sum(beams * beams, axis=2) * (1.0 / FEEDS)
        power = power.astype(jnp.bfloat16).reshape(BEAMS, frames * chans)
        frame = start + jnp.arange(frames, dtype=jnp.int32)[:, None, None]
        spread = jnp.where(shift[None] == frame, HIT, MISS).astype(jnp.bfloat16)
        spread = spread.reshape(frames * chans, -1)
        part = jnp.dot(power, spread, preferred_element_type=jnp.float32)
        return (part if acc is None else part + acc).astype(held)
    series = TRIALS * TIMES
    operands = (received, *gains, weights, shift) + (() if acc is None else (acc,))
    return pl.pallas_call(
        functools.partial(beam_kernel, start, frames, chans),
        out_shape=jax.ShapeDtypeStruct((BEAMS, series), held),
        in_specs=[pl.BlockSpec(memory_space=pltpu.VMEM)] * len(operands),
        out_specs=pl.BlockSpec(memory_space=pltpu.VMEM),
        scratch_shapes=[
            pltpu.VMEM((2 * FEEDS, 2 * width), jnp.bfloat16),
            pltpu.VMEM((2 * FEEDS, 2 * width), jnp.bfloat16),
            pltpu.VMEM((frames * chans, series), jnp.bfloat16),
            pltpu.VMEM((BEAMS, frames * chans), jnp.bfloat16),
        ],
        compiler_params=pltpu.CompilerParams(vmem_limit_bytes=BEAM_VMEM * 1024 * 1024),
    )(*operands)


def local(voltages, gain_table, gain_index, cylinder_map, delays, chan_map):
    feeds = voltages.shape[0]
    grp_count, mem_count = lax.axis_size("grp"), lax.axis_size("mem")
    peers = grp_count * mem_count
    chans = CHANS // peers
    grp, mem = lax.axis_index("grp"), lax.axis_index("mem")

    window = pfb_window(TAPS, NFFT)
    peer = jnp.arange(peers, dtype=jnp.int32)
    base = peer % mem_count * (CHANS // mem_count) + peer // mem_count * chans
    chan_of = base[:, None, None] + jnp.arange(chans, dtype=jnp.int32)[None, None, :]
    quarter = jnp.arange(2, dtype=jnp.int32)[None, :, None]
    chan_of, quarter = (
        jnp.broadcast_to(v, (peers, 2, chans)).reshape(-1) for v in (chan_of, quarter)
    )
    table = channel_table(chan_of, quarter)

    table = lax.optimization_barrier(table)
    starts = [sum(CHUNKS[:i]) for i in range(len(CHUNKS))]

    def exchange(spectra):
        return lax.all_to_all(spectra, PEERS, split_axis=0, concat_axis=0, tiled=True)

    spectra = [
        dft_stage(voltages, window, table, start, frames, peers)
        for start, frames in zip(starts, CHUNKS)
    ]
    received = [exchange(block) for block in spectra[:-1]]

    pairs = lax.axis_size("pair")
    cores = 2 if grp_count % 2 == 0 else 1
    owned = BEAMS // (pairs * peers)
    weights = beam_weights(cylinder_map)
    weights = weights.reshape(pairs, grp_count // cores, cores, mem_count * owned, 2 * FEEDS)
    weights = jnp.moveaxis(weights, 2, 0).reshape(BEAMS, 2 * FEEDS)
    gain_here = lax.dynamic_slice_in_dim(gain_table, grp * chans, chans, 2)
    gain_rows = gain_index[:, lax.axis_index("pair")]
    pick = gain_rows[:, None] == jnp.arange(gain_table.shape[0], dtype=jnp.int32)[None, :]
    gain_values = jnp.dot(
        pick.astype(jnp.float32),
        gain_here.reshape(gain_table.shape[0], 2 * chans),
        precision=lax.Precision.HIGHEST,
    )
    gain_real, gain_imag = gain_values[:, :chans], gain_values[:, chans:]
    gains = (
        jnp.concatenate([gain_real, gain_real], axis=1),
        jnp.concatenate([-gain_imag, gain_imag], axis=1),
    )

    first = mem * (CHANS // mem_count) + grp * chans
    freq = lax.dynamic_slice_in_dim(chan_map, first, chans, 0)
    column = jnp.arange(CHANS, dtype=jnp.int32)[:, None] == freq[None, :]
    delay = jnp.dot(
        delays.astype(jnp.bfloat16), column.astype(jnp.bfloat16), preferred_element_type=jnp.float32
    ).astype(jnp.int32)
    frame = jnp.arange(TIMES, dtype=jnp.int32)[None, None, :]
    shift = ((frame - delay.T[:, :, None]) % TIMES).reshape(chans, TRIALS * TIMES)

    part = None
    for i, start in enumerate(starts):
        if i == len(starts) - 1:
            last, part = lax.optimization_barrier((spectra[-1], held))
            received.append(exchange(last))
            part = beam_stage(received[i - 1], gains, weights, shift, starts[i - 1], part)
        if i == len(starts) - 2:
            held = part
            continue
        part = beam_stage(received[i], gains, weights, shift, start, part)

    series = TRIALS * TIMES
    groups = [[x * cores + c for c in range(cores)] for x in range(grp_count // cores)]
    part = part.reshape(cores, BEAMS // cores, series)
    part = lax.all_to_all(
        part, "grp", split_axis=0, concat_axis=0, axis_index_groups=groups, tiled=True
    )
    part = jnp.sum(part.astype(jnp.float32), axis=0).astype(jnp.bfloat16)
    part = part.reshape(pairs * peers // cores, owned, series)
    groups = [
        [
            (p * grp_count + x * cores + c) * mem_count + m
            for p in range(pairs)
            for x in range(grp_count // cores)
            for m in range(mem_count)
        ]
        for c in range(cores)
    ]
    part = lax.all_to_all(
        part, ("pair",) + PEERS, split_axis=0, concat_axis=0, axis_index_groups=groups, tiled=True
    )
    series = jnp.sum(part.astype(jnp.float32), axis=0)
    return series.reshape(1, owned, TRIALS, TIMES)

GROUP = 4
STEP = 2
AHEAD = 1
WINDOW = 2
FUSED_VMEM = 62


def wave(index, length):
    angles = (index & (length - 1)).astype(jnp.float32) * (2.0 * math.pi / length)
    return jnp.cos(angles), jnp.sin(angles)


def iota(shape, axis):
    return lax.broadcasted_iota(jnp.int32, shape, axis)


def fill_window(window_ref):
    shape = (TAPS, NFFT)
    offsets = (iota(shape, 0) * NFFT + iota(shape, 1)).astype(jnp.float32) + 0.5
    arg = (offsets - TAPS * NFFT / 2.0) / NFFT * math.pi
    taper = 0.5 - 0.5 * jnp.cos(offsets * (2.0 * math.pi / (TAPS * NFFT)))
    window_ref[...] = jnp.sin(arg) / arg * taper


def fill_waves(wave_ref, cores, chans):
    shape = (8, cores * LANES)
    lane = iota(shape, 1)
    chan = lane // LANES * chans + lane % chans
    quarter = lane % LANES // chans * (NFFT // 4)
    start = wave(iota(shape, 0) * chan + quarter, NFFT)
    wave_ref[0, 0:8, :], wave_ref[1, 0:8, :] = start
    step = 8
    while step < NFFT:
        turn_real, turn_imag = (v[None] for v in wave(chan * step, NFFT))
        real, imag = (wave_ref[r, 0:step, :].reshape(step // 8, *shape) for r in range(2))
        rows = slice(step, 2 * step)
        wave_ref[0, rows, :] = (real * turn_real - imag * turn_imag).reshape(step, shape[1])
        wave_ref[1, rows, :] = (real * turn_imag + imag * turn_real).reshape(step, shape[1])
        step *= 2


def fill_table(table_ref, wave_ref, chip, first):
    period = NFFT // LANES
    shape = (period, table_ref.shape[2])
    turn_real, turn_imag = (v[None] for v in wave(iota(shape, 0) * (first // LANES), period))
    block = 256

    def part(i, carry):
        rows = pl.ds(pl.multiple_of(i * block, block), block)
        real, imag = (wave_ref[r, rows, :].reshape(block // period, *shape) for r in range(2))
        filled = (real * turn_real - imag * turn_imag).reshape(block, shape[1])
        table_ref[chip, rows, :] = filled.astype(jnp.bfloat16)
        return carry

    lax.fori_loop(0, NFFT // block, part, 0)


def fill_gains(gains_ref, gain_table_ref, gain_index_ref, grp, pair):
    rows, _, held = gain_table_ref.shape
    chans = LANES // 2
    low = iota((rows, held), 1) < chans

    def twice(values):
        values = pltpu.roll(values, (held - grp * chans) % held, 1)
        return jnp.where(low, values, pltpu.roll(values, chans, 1))[:, :LANES]

    real = twice(gain_table_ref[:, 0, :])
    imag = twice(gain_table_ref[:, 1, :])
    imag = jnp.where(low[:, :LANES], -imag, imag)
    left = jnp.concatenate([real, imag], axis=1)
    index = gain_index_ref[pl.ds(pair, 1), :]
    pick = jnp.where(iota((rows, index.shape[1]), 0) == index, 1.0, 0.0).astype(jnp.bfloat16)
    total = None
    for _ in range(3):
        term = left.astype(jnp.bfloat16)
        left = left - term.astype(jnp.float32)
        picked = lax.dot_general(
            pick, term, (((0,), (0,)), ((), ())), preferred_element_type=jnp.float32
        )
        total = picked if total is None else total + picked
    gains_ref[...] = total


def fill_shifts(shift_ref, final_ref, delays_ref, chan_map_ref, mem):
    held, series = shift_ref.shape
    known = delays_ref[...].astype(jnp.float32).astype(jnp.bfloat16)
    shape = (TRIALS, series)
    spread = jnp.where(iota(shape, 1) // TIMES == iota(shape, 0), 1.0, 0.0).astype(jnp.bfloat16)
    frame = (iota((held, series), 1) % TIMES).astype(jnp.float32)

    def some(m, carry):
        rows = pl.ds(pl.multiple_of(m * held, held), held)
        column = jnp.where(iota((CHANS, held), 0) == chan_map_ref[:, rows], 1.0, 0.0)
        delay = jnp.dot(known, column.astype(jnp.bfloat16), preferred_element_type=jnp.float32)
        late = lax.dot_general(
            delay.astype(jnp.bfloat16),
            spread,
            (((0,), (0,)), ((), ())),
            preferred_element_type=jnp.float32,
        )
        shift = frame - late
        shift = jnp.where(shift < 0.0, shift + TIMES, shift)
        hit = shift == float(TIMES - 1)
        final_ref[rows, :] = jnp.where(hit, HIT, MISS).astype(jnp.bfloat16)

        @pl.when(m == mem)
        def _():
            shift_ref[...] = shift

        return carry

    lax.fori_loop(0, CHANS // held, some, 0)


def fill_weights(w_ref, hit_ref, upper_ref, cylinder_ref):
    block = 128

    def mark(i, carry):
        at = pl.multiple_of(i * block, block)
        hit = iota((block, FEEDS), 0) + at == cylinder_ref[...]
        hit_ref[pl.ds(at, block), :] = jnp.where(hit, 1.0, 0.0).astype(jnp.bfloat16)
        return carry

    lax.fori_loop(0, FEEDS // block, mark, 0)
    shape = (8, FEEDS)
    row, slot = iota(shape, 0), iota(shape, 1)
    digit = jnp.where(row == 0, slot // NS, jnp.where(row == 1, slot % NS // 16, slot % 16))
    digit = digit.astype(jnp.float32).astype(jnp.bfloat16)
    found = lax.dot_general(
        digit, hit_ref[...], (((1,), (1,)), ((), ())), preferred_element_type=jnp.float32
    )
    cyl = found[0:1].astype(jnp.int32)
    pos = (found[1:2] * 16.0 + found[2:3]).astype(jnp.int32)
    shape = (CYL * 16, FEEDS)
    row = iota(shape, 0)
    upper = wave(16 * pos * (row % 16) + (NS // CYL) * cyl * (row // 16), NS)
    upper_ref[0], upper_ref[1] = upper
    shape = (8, FEEDS)
    lower = [wave(pos * (2 * iota(shape, 0) + a), NS) for a in range(2)]

    def pack(i, carry):
        for a in range(2):
            parts = [[], []]
            for v in range(2):
                at = pl.ds(i * 2 + v, 1)
                real, imag = times((upper_ref[0, at, :], upper_ref[1, at, :]), lower[a])
                parts[0].append(real)
                parts[1].append(imag)
            rows = pl.ds(pl.multiple_of(a * (BEAMS // 2) + i * 16, 16), 16)
            for r in range(2):
                both = jnp.concatenate(parts[r], axis=0).astype(jnp.bfloat16)
                w_ref[rows, r * FEEDS : (r + 1) * FEEDS] = both
        return carry

    lax.fori_loop(0, CYL * 16 // 2, pack, 0)


def fused_kernel(
    sizes, gain_table_ref, gain_index_ref, cylinder_ref, delays_ref, chan_map_ref, volt_hbm, out_ref,
    volt_ref, table_ref, w_ref, framed_ref, send_ref, recv_ref, x_ref, psend_ref, precv_ref,
    t_ref, lhs_ref, acc_ref, zsend_ref, zrecv_ref,
    window_ref, wave_ref, gains_ref, shift_ref, hit_ref, upper_ref, part_ref, parts_ref,
    head_sem, volt_sem, send_sem, recv_sem, own_sem,
    psend_sem, precv_sem, pown_sem, zsend_sem, zrecv_sem, lsend_sem, lrecv_sem,
):
    grp_count, mem_count, pairs, cores = sizes
    peers = grp_count * mem_count
    chips = peers // cores
    feeds = volt_hbm.shape[0]
    chans = LANES // 2
    width = LANES
    chunks = TIMES // GROUP
    steps = GROUP // STEP
    last = TIMES // STEP - 1
    grp, mem, pair = (lax.axis_index(n) for n in ("grp", "mem", "pair"))
    me = grp * mem_count + mem
    across = pair * grp_count + grp
    MESH = pl.DeviceIdType.MESH

    def load(src, dst, sem):
        return pltpu.make_async_copy(src, dst, sem)

    head = (TAPS - 1) * NFFT
    load(volt_hbm.at[:, 0:head], volt_ref.at[:, 0:head], head_sem).start()

    def volt_copy(k):
        cols = pl.ds(pl.multiple_of(head + k * (GROUP * NFFT), NFFT), GROUP * NFFT)
        return load(volt_hbm.at[:, cols], volt_ref.at[:, cols], volt_sem.at[k])

    for k in range(chunks):
        volt_copy(k).start()

    barrier = pltpu.get_barrier_semaphore()
    met = 0
    for dg in range(grp_count):
        for dm in range(mem_count):
            for dp in range(pairs):
                if (dg, dm, dp) == (0, 0, 0) or (dm != 0 and dp != 0):
                    continue
                there = {
                    "grp": (grp + dg) % grp_count,
                    "mem": (mem + dm) % mem_count,
                    "pair": (pair + dp) % pairs,
                }
                pl.semaphore_signal(barrier, inc=1, device_id=there, device_id_type=MESH)
                met += 1
    acc_ref[...] = jnp.zeros_like(acc_ref)
    fill_window(window_ref)
    fill_waves(wave_ref, cores, chans)
    load(volt_hbm.at[:, 0:head], volt_ref.at[:, 0:head], head_sem).wait()

    def spectra_copy(q, at, g, m):
        peer = g * mem_count + m
        return pltpu.make_async_remote_copy(
            src_ref=send_ref.at[(at[0], peer) + at[1:]],
            dst_ref=recv_ref.at[(at[0], me) + at[1:]],
            send_sem=send_sem.at[q],
            recv_sem=recv_sem.at[q],
            device_id={"grp": g, "mem": m},
            device_id_type=MESH,
        )

    def own_copy(q, at):
        own = (at[0], me) + at[1:]
        return load(send_ref.at[own], recv_ref.at[own], own_sem.at[q])

    def post(q, at, g, m):
        own = jnp.logical_and(g == grp, m == mem)

        @pl.when(jnp.logical_not(own))
        def _():
            spectra_copy(q, at, g, m).start()

        @pl.when(own)
        def _():
            own_copy(q, at).start()

    def place(s):
        h = s // 2
        far = (mem + 2) % 4 * ((3 - h) // 3) + (3 - mem) * (h % 3 % 2)
        near = (mem + 1 - 2 * (mem % 2)) * (h % 3 // 2) + mem * (h // 3)
        return (x_here + s + 1) % 2, far + near

    def post_all(q, at):
        def some(s, carry):
            x, m = place(s)
            for c in range(cores):
                post(q, at, x * cores + c, m)
            return carry

        lax.fori_loop(0, chips, some, 0)

    x_here = grp // cores

    def dft(k):
        volt_copy(k).wait()
        for t in range(GROUP):
            def tap(j):
                at = pl.multiple_of((k * GROUP + t + j) * NFFT, NFFT)
                return volt_ref[:, pl.ds(at, NFFT)].astype(jnp.float32) * window_ref[j : j + 1, :]

            total = tap(0)
            for j in range(1, TAPS):
                total = total + tap(j)
            framed_ref[t * feeds : (t + 1) * feeds, :] = total.astype(jnp.bfloat16)

        def tile(s, carry):
            x, m = place(s)
            chip = x * mem_count + m

            @pl.when(k == 0)
            def _():
                first = m * (CHANS // mem_count) + x * (cores * chans)
                fill_table(table_ref, wave_ref, chip, first)

            part = jnp.dot(framed_ref[...], table_ref[chip], preferred_element_type=jnp.float32)
            part = (part * (1.0 / math.sqrt(NFFT))).astype(jnp.bfloat16)
            for c in range(cores):
                peer = (x * cores + c) * mem_count + m
                for u in range(steps):
                    rows = part[u * STEP * feeds : (u + 1) * STEP * feeds, c * width : (c + 1) * width]
                    send_ref[k * steps + u, peer] = rows.reshape(STEP, feeds, width)

            @pl.when(jnp.logical_and(k == 0, s == 0))
            def _():
                pl.semaphore_wait(barrier, met)

            @pl.when(k == 0)
            def _():
                for c in range(cores):
                    for u in range(steps):
                        post(u, (u,), x * cores + c, m)

            return carry

        lax.fori_loop(0, chips, tile, 0)

    lane = lax.broadcasted_iota(jnp.int32, (FEEDS, width), 1)
    sign = jnp.where(lane < chans, 1.0, -1.0)
    rows_each = BEAMS // (pairs * grp_count)
    half = BEAMS // pairs
    low = iota((half, width), 1) < chans
    owned = rows_each // mem_count

    def arrived(q, at):
        others = recv_ref.at[(at[0], pl.ds(0, peers - 1)) + at[1:]]
        return load(others, others, recv_sem.at[q])

    def left(q, at):
        others = send_ref.at[(at[0], pl.ds(0, peers - 1)) + at[1:]]
        return load(others, others, send_sem.at[q])

    others_count = pairs * grp_count - 1

    def power_copy(q, src, dst, p, g):
        return pltpu.make_async_remote_copy(
            src_ref=src,
            dst_ref=dst,
            send_sem=psend_sem.at[q],
            recv_sem=precv_sem.at[q],
            device_id={"pair": p, "grp": g},
            device_id_type=MESH,
        )

    def power_from(q, d, u, single):
        size = rows_each // 2 if single else rows_each
        at = u * (half if single else 0) + d * size
        return psend_ref.at[q, pl.ds(pl.multiple_of(at, size), size)]

    def power_to(q, src, u, single):
        size = rows_each // 2 if single else rows_each
        return precv_ref.at[q, src, pl.ds(u * size, size)]

    def power_own(q, u, single):
        src, dst = power_from(q, across, u, single), power_to(q, across, u, single)
        return load(src, dst, pown_sem.at[q + u])

    def power_arrived(q, u, single):
        others = power_to(q, pl.ds(0, others_count), u, single)
        return load(others, others, precv_sem.at[q + u])

    def power_left(q, u, single):
        others = power_to(q, pl.ds(0, others_count), u, single)
        return load(others, others, psend_sem.at[q + u])

    def calibrate(q, u, col):
        volt = recv_ref[q, :, u].reshape(FEEDS, width).astype(jnp.float32)
        cal = volt * gains_ref[:, :width] + pltpu.roll(volt, chans, 1) * gains_ref[:, width:]
        turned = pltpu.roll(cal, chans, 1) * sign
        x_ref[0:FEEDS, col : col + width] = cal.astype(jnp.bfloat16)
        x_ref[FEEDS : 2 * FEEDS, col : col + width] = turned.astype(jnp.bfloat16)

    def send_powers(q, u, p, single):
        for dg in range(grp_count - 1, -1, -1):
            g = (grp + dg) % grp_count
            here = jnp.logical_and(p == pair, g == grp)

            def go():
                src = power_from(q, p * grp_count + g, u, single)
                power_copy(q + u, src, power_to(q, across, u, single), p, g).start()

            if dg:
                go()
            else:
                pl.when(jnp.logical_not(here))(go)

                @pl.when(here)
                def _():
                    power_own(q, u, single).start()

    def beams(q):
        arrived(q, (q,)).wait()
        own_copy(q, (q,)).wait()
        for u in range(STEP):
            calibrate(q, u, u * width)

        def some(h, carry):
            p = (pair + 1 + h) % pairs
            rows = pl.ds(pl.multiple_of(p * half, half), half)
            formed = jnp.dot(w_ref[rows, :], x_ref[...], preferred_element_type=jnp.float32)
            squares = formed * formed
            one, two = squares[:, :width], squares[:, width:]
            first = one + pltpu.roll(one, chans, 1)
            second = two + pltpu.roll(two, chans, 1)
            power = jnp.where(low, first, second) * (1.0 / FEEDS)
            psend_ref[q, rows, :] = power.astype(jnp.bfloat16)
            send_powers(q, 0, p, False)
            return carry

        lax.fori_loop(0, pairs, some, 0)

    def beams_single(u):
        arrived(last + u, (last, u)).wait()
        own_copy(last + u, (last, u)).wait()
        calibrate(last, u, 0)

        def some(h, carry):
            p = (pair + 1 + h) % pairs
            rows = pl.ds(pl.multiple_of(p * half, half), half)
            formed = jnp.dot(
                w_ref[rows, :], x_ref[:, :width], preferred_element_type=jnp.float32
            )
            squares = formed * formed
            power = (squares + pltpu.roll(squares, chans, 1)) * (1.0 / FEEDS)
            power = power.reshape(grp_count, 2, rows_each // 2, width)
            lower = low[: rows_each // 2][None]
            power = jnp.where(lower, power[:, 0], power[:, 1]).reshape(half // 2, width)
            at = u * half + p * (half // 2)
            psend_ref[last, pl.ds(pl.multiple_of(at, half // 2), half // 2), :] = power.astype(
                jnp.bfloat16
            )
            send_powers(last, u, p, True)
            return carry

        lax.fori_loop(0, pairs, some, 0)

    def summed(q, s, rows):
        both = precv_ref[q, s, rows].astype(jnp.float32)
        for p in range(1, pairs):
            both = both + precv_ref[q, p * grp_count + s, rows].astype(jnp.float32)
        return both

    def dedisperse(q):
        for s in range(grp_count):
            for u in range(STEP):
                frame = (q * STEP + u).astype(jnp.float32)
                hit = shift_ref[s * chans : (s + 1) * chans, :] == frame
                at = (s * STEP + u) * chans
                t_ref[at : at + chans, :] = jnp.where(hit, HIT, MISS).astype(jnp.bfloat16)
        power_arrived(q, 0, False).wait()
        power_own(q, 0, False).wait()
        for s in range(grp_count):
            both = summed(q, s, slice(None))
            lhs_ref[:, s * width : (s + 1) * width] = both.astype(jnp.bfloat16)
        acc_ref[...] += jnp.dot(lhs_ref[...], t_ref[...], preferred_element_type=jnp.float32)

    def gather_single(u, into_ref):
        power_arrived(last, u, True).wait()
        power_own(last, u, True).wait()
        size = rows_each // 2
        lower = low[:size]
        for s in range(0, grp_count, 2):
            a, b = (summed(last, v, slice(u * size, (u + 1) * size)) for v in (s, s + 1))
            top = jnp.where(lower, a, pltpu.roll(b, chans, 1))
            bottom = jnp.where(lower, pltpu.roll(a, chans, 1), b)
            cols = slice(s * chans, (s + 2) * chans)
            into_ref[0:size, cols] = top.astype(jnp.bfloat16)
            into_ref[size : 2 * size, cols] = bottom.astype(jnp.bfloat16)

    def body(i, carry):
        j = i - AHEAD * steps
        ready = j + WINDOW

        @pl.when(jnp.logical_and(i % steps == 0, i // steps < chunks))
        def _():
            dft(i // steps)

        @pl.when(jnp.logical_and(ready >= steps, ready < last))
        def _():
            post_all(ready, (ready,))

        @pl.when(jnp.logical_and(ready >= last, ready < last + STEP))
        def _():
            post_all(ready, (last, ready - last))

        @pl.when(j == 0)
        def _():
            fill_gains(gains_ref, gain_table_ref, gain_index_ref, grp, pair)
            fill_weights(w_ref, hit_ref, upper_ref, cylinder_ref)
            fill_shifts(shift_ref, hit_ref, delays_ref, chan_map_ref, mem)

        @pl.when(j >= 2)
        def _():
            dedisperse(j - 2)

        @pl.when(jnp.logical_and(j >= 0, j < last))
        def _():
            beams(j)

        @pl.when(jnp.logical_and(j >= last, j < last + STEP - 1))
        def _():
            beams_single(j - last)

        return carry

    def owned_rows(m):
        return pl.ds(pl.multiple_of(m * owned, owned), owned)

    def z_copy(d):
        m = (mem + d) % mem_count
        return pltpu.make_async_remote_copy(
            src_ref=zsend_ref.at[owned_rows(m)],
            dst_ref=zrecv_ref.at[d - 1],
            send_sem=zsend_sem.at[d - 1],
            recv_sem=zrecv_sem.at[d - 1],
            device_id={"mem": m},
            device_id_type=MESH,
        )

    def part_copy(u, d):
        m = (mem + d) % mem_count
        at = u * (mem_count - 1) + d - 1
        return pltpu.make_async_remote_copy(
            src_ref=part_ref.at[u, owned_rows(m)],
            dst_ref=parts_ref.at[u, mem],
            send_sem=lsend_sem.at[at],
            recv_sem=lrecv_sem.at[at],
            device_id={"mem": m},
            device_id_type=MESH,
        )

    order = sorted(range(1, mem_count), key=lambda d: abs(d - mem_count // 2))

    def share(u):
        gather_single(u, part_ref.at[u])
        for d in order:
            part_copy(u, d).start()
        parts_ref[u, mem] = part_ref[u, owned_rows(mem), :]

    def finish(u):
        for d in order:
            part_copy(u, d).wait()
        held = CHANS // mem_count
        done = None
        for m in range(mem_count):
            more = jnp.dot(
                parts_ref[u, m],
                hit_ref[m * held : (m + 1) * held, :],
                preferred_element_type=jnp.float32,
            )
            done = more if done is None else done + more
        return done

    def drain(q, carry):
        left(q, (q,)).wait()
        power_left(q, 0, False).wait()
        return carry

    lax.fori_loop(0, AHEAD * steps + last + STEP - 1, body, 0)
    for q in range(last - 1, last):
        dedisperse(jnp.int32(q))
    zsend_ref[...] = acc_ref[...].astype(jnp.bfloat16)
    for d in order:
        z_copy(d).start()
    beams_single(STEP - 1)
    share(0)
    lax.fori_loop(0, last, drain, 0)
    share(1)
    for u in range(STEP):
        left(last + u, (last, u)).wait()
        power_left(last, u, True).wait()
    total = acc_ref[owned_rows(mem), :]
    for d in order:
        z_copy(d).wait()
        total = total + zrecv_ref[d - 1].astype(jnp.float32)
    before = finish(0)
    series = before.shape[1]
    time = iota(before.shape, 1) % TIMES
    wrapped = pltpu.roll(before, TIMES - 1, 1)
    total = total + jnp.where(time == TIMES - 1, wrapped, pltpu.roll(before, series - 1, 1))
    total = total + finish(1)
    out_ref[...] = total


def fused_stage(sizes, gain_table, gain_index, cylinder_map, delays, chan_map, voltages):
    grp_count, mem_count, pairs, cores = sizes
    peers = grp_count * mem_count
    chips = peers // cores
    feeds, samples = voltages.shape
    series = TRIALS * TIMES
    count = TIMES // STEP
    groups = pairs * grp_count
    rows_each = BEAMS // groups
    owned = rows_each // mem_count
    bf16, f32 = jnp.bfloat16, jnp.float32
    dma = pltpu.SemaphoreType.DMA
    vmem = pl.BlockSpec(memory_space=pltpu.VMEM)
    return pl.pallas_call(
        functools.partial(fused_kernel, sizes),
        out_shape=jax.ShapeDtypeStruct((owned, series), f32),
        in_specs=[vmem] * 5 + [pl.BlockSpec(memory_space=pl.ANY)],
        out_specs=vmem,
        scratch_shapes=[
            pltpu.VMEM((feeds, samples), bf16),
            pltpu.VMEM((chips, NFFT, cores * LANES), bf16),
            pltpu.VMEM((BEAMS, 2 * FEEDS), bf16),
            pltpu.VMEM((GROUP * feeds, NFFT), bf16),
            pltpu.VMEM((count, peers, STEP, feeds, LANES), bf16),
            pltpu.VMEM((count, peers, STEP, feeds, LANES), bf16),
            pltpu.VMEM((2 * FEEDS, STEP * LANES), bf16),
            pltpu.VMEM((count, BEAMS, LANES), bf16),
            pltpu.VMEM((count, groups, rows_each, LANES), bf16),
            pltpu.VMEM((grp_count * LANES, series), bf16),
            pltpu.VMEM((rows_each, grp_count * LANES), bf16),
            pltpu.VMEM((rows_each, series), f32),
            pltpu.VMEM((rows_each, series), bf16),
            pltpu.VMEM((mem_count - 1, owned, series), bf16),
            pltpu.VMEM((TAPS, NFFT), f32),
            pltpu.VMEM((2, NFFT, cores * LANES), f32),
            pltpu.VMEM((FEEDS, 2 * LANES), f32),
            pltpu.VMEM((CHANS // mem_count, series), f32),
            pltpu.VMEM((FEEDS, FEEDS), bf16),
            pltpu.VMEM((2, CYL * 16, FEEDS), f32),
            pltpu.VMEM((STEP, rows_each, CHANS // mem_count), bf16),
            pltpu.VMEM((STEP, mem_count, owned, CHANS // mem_count), bf16),
            dma,
            dma((TIMES // GROUP,)),
            *[dma((count - 1 + STEP,))] * 6,
            *[dma((mem_count - 1,))] * 2,
            *[dma((STEP * (mem_count - 1),))] * 2,
        ],
        compiler_params=pltpu.CompilerParams(
            collective_id=0, has_side_effects=True, vmem_limit_bytes=FUSED_VMEM * 1024 * 1024
        ),
    )(gain_table, gain_index, cylinder_map, delays, chan_map, voltages)


def local_fused(voltages, gain_table, gain_index, cylinder_map, delays, chan_map):
    feeds, _, samples = voltages.shape
    sizes = (lax.axis_size("grp"), lax.axis_size("mem"), lax.axis_size("pair"), 2)
    series = fused_stage(
        sizes,
        gain_table,
        gain_index.T,
        cylinder_map.reshape(1, FEEDS),
        delays,
        chan_map.reshape(1, CHANS),
        voltages.reshape(feeds, samples),
    )
    return series.reshape(1, -1, TRIALS, TIMES)


def solution(mesh):
    shape = (mesh.shape["grp"], mesh.shape["mem"], mesh.shape["pair"])
    return jax.shard_map(
        local_fused if shape == (4, 4, 2) else local,
        mesh=mesh,
        in_specs=(P(PEERS, "pair", None), P(None, None, "mem"), P(), P(), P(), P()),
        out_specs=P("pair", PEERS, None, None),
        check_vma=False,
    )
```

```python
import functools
import math

import jax
import jax.numpy as jnp
from jax import lax
from jax.experimental import pallas as pl
from jax.experimental.pallas import tpu as pltpu
from jax.sharding import PartitionSpec as P

NFFT = 2048
CHANS = 1024
TAPS = 4
CYL = 4
NS = 256
FEEDS = 1024
BEAMS = 1024
TIMES = 32
TRIALS = 32
PEERS = ("grp", "mem")
LANES = 128


def pfb_window(tap_count, length):
    offsets = jnp.arange(tap_count * length, dtype=jnp.float32) + 0.5
    shaped = jnp.sinc((offsets - tap_count * length / 2.0) / length)
    taper_term = 0.5 - 0.5 * jnp.cos(offsets * (2.0 * math.pi / (tap_count * length)))
    return (shaped * taper_term).reshape(tap_count, length)


def turn(index, length):
    angles = (index % length).astype(jnp.float32) * (2.0 * math.pi / length)
    return lax.optimization_barrier((jnp.cos(angles), jnp.sin(angles)))


def times(a, b):
    return (a[0] * b[0] - a[1] * b[1], a[0] * b[1] + a[1] * b[0])


def channel_table(chan_of, quarter):
    chan = chan_of[None, :]
    high = turn(jnp.arange(16, dtype=jnp.int32)[:, None] * 128 * chan, NFFT)
    mid = turn(jnp.arange(16, dtype=jnp.int32)[:, None] * 8 * chan, NFFT)
    low = turn(jnp.arange(8, dtype=jnp.int32)[:, None] * chan + quarter[None, :] * (NFFT // 4), NFFT)
    upper = times([p[:, None, :] for p in high], [p[None, :, :] for p in mid])
    upper = lax.optimization_barrier(tuple(p.reshape(NFFT // 8, 1, -1) for p in upper))
    table = upper[0] * low[0][None] - upper[1] * low[1][None]
    return table.astype(jnp.bfloat16).reshape(NFFT, -1)


def beam_weights(cylinder_map):
    slots = jnp.arange(FEEDS, dtype=jnp.int32)
    hit = cylinder_map[:, None] == slots[None, :]
    slot_of = jnp.sum(jnp.where(hit, slots[:, None], 0), axis=0)
    cyl, pos = slot_of // NS, slot_of % NS
    e = jnp.arange(CYL, dtype=jnp.int32).reshape(CYL, 1, 1)
    hh = jnp.arange(16, dtype=jnp.int32).reshape(1, 16, 1)
    upper = turn(16 * pos * hh + (NS // CYL) * e * cyl, NS)
    a = jnp.arange(2, dtype=jnp.int32).reshape(2, 1, 1)
    hl = jnp.arange(8, dtype=jnp.int32).reshape(1, 8, 1)
    lower = turn(pos * (2 * hl + a), NS)
    real, imag = times(
        [p[None, :, :, None, :] for p in upper], [p[:, None, None, :, :] for p in lower]
    )
    return jnp.concatenate(
        [p.astype(jnp.bfloat16).reshape(BEAMS, FEEDS) for p in (real, imag)], axis=1
    )


BEAM_VMEM = 40
DFT_VMEM = 40
CHUNKS = (8, 20, 4)


def dft_kernel(frames, feeds, window_ref, volt_ref, table_ref, out_ref, framed_ref):
    @pl.when(pl.program_id(0) == 0)
    def _():
        for t in range(frames):
            total = volt_ref[:, t * NFFT : (t + 1) * NFFT].astype(jnp.float32) * window_ref[0:1, :]
            for j in range(1, TAPS):
                tap = volt_ref[:, (t + j) * NFFT : (t + j + 1) * NFFT].astype(jnp.float32)
                total = total + tap * window_ref[j : j + 1, :]
            framed_ref[t * feeds : (t + 1) * feeds, :] = total.astype(jnp.bfloat16)

    part = jnp.dot(framed_ref[...], table_ref[...], preferred_element_type=jnp.float32)
    part = (part * (1.0 / math.sqrt(NFFT))).astype(jnp.bfloat16)
    for i in range(out_ref.shape[0]):
        out_ref[i] = part[:, i * LANES : (i + 1) * LANES].reshape(frames, feeds, LANES)


def dft_stage(voltages, window, table, start, frames, peers):
    feeds = voltages.shape[0]
    length = (frames + TAPS - 1) * NFFT
    volt = lax.slice_in_dim(voltages, start * NFFT, start * NFFT + length, axis=2)
    volt = volt.reshape(feeds, length)
    width = table.shape[1] // peers
    if width != LANES:
        view = volt.reshape(feeds, frames + TAPS - 1, NFFT).astype(jnp.float32)
        framed = view[:, 0:frames] * window[0]
        for j in range(1, TAPS):
            framed = framed + view[:, j : j + frames] * window[j]
        rows = jnp.swapaxes(framed.astype(jnp.bfloat16), 0, 1).reshape(frames * feeds, NFFT)
        part = jnp.dot(rows, table, preferred_element_type=jnp.float32) * (1.0 / math.sqrt(NFFT))
        part = part.astype(jnp.bfloat16).reshape(frames, feeds, peers, width)
        return jnp.moveaxis(part, 2, 0)
    step = 4
    return pl.pallas_call(
        functools.partial(dft_kernel, frames, feeds),
        grid=(peers // step,),
        out_shape=jax.ShapeDtypeStruct((peers, frames, feeds, width), jnp.bfloat16),
        in_specs=[
            pl.BlockSpec((TAPS, NFFT), lambda i: (0, 0)),
            pl.BlockSpec((feeds, length), lambda i: (0, 0)),
            pl.BlockSpec((NFFT, step * width), lambda i: (0, i)),
        ],
        out_specs=pl.BlockSpec((step, frames, feeds, width), lambda i: (i, 0, 0, 0)),
        scratch_shapes=[pltpu.VMEM((frames * feeds, NFFT), jnp.bfloat16)],
        compiler_params=pltpu.CompilerParams(
            dimension_semantics=("arbitrary",), vmem_limit_bytes=DFT_VMEM * 1024 * 1024
        ),
    )(window, volt, table)


HIT = (TIMES - 1) / (TIMES * TIMES)
MISS = -1.0 / (TIMES * TIMES)


def beam_kernel(start, frames, chans, r_ref, ga_ref, gb_ref, w_ref, e_ref, *rest):
    acc_ref = rest[0] if len(rest) == 6 else None
    out_ref, even_ref, odd_ref, t_ref, p_ref = rest[-5:]
    width = 2 * chans
    lane = lax.broadcasted_iota(jnp.int32, (FEEDS, width), 1)
    sign = jnp.where(lane < chans, 1.0, -1.0)
    low = lax.broadcasted_iota(jnp.int32, (BEAMS, width), 1) < chans

    def calibrate(pair, x_ref):
        for u in range(2):
            i = 2 * pair + u
            volt = r_ref[:, i].reshape(FEEDS, width).astype(jnp.float32)
            cal = volt * ga_ref[...] + pltpu.roll(volt, chans, 1) * gb_ref[...]
            turned = pltpu.roll(cal, chans, 1) * sign
            cols = slice(u * width, (u + 1) * width)
            x_ref[0:FEEDS, cols] = cal.astype(jnp.bfloat16)
            x_ref[FEEDS : 2 * FEEDS, cols] = turned.astype(jnp.bfloat16)
            hit = e_ref[...] == start + i
            rows = pl.ds(pl.multiple_of(i * chans, chans), chans)
            t_ref[rows, :] = jnp.where(hit, HIT, MISS).astype(jnp.bfloat16)

    def form(pair, x_ref):
        beams = jnp.dot(w_ref[...], x_ref[...], preferred_element_type=jnp.float32)
        squares = beams * beams
        one, two = squares[:, :width], squares[:, width:]
        first = one + pltpu.roll(one, chans, 1)
        second = two + pltpu.roll(two, chans, 1)
        power = jnp.where(low, first, second) * (1.0 / FEEDS)
        p_ref[:, pl.ds(pl.multiple_of(pair * width, width), width)] = power.astype(jnp.bfloat16)

    pairs = frames // 2
    calibrate(0, even_ref)

    def body(k, carry):
        form(2 * k, even_ref)
        calibrate(2 * k + 1, odd_ref)
        form(2 * k + 1, odd_ref)
        calibrate(jnp.minimum(2 * k + 2, pairs - 1), even_ref)
        return carry

    lax.fori_loop(0, pairs // 2, body, 0)
    if pairs % 2:
        form(pairs - 1, even_ref)
    part = jnp.dot(p_ref[...], t_ref[...], preferred_element_type=jnp.float32)
    if acc_ref is not None:
        part = part + acc_ref[...]
    out_ref[...] = part.astype(out_ref.dtype)


def beam_stage(received, gains, weights, shift, start, acc):
    _, frames, _, width = received.shape
    chans = width // 2
    last = start + frames == TIMES
    held = jnp.bfloat16 if last else jnp.float32
    if width != LANES:
        volt = jnp.moveaxis(received, 1, 0).reshape(frames, FEEDS, 2, chans).astype(jnp.float32)
        ga, gb = (g.reshape(FEEDS, 2, chans) for g in gains)
        cal = (volt * ga + volt[:, :, ::-1] * gb).astype(jnp.bfloat16)
        turned = jnp.stack([cal[:, :, 1], -cal[:, :, 0]], axis=2)
        both = jnp.concatenate([cal, turned], axis=1)
        beams = jnp.einsum("bf,tfrc->btrc", weights, both, preferred_element_type=jnp.float32)
        power = jnp.sum(beams * beams, axis=2) * (1.0 / FEEDS)
        power = power.astype(jnp.bfloat16).reshape(BEAMS, frames * chans)
        frame = start + jnp.arange(frames, dtype=jnp.int32)[:, None, None]
        spread = jnp.where(shift[None] == frame, HIT, MISS).astype(jnp.bfloat16)
        spread = spread.reshape(frames * chans, -1)
        part = jnp.dot(power, spread, preferred_element_type=jnp.float32)
        return (part if acc is None else part + acc).astype(held)
    series = TRIALS * TIMES
    operands = (received, *gains, weights, shift) + (() if acc is None else (acc,))
    return pl.pallas_call(
        functools.partial(beam_kernel, start, frames, chans),
        out_shape=jax.ShapeDtypeStruct((BEAMS, series), held),
        in_specs=[pl.BlockSpec(memory_space=pltpu.VMEM)] * len(operands),
        out_specs=pl.BlockSpec(memory_space=pltpu.VMEM),
        scratch_shapes=[
            pltpu.VMEM((2 * FEEDS, 2 * width), jnp.bfloat16),
            pltpu.VMEM((2 * FEEDS, 2 * width), jnp.bfloat16),
            pltpu.VMEM((frames * chans, series), jnp.bfloat16),
            pltpu.VMEM((BEAMS, frames * chans), jnp.bfloat16),
        ],
        compiler_params=pltpu.CompilerParams(vmem_limit_bytes=BEAM_VMEM * 1024 * 1024),
    )(*operands)


def local(voltages, gain_table, gain_index, cylinder_map, delays, chan_map):
    feeds = voltages.shape[0]
    grp_count, mem_count = lax.axis_size("grp"), lax.axis_size("mem")
    peers = grp_count * mem_count
    chans = CHANS // peers
    grp, mem = lax.axis_index("grp"), lax.axis_index("mem")

    window = pfb_window(TAPS, NFFT)
    peer = jnp.arange(peers, dtype=jnp.int32)
    base = peer % mem_count * (CHANS // mem_count) + peer // mem_count * chans
    chan_of = base[:, None, None] + jnp.arange(chans, dtype=jnp.int32)[None, None, :]
    quarter = jnp.arange(2, dtype=jnp.int32)[None, :, None]
    chan_of, quarter = (
        jnp.broadcast_to(v, (peers, 2, chans)).reshape(-1) for v in (chan_of, quarter)
    )
    table = channel_table(chan_of, quarter)

    table = lax.optimization_barrier(table)
    starts = [sum(CHUNKS[:i]) for i in range(len(CHUNKS))]

    def exchange(spectra):
        return lax.all_to_all(spectra, PEERS, split_axis=0, concat_axis=0, tiled=True)

    spectra = [
        dft_stage(voltages, window, table, start, frames, peers)
        for start, frames in zip(starts, CHUNKS)
    ]
    received = [exchange(block) for block in spectra[:-1]]

    pairs = lax.axis_size("pair")
    cores = 2 if grp_count % 2 == 0 else 1
    owned = BEAMS // (pairs * peers)
    weights = beam_weights(cylinder_map)
    weights = weights.reshape(pairs, grp_count // cores, cores, mem_count * owned, 2 * FEEDS)
    weights = jnp.moveaxis(weights, 2, 0).reshape(BEAMS, 2 * FEEDS)
    gain_here = lax.dynamic_slice_in_dim(gain_table, grp * chans, chans, 2)
    gain_rows = gain_index[:, lax.axis_index("pair")]
    pick = gain_rows[:, None] == jnp.arange(gain_table.shape[0], dtype=jnp.int32)[None, :]
    gain_values = jnp.dot(
        pick.astype(jnp.float32),
        gain_here.reshape(gain_table.shape[0], 2 * chans),
        precision=lax.Precision.HIGHEST,
    )
    gain_real, gain_imag = gain_values[:, :chans], gain_values[:, chans:]
    gains = (
        jnp.concatenate([gain_real, gain_real], axis=1),
        jnp.concatenate([-gain_imag, gain_imag], axis=1),
    )

    first = mem * (CHANS // mem_count) + grp * chans
    freq = lax.dynamic_slice_in_dim(chan_map, first, chans, 0)
    column = jnp.arange(CHANS, dtype=jnp.int32)[:, None] == freq[None, :]
    delay = jnp.dot(
        delays.astype(jnp.bfloat16), column.astype(jnp.bfloat16), preferred_element_type=jnp.float32
    ).astype(jnp.int32)
    frame = jnp.arange(TIMES, dtype=jnp.int32)[None, None, :]
    shift = ((frame - delay.T[:, :, None]) % TIMES).reshape(chans, TRIALS * TIMES)

    part = None
    for i, start in enumerate(starts):
        if i == len(starts) - 1:
            last, part = lax.optimization_barrier((spectra[-1], held))
            received.append(exchange(last))
            part = beam_stage(received[i - 1], gains, weights, shift, starts[i - 1], part)
        if i == len(starts) - 2:
            held = part
            continue
        part = beam_stage(received[i], gains, weights, shift, start, part)

    series = TRIALS * TIMES
    groups = [[x * cores + c for c in range(cores)] for x in range(grp_count // cores)]
    part = part.reshape(cores, BEAMS // cores, series)
    part = lax.all_to_all(
        part, "grp", split_axis=0, concat_axis=0, axis_index_groups=groups, tiled=True
    )
    part = jnp.sum(part.astype(jnp.float32), axis=0).astype(jnp.bfloat16)
    part = part.reshape(pairs * peers // cores, owned, series)
    groups = [
        [
            (p * grp_count + x * cores + c) * mem_count + m
            for p in range(pairs)
            for x in range(grp_count // cores)
            for m in range(mem_count)
        ]
        for c in range(cores)
    ]
    part = lax.all_to_all(
        part, ("pair",) + PEERS, split_axis=0, concat_axis=0, axis_index_groups=groups, tiled=True
    )
    series = jnp.sum(part.astype(jnp.float32), axis=0)
    return series.reshape(1, owned, TRIALS, TIMES)

GROUP = 4
STEP = 2
AHEAD = 1
WINDOW = 2
FUSED_VMEM = 62


def wave(index, length):
    angles = (index & (length - 1)).astype(jnp.float32) * (2.0 * math.pi / length)
    return jnp.cos(angles), jnp.sin(angles)


def iota(shape, axis):
    return lax.broadcasted_iota(jnp.int32, shape, axis)


def fill_window(window_ref):
    shape = (TAPS, NFFT)
    offsets = (iota(shape, 0) * NFFT + iota(shape, 1)).astype(jnp.float32) + 0.5
    arg = (offsets - TAPS * NFFT / 2.0) / NFFT * math.pi
    taper = 0.5 - 0.5 * jnp.cos(offsets * (2.0 * math.pi / (TAPS * NFFT)))
    window_ref[...] = jnp.sin(arg) / arg * taper


def fill_waves(wave_ref, cores, chans):
    shape = (8, cores * LANES)
    lane = iota(shape, 1)
    chan = lane // LANES * chans + lane % chans
    quarter = lane % LANES // chans * (NFFT // 4)
    start = wave(iota(shape, 0) * chan + quarter, NFFT)
    wave_ref[0, 0:8, :], wave_ref[1, 0:8, :] = start
    step = 8
    while step < NFFT:
        turn_real, turn_imag = (v[None] for v in wave(chan * step, NFFT))
        real, imag = (wave_ref[r, 0:step, :].reshape(step // 8, *shape) for r in range(2))
        rows = slice(step, 2 * step)
        wave_ref[0, rows, :] = (real * turn_real - imag * turn_imag).reshape(step, shape[1])
        wave_ref[1, rows, :] = (real * turn_imag + imag * turn_real).reshape(step, shape[1])
        step *= 2


def fill_table(table_ref, wave_ref, chip, first):
    period = NFFT // LANES
    shape = (period, table_ref.shape[2])
    turn_real, turn_imag = (v[None] for v in wave(iota(shape, 0) * (first // LANES), period))
    block = 256

    def part(i, carry):
        rows = pl.ds(pl.multiple_of(i * block, block), block)
        real, imag = (wave_ref[r, rows, :].reshape(block // period, *shape) for r in range(2))
        filled = (real * turn_real - imag * turn_imag).reshape(block, shape[1])
        table_ref[chip, rows, :] = filled.astype(jnp.bfloat16)
        return carry

    lax.fori_loop(0, NFFT // block, part, 0)


def fill_gains(gains_ref, gain_table_ref, gain_index_ref, grp, pair):
    rows, _, held = gain_table_ref.shape
    chans = LANES // 2
    low = iota((rows, held), 1) < chans

    def twice(values):
        values = pltpu.roll(values, (held - grp * chans) % held, 1)
        return jnp.where(low, values, pltpu.roll(values, chans, 1))[:, :LANES]

    real = twice(gain_table_ref[:, 0, :])
    imag = twice(gain_table_ref[:, 1, :])
    imag = jnp.where(low[:, :LANES], -imag, imag)
    left = jnp.concatenate([real, imag], axis=1)
    index = gain_index_ref[pl.ds(pair, 1), :]
    pick = jnp.where(iota((rows, index.shape[1]), 0) == index, 1.0, 0.0).astype(jnp.bfloat16)
    total = None
    for _ in range(3):
        term = left.astype(jnp.bfloat16)
        left = left - term.astype(jnp.float32)
        picked = lax.dot_general(
            pick, term, (((0,), (0,)), ((), ())), preferred_element_type=jnp.float32
        )
        total = picked if total is None else total + picked
    gains_ref[...] = total


def fill_shifts(shift_ref, final_ref, delays_ref, chan_map_ref, mem):
    held, series = shift_ref.shape
    known = delays_ref[...].astype(jnp.float32).astype(jnp.bfloat16)
    shape = (TRIALS, series)
    spread = jnp.where(iota(shape, 1) // TIMES == iota(shape, 0), 1.0, 0.0).astype(jnp.bfloat16)
    frame = (iota((held, series), 1) % TIMES).astype(jnp.float32)

    def some(m, carry):
        rows = pl.ds(pl.multiple_of(m * held, held), held)
        column = jnp.where(iota((CHANS, held), 0) == chan_map_ref[:, rows], 1.0, 0.0)
        delay = jnp.dot(known, column.astype(jnp.bfloat16), preferred_element_type=jnp.float32)
        late = lax.dot_general(
            delay.astype(jnp.bfloat16),
            spread,
            (((0,), (0,)), ((), ())),
            preferred_element_type=jnp.float32,
        )
        shift = frame - late
        shift = jnp.where(shift < 0.0, shift + TIMES, shift)
        hit = shift == float(TIMES - 1)
        final_ref[rows, :] = jnp.where(hit, HIT, MISS).astype(jnp.bfloat16)

        @pl.when(m == mem)
        def _():
            shift_ref[...] = shift

        return carry

    lax.fori_loop(0, CHANS // held, some, 0)


def fill_weights(w_ref, hit_ref, upper_ref, cylinder_ref):
    block = 128

    def mark(i, carry):
        at = pl.multiple_of(i * block, block)
        hit = iota((block, FEEDS), 0) + at == cylinder_ref[...]
        hit_ref[pl.ds(at, block), :] = jnp.where(hit, 1.0, 0.0).astype(jnp.bfloat16)
        return carry

    lax.fori_loop(0, FEEDS // block, mark, 0)
    shape = (8, FEEDS)
    row, slot = iota(shape, 0), iota(shape, 1)
    digit = jnp.where(row == 0, slot // NS, jnp.where(row == 1, slot % NS // 16, slot % 16))
    digit = digit.astype(jnp.float32).astype(jnp.bfloat16)
    found = lax.dot_general(
        digit, hit_ref[...], (((1,), (1,)), ((), ())), preferred_element_type=jnp.float32
    )
    cyl = found[0:1].astype(jnp.int32)
    pos = (found[1:2] * 16.0 + found[2:3]).astype(jnp.int32)
    shape = (CYL * 16, FEEDS)
    row = iota(shape, 0)
    upper = wave(16 * pos * (row % 16) + (NS // CYL) * cyl * (row // 16), NS)
    upper_ref[0], upper_ref[1] = upper
    shape = (8, FEEDS)
    lower = [wave(pos * (2 * iota(shape, 0) + a), NS) for a in range(2)]

    def pack(i, carry):
        for a in range(2):
            parts = [[], []]
            for v in range(2):
                at = pl.ds(i * 2 + v, 1)
                real, imag = times((upper_ref[0, at, :], upper_ref[1, at, :]), lower[a])
                parts[0].append(real)
                parts[1].append(imag)
            rows = pl.ds(pl.multiple_of(a * (BEAMS // 2) + i * 16, 16), 16)
            for r in range(2):
                both = jnp.concatenate(parts[r], axis=0).astype(jnp.bfloat16)
                w_ref[rows, r * FEEDS : (r + 1) * FEEDS] = both
        return carry

    lax.fori_loop(0, CYL * 16 // 2, pack, 0)


def fused_kernel(
    sizes, gain_table_ref, gain_index_ref, cylinder_ref, delays_ref, chan_map_ref, volt_hbm, out_ref,
    volt_ref, table_ref, w_ref, framed_ref, send_ref, recv_ref, x_ref, psend_ref, precv_ref,
    t_ref, lhs_ref, acc_ref, zsend_ref, zrecv_ref,
    window_ref, wave_ref, gains_ref, shift_ref, hit_ref, upper_ref, part_ref, parts_ref,
    head_sem, volt_sem, send_sem, recv_sem, own_sem,
    psend_sem, precv_sem, pown_sem, zsend_sem, zrecv_sem, lsend_sem, lrecv_sem,
):
    grp_count, mem_count, pairs, cores = sizes
    peers = grp_count * mem_count
    chips = peers // cores
    feeds = volt_hbm.shape[0]
    chans = LANES // 2
    width = LANES
    chunks = TIMES // GROUP
    steps = GROUP // STEP
    last = TIMES // STEP - 1
    grp, mem, pair = (lax.axis_index(n) for n in ("grp", "mem", "pair"))
    me = grp * mem_count + mem
    across = pair * grp_count + grp
    MESH = pl.DeviceIdType.MESH

    def load(src, dst, sem):
        return pltpu.make_async_copy(src, dst, sem)

    head = (TAPS - 1) * NFFT
    load(volt_hbm.at[:, 0:head], volt_ref.at[:, 0:head], head_sem).start()

    def volt_copy(k):
        cols = pl.ds(pl.multiple_of(head + k * (GROUP * NFFT), NFFT), GROUP * NFFT)
        return load(volt_hbm.at[:, cols], volt_ref.at[:, cols], volt_sem.at[k])

    for k in range(chunks):
        volt_copy(k).start()

    barrier = pltpu.get_barrier_semaphore()
    met = 0
    for dg in range(grp_count):
        for dm in range(mem_count):
            for dp in range(pairs):
                if (dg, dm, dp) == (0, 0, 0) or (dm != 0 and dp != 0):
                    continue
                there = {
                    "grp": (grp + dg) % grp_count,
                    "mem": (mem + dm) % mem_count,
                    "pair": (pair + dp) % pairs,
                }
                pl.semaphore_signal(barrier, inc=1, device_id=there, device_id_type=MESH)
                met += 1
    acc_ref[...] = jnp.zeros_like(acc_ref)
    fill_window(window_ref)
    fill_waves(wave_ref, cores, chans)
    load(volt_hbm.at[:, 0:head], volt_ref.at[:, 0:head], head_sem).wait()

    def spectra_copy(q, at, g, m):
        peer = g * mem_count + m
        return pltpu.make_async_remote_copy(
            src_ref=send_ref.at[(at[0], peer) + at[1:]],
            dst_ref=recv_ref.at[(at[0], me) + at[1:]],
            send_sem=send_sem.at[q],
            recv_sem=recv_sem.at[q],
            device_id={"grp": g, "mem": m},
            device_id_type=MESH,
        )

    def own_copy(q, at):
        own = (at[0], me) + at[1:]
        return load(send_ref.at[own], recv_ref.at[own], own_sem.at[q])

    def post(q, at, g, m):
        own = jnp.logical_and(g == grp, m == mem)

        @pl.when(jnp.logical_not(own))
        def _():
            spectra_copy(q, at, g, m).start()

        @pl.when(own)
        def _():
            own_copy(q, at).start()

    def place(s):
        h = s // 2
        one, two = (3 - h) // 3, h % 3 % 2
        one, two = one + (two - one) * (grp % cores), two + (one - two) * (grp % cores)
        far = (3 - mem) * one + (mem + 2) % 4 * two
        near = (mem + 1 - 2 * (mem % 2)) * (h % 3 // 2) + mem * (h // 3)
        return (x_here + s + 1) % 2, far + near

    def post_all(q, at):
        def some(s, carry):
            x, m = place(s)
            for c in range(cores):
                post(q, at, x * cores + (grp + c) % cores, m)
            return carry

        lax.fori_loop(0, chips, some, 0)

    x_here = grp // cores

    def dft(k):
        volt_copy(k).wait()
        for t in range(GROUP):
            def tap(j):
                at = pl.multiple_of((k * GROUP + t + j) * NFFT, NFFT)
                return volt_ref[:, pl.ds(at, NFFT)].astype(jnp.float32) * window_ref[j : j + 1, :]

            total = tap(0)
            for j in range(1, TAPS):
                total = total + tap(j)
            framed_ref[t * feeds : (t + 1) * feeds, :] = total.astype(jnp.bfloat16)

        def tile(s, carry):
            x, m = place(s)
            chip = x * mem_count + m

            @pl.when(k == 0)
            def _():
                first = m * (CHANS // mem_count) + x * (cores * chans)
                fill_table(table_ref, wave_ref, chip, first)

            part = jnp.dot(framed_ref[...], table_ref[chip], preferred_element_type=jnp.float32)
            part = (part * (1.0 / math.sqrt(NFFT))).astype(jnp.bfloat16)
            for c in range(cores):
                peer = (x * cores + c) * mem_count + m
                for u in range(steps):
                    rows = part[u * STEP * feeds : (u + 1) * STEP * feeds, c * width : (c + 1) * width]
                    send_ref[k * steps + u, peer] = rows.reshape(STEP, feeds, width)

            @pl.when(jnp.logical_and(k == 0, s == 0))
            def _():
                pl.semaphore_wait(barrier, met)

            @pl.when(k == 0)
            def _():
                for c in range(cores):
                    for u in range(steps):
                        post(u, (u,), x * cores + c, m)

            return carry

        lax.fori_loop(0, chips, tile, 0)

    lane = lax.broadcasted_iota(jnp.int32, (FEEDS, width), 1)
    sign = jnp.where(lane < chans, 1.0, -1.0)
    rows_each = BEAMS // (pairs * grp_count)
    half = BEAMS // pairs
    low = iota((half, width), 1) < chans
    owned = rows_each // mem_count

    def arrived(q, at):
        others = recv_ref.at[(at[0], pl.ds(0, peers - 1)) + at[1:]]
        return load(others, others, recv_sem.at[q])

    def left(q, at):
        others = send_ref.at[(at[0], pl.ds(0, peers - 1)) + at[1:]]
        return load(others, others, send_sem.at[q])

    others_count = pairs * grp_count - 1

    def power_copy(q, src, dst, p, g):
        return pltpu.make_async_remote_copy(
            src_ref=src,
            dst_ref=dst,
            send_sem=psend_sem.at[q],
            recv_sem=precv_sem.at[q],
            device_id={"pair": p, "grp": g},
            device_id_type=MESH,
        )

    def power_from(q, d, u, single):
        size = rows_each // 2 if single else rows_each
        at = u * (half if single else 0) + d * size
        return psend_ref.at[q, pl.ds(pl.multiple_of(at, size), size)]

    def power_to(q, src, u, single):
        size = rows_each // 2 if single else rows_each
        return precv_ref.at[q, src, pl.ds(u * size, size)]

    def power_own(q, u, single):
        src, dst = power_from(q, across, u, single), power_to(q, across, u, single)
        return load(src, dst, pown_sem.at[q + u])

    def power_arrived(q, u, single):
        others = power_to(q, pl.ds(0, others_count), u, single)
        return load(others, others, precv_sem.at[q + u])

    def power_left(q, u, single):
        others = power_to(q, pl.ds(0, others_count), u, single)
        return load(others, others, psend_sem.at[q + u])

    def calibrate(q, u, col):
        volt = recv_ref[q, :, u].reshape(FEEDS, width).astype(jnp.float32)
        cal = volt * gains_ref[:, :width] + pltpu.roll(volt, chans, 1) * gains_ref[:, width:]
        turned = pltpu.roll(cal, chans, 1) * sign
        x_ref[0:FEEDS, col : col + width] = cal.astype(jnp.bfloat16)
        x_ref[FEEDS : 2 * FEEDS, col : col + width] = turned.astype(jnp.bfloat16)

    def send_powers(q, u, p, single):
        for dg in range(grp_count - 1, -1, -1):
            g = (grp + dg) % grp_count
            here = jnp.logical_and(p == pair, g == grp)

            def go():
                src = power_from(q, p * grp_count + g, u, single)
                power_copy(q + u, src, power_to(q, across, u, single), p, g).start()

            if dg:
                go()
            else:
                pl.when(jnp.logical_not(here))(go)

                @pl.when(here)
                def _():
                    power_own(q, u, single).start()

    def beams(q):
        arrived(q, (q,)).wait()
        own_copy(q, (q,)).wait()
        for u in range(STEP):
            calibrate(q, u, u * width)

        def some(h, carry):
            p = (pair + 1 + h) % pairs
            rows = pl.ds(pl.multiple_of(p * half, half), half)
            formed = jnp.dot(w_ref[rows, :], x_ref[...], preferred_element_type=jnp.float32)
            squares = formed * formed
            one, two = squares[:, :width], squares[:, width:]
            first = one + pltpu.roll(one, chans, 1)
            second = two + pltpu.roll(two, chans, 1)
            power = jnp.where(low, first, second) * (1.0 / FEEDS)
            psend_ref[q, rows, :] = power.astype(jnp.bfloat16)
            send_powers(q, 0, p, False)
            return carry

        lax.fori_loop(0, pairs, some, 0)

    def beams_single(u):
        arrived(last + u, (last, u)).wait()
        own_copy(last + u, (last, u)).wait()
        calibrate(last, u, 0)

        def some(h, carry):
            p = (pair + 1 + h) % pairs
            rows = pl.ds(pl.multiple_of(p * half, half), half)
            formed = jnp.dot(
                w_ref[rows, :], x_ref[:, :width], preferred_element_type=jnp.float32
            )
            squares = formed * formed
            power = (squares + pltpu.roll(squares, chans, 1)) * (1.0 / FEEDS)
            power = power.reshape(grp_count, 2, rows_each // 2, width)
            lower = low[: rows_each // 2][None]
            power = jnp.where(lower, power[:, 0], power[:, 1]).reshape(half // 2, width)
            at = u * half + p * (half // 2)
            psend_ref[last, pl.ds(pl.multiple_of(at, half // 2), half // 2), :] = power.astype(
                jnp.bfloat16
            )
            send_powers(last, u, p, True)
            return carry

        lax.fori_loop(0, pairs, some, 0)

    def summed(q, s, rows):
        both = precv_ref[q, s, rows].astype(jnp.float32)
        for p in range(1, pairs):
            both = both + precv_ref[q, p * grp_count + s, rows].astype(jnp.float32)
        return both

    def dedisperse(q):
        for s in range(grp_count):
            for u in range(STEP):
                frame = (q * STEP + u).astype(jnp.float32)
                hit = shift_ref[s * chans : (s + 1) * chans, :] == frame
                at = (s * STEP + u) * chans
                t_ref[at : at + chans, :] = jnp.where(hit, HIT, MISS).astype(jnp.bfloat16)
        power_arrived(q, 0, False).wait()
        power_own(q, 0, False).wait()
        for s in range(grp_count):
            both = summed(q, s, slice(None))
            lhs_ref[:, s * width : (s + 1) * width] = both.astype(jnp.bfloat16)
        acc_ref[...] += jnp.dot(lhs_ref[...], t_ref[...], preferred_element_type=jnp.float32)

    def gather_single(u, into_ref):
        power_arrived(last, u, True).wait()
        power_own(last, u, True).wait()
        size = rows_each // 2
        lower = low[:size]
        for s in range(0, grp_count, 2):
            a, b = (summed(last, v, slice(u * size, (u + 1) * size)) for v in (s, s + 1))
            top = jnp.where(lower, a, pltpu.roll(b, chans, 1))
            bottom = jnp.where(lower, pltpu.roll(a, chans, 1), b)
            cols = slice(s * chans, (s + 2) * chans)
            into_ref[0:size, cols] = top.astype(jnp.bfloat16)
            into_ref[size : 2 * size, cols] = bottom.astype(jnp.bfloat16)

    def body(i, carry):
        j = i - AHEAD * steps
        ready = j + WINDOW

        @pl.when(jnp.logical_and(i % steps == 0, i // steps < chunks))
        def _():
            dft(i // steps)

        @pl.when(jnp.logical_and(ready >= steps, ready < last))
        def _():
            post_all(ready, (ready,))

        @pl.when(jnp.logical_and(ready >= last, ready < last + STEP))
        def _():
            post_all(ready, (last, ready - last))

        @pl.when(j == 0)
        def _():
            fill_gains(gains_ref, gain_table_ref, gain_index_ref, grp, pair)
            fill_weights(w_ref, hit_ref, upper_ref, cylinder_ref)
            fill_shifts(shift_ref, hit_ref, delays_ref, chan_map_ref, mem)

        @pl.when(j >= 2)
        def _():
            dedisperse(j - 2)

        @pl.when(jnp.logical_and(j >= 0, j < last))
        def _():
            beams(j)

        @pl.when(jnp.logical_and(j >= last, j < last + STEP - 1))
        def _():
            beams_single(j - last)

        return carry

    def owned_rows(m):
        return pl.ds(pl.multiple_of(m * owned, owned), owned)

    def z_copy(d):
        m = (mem + d) % mem_count
        return pltpu.make_async_remote_copy(
            src_ref=zsend_ref.at[owned_rows(m)],
            dst_ref=zrecv_ref.at[d - 1],
            send_sem=zsend_sem.at[d - 1],
            recv_sem=zrecv_sem.at[d - 1],
            device_id={"mem": m},
            device_id_type=MESH,
        )

    def part_copy(u, d):
        m = (mem + d) % mem_count
        at = u * (mem_count - 1) + d - 1
        return pltpu.make_async_remote_copy(
            src_ref=part_ref.at[u, owned_rows(m)],
            dst_ref=parts_ref.at[u, mem],
            send_sem=lsend_sem.at[at],
            recv_sem=lrecv_sem.at[at],
            device_id={"mem": m},
            device_id_type=MESH,
        )

    order = sorted(range(1, mem_count), key=lambda d: abs(d - mem_count // 2))

    def share(u):
        gather_single(u, part_ref.at[u])
        for d in order:
            part_copy(u, d).start()
        parts_ref[u, mem] = part_ref[u, owned_rows(mem), :]

    def finish(u):
        for d in order:
            part_copy(u, d).wait()
        held = CHANS // mem_count
        done = None
        for m in range(mem_count):
            more = jnp.dot(
                parts_ref[u, m],
                hit_ref[m * held : (m + 1) * held, :],
                preferred_element_type=jnp.float32,
            )
            done = more if done is None else done + more
        return done

    def drain(q, carry):
        left(q, (q,)).wait()
        power_left(q, 0, False).wait()
        return carry

    lax.fori_loop(0, AHEAD * steps + last + STEP - 1, body, 0)
    for q in range(last - 1, last):
        dedisperse(jnp.int32(q))
    zsend_ref[...] = acc_ref[...].astype(jnp.bfloat16)
    for d in order:
        z_copy(d).start()
    beams_single(STEP - 1)
    share(0)
    lax.fori_loop(0, last, drain, 0)
    share(1)
    for u in range(STEP):
        left(last + u, (last, u)).wait()
        power_left(last, u, True).wait()
    total = acc_ref[owned_rows(mem), :]
    for d in order:
        z_copy(d).wait()
        total = total + zrecv_ref[d - 1].astype(jnp.float32)
    before = finish(0)
    series = before.shape[1]
    time = iota(before.shape, 1) % TIMES
    wrapped = pltpu.roll(before, TIMES - 1, 1)
    total = total + jnp.where(time == TIMES - 1, wrapped, pltpu.roll(before, series - 1, 1))
    total = total + finish(1)
    out_ref[...] = total


def fused_stage(sizes, gain_table, gain_index, cylinder_map, delays, chan_map, voltages):
    grp_count, mem_count, pairs, cores = sizes
    peers = grp_count * mem_count
    chips = peers // cores
    feeds, samples = voltages.shape
    series = TRIALS * TIMES
    count = TIMES // STEP
    groups = pairs * grp_count
    rows_each = BEAMS // groups
    owned = rows_each // mem_count
    bf16, f32 = jnp.bfloat16, jnp.float32
    dma = pltpu.SemaphoreType.DMA
    vmem = pl.BlockSpec(memory_space=pltpu.VMEM)
    return pl.pallas_call(
        functools.partial(fused_kernel, sizes),
        out_shape=jax.ShapeDtypeStruct((owned, series), f32),
        in_specs=[vmem] * 5 + [pl.BlockSpec(memory_space=pl.ANY)],
        out_specs=vmem,
        scratch_shapes=[
            pltpu.VMEM((feeds, samples), bf16),
            pltpu.VMEM((chips, NFFT, cores * LANES), bf16),
            pltpu.VMEM((BEAMS, 2 * FEEDS), bf16),
            pltpu.VMEM((GROUP * feeds, NFFT), bf16),
            pltpu.VMEM((count, peers, STEP, feeds, LANES), bf16),
            pltpu.VMEM((count, peers, STEP, feeds, LANES), bf16),
            pltpu.VMEM((2 * FEEDS, STEP * LANES), bf16),
            pltpu.VMEM((count, BEAMS, LANES), bf16),
            pltpu.VMEM((count, groups, rows_each, LANES), bf16),
            pltpu.VMEM((grp_count * LANES, series), bf16),
            pltpu.VMEM((rows_each, grp_count * LANES), bf16),
            pltpu.VMEM((rows_each, series), f32),
            pltpu.VMEM((rows_each, series), bf16),
            pltpu.VMEM((mem_count - 1, owned, series), bf16),
            pltpu.VMEM((TAPS, NFFT), f32),
            pltpu.VMEM((2, NFFT, cores * LANES), f32),
            pltpu.VMEM((FEEDS, 2 * LANES), f32),
            pltpu.VMEM((CHANS // mem_count, series), f32),
            pltpu.VMEM((FEEDS, FEEDS), bf16),
            pltpu.VMEM((2, CYL * 16, FEEDS), f32),
            pltpu.VMEM((STEP, rows_each, CHANS // mem_count), bf16),
            pltpu.VMEM((STEP, mem_count, owned, CHANS // mem_count), bf16),
            dma,
            dma((TIMES // GROUP,)),
            *[dma((count - 1 + STEP,))] * 6,
            *[dma((mem_count - 1,))] * 2,
            *[dma((STEP * (mem_count - 1),))] * 2,
        ],
        compiler_params=pltpu.CompilerParams(
            collective_id=0, has_side_effects=True, vmem_limit_bytes=FUSED_VMEM * 1024 * 1024
        ),
    )(gain_table, gain_index, cylinder_map, delays, chan_map, voltages)


def local_fused(voltages, gain_table, gain_index, cylinder_map, delays, chan_map):
    feeds, _, samples = voltages.shape
    sizes = (lax.axis_size("grp"), lax.axis_size("mem"), lax.axis_size("pair"), 2)
    series = fused_stage(
        sizes,
        gain_table,
        gain_index.T,
        cylinder_map.reshape(1, FEEDS),
        delays,
        chan_map.reshape(1, CHANS),
        voltages.reshape(feeds, samples),
    )
    return series.reshape(1, -1, TRIALS, TIMES)


def solution(mesh):
    shape = (mesh.shape["grp"], mesh.shape["mem"], mesh.shape["pair"])
    return jax.shard_map(
        local_fused if shape == (4, 4, 2) else local,
        mesh=mesh,
        in_specs=(P(PEERS, "pair", None), P(None, None, "mem"), P(), P(), P(), P()),
        out_specs=P("pair", PEERS, None, None),
        check_vma=False,
    )
```

```python
import functools
import math

import jax
import jax.numpy as jnp
from jax import lax
from jax.experimental import pallas as pl
from jax.experimental.pallas import tpu as pltpu
from jax.sharding import PartitionSpec as P

NFFT = 2048
CHANS = 1024
TAPS = 4
CYL = 4
NS = 256
FEEDS = 1024
BEAMS = 1024
TIMES = 32
TRIALS = 32
PEERS = ("grp", "mem")
LANES = 128


def pfb_window(tap_count, length):
    offsets = jnp.arange(tap_count * length, dtype=jnp.float32) + 0.5
    shaped = jnp.sinc((offsets - tap_count * length / 2.0) / length)
    taper_term = 0.5 - 0.5 * jnp.cos(offsets * (2.0 * math.pi / (tap_count * length)))
    return (shaped * taper_term).reshape(tap_count, length)


def turn(index, length):
    angles = (index % length).astype(jnp.float32) * (2.0 * math.pi / length)
    return lax.optimization_barrier((jnp.cos(angles), jnp.sin(angles)))


def times(a, b):
    return (a[0] * b[0] - a[1] * b[1], a[0] * b[1] + a[1] * b[0])


def channel_table(chan_of, quarter):
    chan = chan_of[None, :]
    high = turn(jnp.arange(16, dtype=jnp.int32)[:, None] * 128 * chan, NFFT)
    mid = turn(jnp.arange(16, dtype=jnp.int32)[:, None] * 8 * chan, NFFT)
    low = turn(jnp.arange(8, dtype=jnp.int32)[:, None] * chan + quarter[None, :] * (NFFT // 4), NFFT)
    upper = times([p[:, None, :] for p in high], [p[None, :, :] for p in mid])
    upper = lax.optimization_barrier(tuple(p.reshape(NFFT // 8, 1, -1) for p in upper))
    table = upper[0] * low[0][None] - upper[1] * low[1][None]
    return table.astype(jnp.bfloat16).reshape(NFFT, -1)


def beam_weights(cylinder_map):
    slots = jnp.arange(FEEDS, dtype=jnp.int32)
    hit = cylinder_map[:, None] == slots[None, :]
    slot_of = jnp.sum(jnp.where(hit, slots[:, None], 0), axis=0)
    cyl, pos = slot_of // NS, slot_of % NS
    e = jnp.arange(CYL, dtype=jnp.int32).reshape(CYL, 1, 1)
    hh = jnp.arange(16, dtype=jnp.int32).reshape(1, 16, 1)
    upper = turn(16 * pos * hh + (NS // CYL) * e * cyl, NS)
    a = jnp.arange(2, dtype=jnp.int32).reshape(2, 1, 1)
    hl = jnp.arange(8, dtype=jnp.int32).reshape(1, 8, 1)
    lower = turn(pos * (2 * hl + a), NS)
    real, imag = times(
        [p[None, :, :, None, :] for p in upper], [p[:, None, None, :, :] for p in lower]
    )
    return jnp.concatenate(
        [p.astype(jnp.bfloat16).reshape(BEAMS, FEEDS) for p in (real, imag)], axis=1
    )


BEAM_VMEM = 40
DFT_VMEM = 40
CHUNKS = (8, 20, 4)


def dft_kernel(frames, feeds, window_ref, volt_ref, table_ref, out_ref, framed_ref):
    @pl.when(pl.program_id(0) == 0)
    def _():
        for t in range(frames):
            total = volt_ref[:, t * NFFT : (t + 1) * NFFT].astype(jnp.float32) * window_ref[0:1, :]
            for j in range(1, TAPS):
                tap = volt_ref[:, (t + j) * NFFT : (t + j + 1) * NFFT].astype(jnp.float32)
                total = total + tap * window_ref[j : j + 1, :]
            framed_ref[t * feeds : (t + 1) * feeds, :] = total.astype(jnp.bfloat16)

    part = jnp.dot(framed_ref[...], table_ref[...], preferred_element_type=jnp.float32)
    part = (part * (1.0 / math.sqrt(NFFT))).astype(jnp.bfloat16)
    for i in range(out_ref.shape[0]):
        out_ref[i] = part[:, i * LANES : (i + 1) * LANES].reshape(frames, feeds, LANES)


def dft_stage(voltages, window, table, start, frames, peers):
    feeds = voltages.shape[0]
    length = (frames + TAPS - 1) * NFFT
    volt = lax.slice_in_dim(voltages, start * NFFT, start * NFFT + length, axis=2)
    volt = volt.reshape(feeds, length)
    width = table.shape[1] // peers
    if width != LANES:
        view = volt.reshape(feeds, frames + TAPS - 1, NFFT).astype(jnp.float32)
        framed = view[:, 0:frames] * window[0]
        for j in range(1, TAPS):
            framed = framed + view[:, j : j + frames] * window[j]
        rows = jnp.swapaxes(framed.astype(jnp.bfloat16), 0, 1).reshape(frames * feeds, NFFT)
        part = jnp.dot(rows, table, preferred_element_type=jnp.float32) * (1.0 / math.sqrt(NFFT))
        part = part.astype(jnp.bfloat16).reshape(frames, feeds, peers, width)
        return jnp.moveaxis(part, 2, 0)
    step = 4
    return pl.pallas_call(
        functools.partial(dft_kernel, frames, feeds),
        grid=(peers // step,),
        out_shape=jax.ShapeDtypeStruct((peers, frames, feeds, width), jnp.bfloat16),
        in_specs=[
            pl.BlockSpec((TAPS, NFFT), lambda i: (0, 0)),
            pl.BlockSpec((feeds, length), lambda i: (0, 0)),
            pl.BlockSpec((NFFT, step * width), lambda i: (0, i)),
        ],
        out_specs=pl.BlockSpec((step, frames, feeds, width), lambda i: (i, 0, 0, 0)),
        scratch_shapes=[pltpu.VMEM((frames * feeds, NFFT), jnp.bfloat16)],
        compiler_params=pltpu.CompilerParams(
            dimension_semantics=("arbitrary",), vmem_limit_bytes=DFT_VMEM * 1024 * 1024
        ),
    )(window, volt, table)


HIT = (TIMES - 1) / (TIMES * TIMES)
MISS = -1.0 / (TIMES * TIMES)


def beam_kernel(start, frames, chans, r_ref, ga_ref, gb_ref, w_ref, e_ref, *rest):
    acc_ref = rest[0] if len(rest) == 6 else None
    out_ref, even_ref, odd_ref, t_ref, p_ref = rest[-5:]
    width = 2 * chans
    lane = lax.broadcasted_iota(jnp.int32, (FEEDS, width), 1)
    sign = jnp.where(lane < chans, 1.0, -1.0)
    low = lax.broadcasted_iota(jnp.int32, (BEAMS, width), 1) < chans

    def calibrate(pair, x_ref):
        for u in range(2):
            i = 2 * pair + u
            volt = r_ref[:, i].reshape(FEEDS, width).astype(jnp.float32)
            cal = volt * ga_ref[...] + pltpu.roll(volt, chans, 1) * gb_ref[...]
            turned = pltpu.roll(cal, chans, 1) * sign
            cols = slice(u * width, (u + 1) * width)
            x_ref[0:FEEDS, cols] = cal.astype(jnp.bfloat16)
            x_ref[FEEDS : 2 * FEEDS, cols] = turned.astype(jnp.bfloat16)
            hit = e_ref[...] == start + i
            rows = pl.ds(pl.multiple_of(i * chans, chans), chans)
            t_ref[rows, :] = jnp.where(hit, HIT, MISS).astype(jnp.bfloat16)

    def form(pair, x_ref):
        beams = jnp.dot(w_ref[...], x_ref[...], preferred_element_type=jnp.float32)
        squares = beams * beams
        one, two = squares[:, :width], squares[:, width:]
        first = one + pltpu.roll(one, chans, 1)
        second = two + pltpu.roll(two, chans, 1)
        power = jnp.where(low, first, second) * (1.0 / FEEDS)
        p_ref[:, pl.ds(pl.multiple_of(pair * width, width), width)] = power.astype(jnp.bfloat16)

    pairs = frames // 2
    calibrate(0, even_ref)

    def body(k, carry):
        form(2 * k, even_ref)
        calibrate(2 * k + 1, odd_ref)
        form(2 * k + 1, odd_ref)
        calibrate(jnp.minimum(2 * k + 2, pairs - 1), even_ref)
        return carry

    lax.fori_loop(0, pairs // 2, body, 0)
    if pairs % 2:
        form(pairs - 1, even_ref)
    part = jnp.dot(p_ref[...], t_ref[...], preferred_element_type=jnp.float32)
    if acc_ref is not None:
        part = part + acc_ref[...]
    out_ref[...] = part.astype(out_ref.dtype)


def beam_stage(received, gains, weights, shift, start, acc):
    _, frames, _, width = received.shape
    chans = width // 2
    last = start + frames == TIMES
    held = jnp.bfloat16 if last else jnp.float32
    if width != LANES:
        volt = jnp.moveaxis(received, 1, 0).reshape(frames, FEEDS, 2, chans).astype(jnp.float32)
        ga, gb = (g.reshape(FEEDS, 2, chans) for g in gains)
        cal = (volt * ga + volt[:, :, ::-1] * gb).astype(jnp.bfloat16)
        turned = jnp.stack([cal[:, :, 1], -cal[:, :, 0]], axis=2)
        both = jnp.concatenate([cal, turned], axis=1)
        beams = jnp.einsum("bf,tfrc->btrc", weights, both, preferred_element_type=jnp.float32)
        power = jnp.sum(beams * beams, axis=2) * (1.0 / FEEDS)
        power = power.astype(jnp.bfloat16).reshape(BEAMS, frames * chans)
        frame = start + jnp.arange(frames, dtype=jnp.int32)[:, None, None]
        spread = jnp.where(shift[None] == frame, HIT, MISS).astype(jnp.bfloat16)
        spread = spread.reshape(frames * chans, -1)
        part = jnp.dot(power, spread, preferred_element_type=jnp.float32)
        return (part if acc is None else part + acc).astype(held)
    series = TRIALS * TIMES
    operands = (received, *gains, weights, shift) + (() if acc is None else (acc,))
    return pl.pallas_call(
        functools.partial(beam_kernel, start, frames, chans),
        out_shape=jax.ShapeDtypeStruct((BEAMS, series), held),
        in_specs=[pl.BlockSpec(memory_space=pltpu.VMEM)] * len(operands),
        out_specs=pl.BlockSpec(memory_space=pltpu.VMEM),
        scratch_shapes=[
            pltpu.VMEM((2 * FEEDS, 2 * width), jnp.bfloat16),
            pltpu.VMEM((2 * FEEDS, 2 * width), jnp.bfloat16),
            pltpu.VMEM((frames * chans, series), jnp.bfloat16),
            pltpu.VMEM((BEAMS, frames * chans), jnp.bfloat16),
        ],
        compiler_params=pltpu.CompilerParams(vmem_limit_bytes=BEAM_VMEM * 1024 * 1024),
    )(*operands)


def local(voltages, gain_table, gain_index, cylinder_map, delays, chan_map):
    feeds = voltages.shape[0]
    grp_count, mem_count = lax.axis_size("grp"), lax.axis_size("mem")
    peers = grp_count * mem_count
    chans = CHANS // peers
    grp, mem = lax.axis_index("grp"), lax.axis_index("mem")

    window = pfb_window(TAPS, NFFT)
    peer = jnp.arange(peers, dtype=jnp.int32)
    base = peer % mem_count * (CHANS // mem_count) + peer // mem_count * chans
    chan_of = base[:, None, None] + jnp.arange(chans, dtype=jnp.int32)[None, None, :]
    quarter = jnp.arange(2, dtype=jnp.int32)[None, :, None]
    chan_of, quarter = (
        jnp.broadcast_to(v, (peers, 2, chans)).reshape(-1) for v in (chan_of, quarter)
    )
    table = channel_table(chan_of, quarter)

    table = lax.optimization_barrier(table)
    starts = [sum(CHUNKS[:i]) for i in range(len(CHUNKS))]

    def exchange(spectra):
        return lax.all_to_all(spectra, PEERS, split_axis=0, concat_axis=0, tiled=True)

    spectra = [
        dft_stage(voltages, window, table, start, frames, peers)
        for start, frames in zip(starts, CHUNKS)
    ]
    received = [exchange(block) for block in spectra[:-1]]

    pairs = lax.axis_size("pair")
    cores = 2 if grp_count % 2 == 0 else 1
    owned = BEAMS // (pairs * peers)
    weights = beam_weights(cylinder_map)
    weights = weights.reshape(pairs, grp_count // cores, cores, mem_count * owned, 2 * FEEDS)
    weights = jnp.moveaxis(weights, 2, 0).reshape(BEAMS, 2 * FEEDS)
    gain_here = lax.dynamic_slice_in_dim(gain_table, grp * chans, chans, 2)
    gain_rows = gain_index[:, lax.axis_index("pair")]
    pick = gain_rows[:, None] == jnp.arange(gain_table.shape[0], dtype=jnp.int32)[None, :]
    gain_values = jnp.dot(
        pick.astype(jnp.float32),
        gain_here.reshape(gain_table.shape[0], 2 * chans),
        precision=lax.Precision.HIGHEST,
    )
    gain_real, gain_imag = gain_values[:, :chans], gain_values[:, chans:]
    gains = (
        jnp.concatenate([gain_real, gain_real], axis=1),
        jnp.concatenate([-gain_imag, gain_imag], axis=1),
    )

    first = mem * (CHANS // mem_count) + grp * chans
    freq = lax.dynamic_slice_in_dim(chan_map, first, chans, 0)
    column = jnp.arange(CHANS, dtype=jnp.int32)[:, None] == freq[None, :]
    delay = jnp.dot(
        delays.astype(jnp.bfloat16), column.astype(jnp.bfloat16), preferred_element_type=jnp.float32
    ).astype(jnp.int32)
    frame = jnp.arange(TIMES, dtype=jnp.int32)[None, None, :]
    shift = ((frame - delay.T[:, :, None]) % TIMES).reshape(chans, TRIALS * TIMES)

    part = None
    for i, start in enumerate(starts):
        if i == len(starts) - 1:
            last, part = lax.optimization_barrier((spectra[-1], held))
            received.append(exchange(last))
            part = beam_stage(received[i - 1], gains, weights, shift, starts[i - 1], part)
        if i == len(starts) - 2:
            held = part
            continue
        part = beam_stage(received[i], gains, weights, shift, start, part)

    series = TRIALS * TIMES
    groups = [[x * cores + c for c in range(cores)] for x in range(grp_count // cores)]
    part = part.reshape(cores, BEAMS // cores, series)
    part = lax.all_to_all(
        part, "grp", split_axis=0, concat_axis=0, axis_index_groups=groups, tiled=True
    )
    part = jnp.sum(part.astype(jnp.float32), axis=0).astype(jnp.bfloat16)
    part = part.reshape(pairs * peers // cores, owned, series)
    groups = [
        [
            (p * grp_count + x * cores + c) * mem_count + m
            for p in range(pairs)
            for x in range(grp_count // cores)
            for m in range(mem_count)
        ]
        for c in range(cores)
    ]
    part = lax.all_to_all(
        part, ("pair",) + PEERS, split_axis=0, concat_axis=0, axis_index_groups=groups, tiled=True
    )
    series = jnp.sum(part.astype(jnp.float32), axis=0)
    return series.reshape(1, owned, TRIALS, TIMES)

GROUP = 4
STEP = 2
AHEAD = 1
WINDOW = 2
FUSED_VMEM = 62


def wave(index, length):
    angles = (index & (length - 1)).astype(jnp.float32) * (2.0 * math.pi / length)
    return jnp.cos(angles), jnp.sin(angles)


def iota(shape, axis):
    return lax.broadcasted_iota(jnp.int32, shape, axis)


def fill_window(window_ref):
    shape = (TAPS, NFFT)
    offsets = (iota(shape, 0) * NFFT + iota(shape, 1)).astype(jnp.float32) + 0.5
    arg = (offsets - TAPS * NFFT / 2.0) / NFFT * math.pi
    taper = 0.5 - 0.5 * jnp.cos(offsets * (2.0 * math.pi / (TAPS * NFFT)))
    window_ref[...] = jnp.sin(arg) / arg * taper


def fill_waves(wave_ref, cores, chans):
    shape = (8, cores * LANES)
    lane = iota(shape, 1)
    chan = lane // LANES * chans + lane % chans
    quarter = lane % LANES // chans * (NFFT // 4)
    start = wave(iota(shape, 0) * chan + quarter, NFFT)
    wave_ref[0, 0:8, :], wave_ref[1, 0:8, :] = start
    step = 8
    while step < NFFT:
        turn_real, turn_imag = (v[None] for v in wave(chan * step, NFFT))
        real, imag = (wave_ref[r, 0:step, :].reshape(step // 8, *shape) for r in range(2))
        rows = slice(step, 2 * step)
        wave_ref[0, rows, :] = (real * turn_real - imag * turn_imag).reshape(step, shape[1])
        wave_ref[1, rows, :] = (real * turn_imag + imag * turn_real).reshape(step, shape[1])
        step *= 2


def fill_table(table_ref, wave_ref, chip, first):
    period = NFFT // LANES
    shape = (period, table_ref.shape[2])
    turn_real, turn_imag = (v[None] for v in wave(iota(shape, 0) * (first // LANES), period))
    block = 256

    def part(i, carry):
        rows = pl.ds(pl.multiple_of(i * block, block), block)
        real, imag = (wave_ref[r, rows, :].reshape(block // period, *shape) for r in range(2))
        filled = (real * turn_real - imag * turn_imag).reshape(block, shape[1])
        table_ref[chip, rows, :] = filled.astype(jnp.bfloat16)
        return carry

    lax.fori_loop(0, NFFT // block, part, 0)


def fill_gains(gains_ref, gain_table_ref, gain_index_ref, grp, pair):
    rows, _, held = gain_table_ref.shape
    chans = LANES // 2
    low = iota((rows, held), 1) < chans

    def twice(values):
        values = pltpu.roll(values, (held - grp * chans) % held, 1)
        return jnp.where(low, values, pltpu.roll(values, chans, 1))[:, :LANES]

    real = twice(gain_table_ref[:, 0, :])
    imag = twice(gain_table_ref[:, 1, :])
    imag = jnp.where(low[:, :LANES], -imag, imag)
    left = jnp.concatenate([real, imag], axis=1)
    index = gain_index_ref[pl.ds(pair, 1), :]
    pick = jnp.where(iota((rows, index.shape[1]), 0) == index, 1.0, 0.0).astype(jnp.bfloat16)
    total = None
    for _ in range(3):
        term = left.astype(jnp.bfloat16)
        left = left - term.astype(jnp.float32)
        picked = lax.dot_general(
            pick, term, (((0,), (0,)), ((), ())), preferred_element_type=jnp.float32
        )
        total = picked if total is None else total + picked
    gains_ref[...] = total


def fill_shifts(shift_ref, final_ref, delays_ref, chan_map_ref, mem):
    held, series = shift_ref.shape
    known = delays_ref[...].astype(jnp.float32).astype(jnp.bfloat16)
    shape = (TRIALS, series)
    spread = jnp.where(iota(shape, 1) // TIMES == iota(shape, 0), 1.0, 0.0).astype(jnp.bfloat16)
    frame = (iota((held, series), 1) % TIMES).astype(jnp.float32)

    def some(m, carry):
        rows = pl.ds(pl.multiple_of(m * held, held), held)
        column = jnp.where(iota((CHANS, held), 0) == chan_map_ref[:, rows], 1.0, 0.0)
        delay = jnp.dot(known, column.astype(jnp.bfloat16), preferred_element_type=jnp.float32)
        late = lax.dot_general(
            delay.astype(jnp.bfloat16),
            spread,
            (((0,), (0,)), ((), ())),
            preferred_element_type=jnp.float32,
        )
        shift = frame - late
        shift = jnp.where(shift < 0.0, shift + TIMES, shift)
        hit = shift == float(TIMES - 1)
        final_ref[rows, :] = jnp.where(hit, HIT, MISS).astype(jnp.bfloat16)

        @pl.when(m == mem)
        def _():
            shift_ref[...] = shift

        return carry

    lax.fori_loop(0, CHANS // held, some, 0)


def fill_weights(w_ref, hit_ref, upper_ref, cylinder_ref):
    block = 128

    def mark(i, carry):
        at = pl.multiple_of(i * block, block)
        hit = iota((block, FEEDS), 0) + at == cylinder_ref[...]
        hit_ref[pl.ds(at, block), :] = jnp.where(hit, 1.0, 0.0).astype(jnp.bfloat16)
        return carry

    lax.fori_loop(0, FEEDS // block, mark, 0)
    shape = (8, FEEDS)
    row, slot = iota(shape, 0), iota(shape, 1)
    digit = jnp.where(row == 0, slot // NS, jnp.where(row == 1, slot % NS // 16, slot % 16))
    digit = digit.astype(jnp.float32).astype(jnp.bfloat16)
    found = lax.dot_general(
        digit, hit_ref[...], (((1,), (1,)), ((), ())), preferred_element_type=jnp.float32
    )
    cyl = found[0:1].astype(jnp.int32)
    pos = (found[1:2] * 16.0 + found[2:3]).astype(jnp.int32)
    shape = (CYL * 16, FEEDS)
    row = iota(shape, 0)
    upper = wave(16 * pos * (row % 16) + (NS // CYL) * cyl * (row // 16), NS)
    upper_ref[0], upper_ref[1] = upper
    shape = (8, FEEDS)
    lower = [wave(pos * (2 * iota(shape, 0) + a), NS) for a in range(2)]

    def pack(i, carry):
        for a in range(2):
            parts = [[], []]
            for v in range(2):
                at = pl.ds(i * 2 + v, 1)
                real, imag = times((upper_ref[0, at, :], upper_ref[1, at, :]), lower[a])
                parts[0].append(real)
                parts[1].append(imag)
            rows = pl.ds(pl.multiple_of(a * (BEAMS // 2) + i * 16, 16), 16)
            for r in range(2):
                both = jnp.concatenate(parts[r], axis=0).astype(jnp.bfloat16)
                w_ref[rows, r * FEEDS : (r + 1) * FEEDS] = both
        return carry

    lax.fori_loop(0, CYL * 16 // 2, pack, 0)


def fused_kernel(
    sizes, gain_table_ref, gain_index_ref, cylinder_ref, delays_ref, chan_map_ref, volt_hbm, out_ref,
    volt_ref, table_ref, w_ref, framed_ref, send_ref, recv_ref, x_ref, psend_ref, precv_ref,
    t_ref, lhs_ref, acc_ref, zsend_ref, zrecv_ref,
    window_ref, wave_ref, gains_ref, shift_ref, hit_ref, upper_ref, part_ref, parts_ref,
    head_sem, volt_sem, send_sem, recv_sem, own_sem,
    psend_sem, precv_sem, pown_sem, zsend_sem, zrecv_sem, lsend_sem, lrecv_sem,
):
    grp_count, mem_count, pairs, cores = sizes
    peers = grp_count * mem_count
    chips = peers // cores
    feeds = volt_hbm.shape[0]
    chans = LANES // 2
    width = LANES
    chunks = TIMES // GROUP
    steps = GROUP // STEP
    last = TIMES // STEP - 1
    grp, mem, pair = (lax.axis_index(n) for n in ("grp", "mem", "pair"))
    me = grp * mem_count + mem
    across = pair * grp_count + grp
    MESH = pl.DeviceIdType.MESH

    def load(src, dst, sem):
        return pltpu.make_async_copy(src, dst, sem)

    head = (TAPS - 1) * NFFT
    load(volt_hbm.at[:, 0:head], volt_ref.at[:, 0:head], head_sem).start()

    def volt_copy(k):
        cols = pl.ds(pl.multiple_of(head + k * (GROUP * NFFT), NFFT), GROUP * NFFT)
        return load(volt_hbm.at[:, cols], volt_ref.at[:, cols], volt_sem.at[k])

    for k in range(chunks):
        volt_copy(k).start()

    barrier = pltpu.get_barrier_semaphore()
    met = 0
    for dg in range(grp_count):
        for dm in range(mem_count):
            for dp in range(pairs):
                if (dg, dm, dp) == (0, 0, 0) or (dm != 0 and dp != 0):
                    continue
                there = {
                    "grp": (grp + dg) % grp_count,
                    "mem": (mem + dm) % mem_count,
                    "pair": (pair + dp) % pairs,
                }
                pl.semaphore_signal(barrier, inc=1, device_id=there, device_id_type=MESH)
                met += 1
    acc_ref[...] = jnp.zeros_like(acc_ref)
    fill_window(window_ref)
    fill_waves(wave_ref, cores, chans)
    load(volt_hbm.at[:, 0:head], volt_ref.at[:, 0:head], head_sem).wait()

    def spectra_copy(q, at, g, m):
        peer = g * mem_count + m
        return pltpu.make_async_remote_copy(
            src_ref=send_ref.at[(at[0], peer) + at[1:]],
            dst_ref=recv_ref.at[(at[0], me) + at[1:]],
            send_sem=send_sem.at[q],
            recv_sem=recv_sem.at[q],
            device_id={"grp": g, "mem": m},
            device_id_type=MESH,
        )

    def own_copy(q, at):
        own = (at[0], me) + at[1:]
        return load(send_ref.at[own], recv_ref.at[own], own_sem.at[q])

    def post(q, at, g, m):
        own = jnp.logical_and(g == grp, m == mem)

        @pl.when(jnp.logical_not(own))
        def _():
            spectra_copy(q, at, g, m).start()

        @pl.when(own)
        def _():
            own_copy(q, at).start()

    def place(s):
        h = s // 2
        one, two = (3 - h) // 3, h % 3 % 2
        one, two = one + (two - one) * (grp % cores), two + (one - two) * (grp % cores)
        far = (3 - mem) * one + (mem + 2) % 4 * two
        near = (mem + 1 - 2 * (mem % 2)) * (h % 3 // 2) + mem * (h // 3)
        return (x_here + s + 1) % 2, far + near

    def post_all(q, at):
        def some(s, carry):
            x, m = place(s)
            for c in range(cores):
                post(q, at, x * cores + (grp + c) % cores, m)
            return carry

        lax.fori_loop(0, chips, some, 0)

    x_here = grp // cores

    def dft(k):
        volt_copy(k).wait()
        for t in range(GROUP):
            def tap(j):
                at = pl.multiple_of((k * GROUP + t + j) * NFFT, NFFT)
                return volt_ref[:, pl.ds(at, NFFT)].astype(jnp.float32) * window_ref[j : j + 1, :]

            total = tap(0)
            for j in range(1, TAPS):
                total = total + tap(j)
            framed_ref[t * feeds : (t + 1) * feeds, :] = total.astype(jnp.bfloat16)

        def tile(s, carry):
            x, m = place(s)
            chip = x * mem_count + m

            @pl.when(k == 0)
            def _():
                first = m * (CHANS // mem_count) + x * (cores * chans)
                fill_table(table_ref, wave_ref, chip, first)

            part = jnp.dot(framed_ref[...], table_ref[chip], preferred_element_type=jnp.float32)
            part = (part * (1.0 / math.sqrt(NFFT))).astype(jnp.bfloat16)
            for c in range(cores):
                peer = (x * cores + c) * mem_count + m
                for u in range(steps):
                    rows = part[u * STEP * feeds : (u + 1) * STEP * feeds, c * width : (c + 1) * width]
                    send_ref[k * steps + u, peer] = rows.reshape(STEP, feeds, width)

            @pl.when(jnp.logical_and(k == 0, s == 0))
            def _():
                pl.semaphore_wait(barrier, met)

            @pl.when(k == 0)
            def _():
                for c in range(cores):
                    for u in range(steps):
                        post(u, (u,), x * cores + c, m)

            return carry

        lax.fori_loop(0, chips, tile, 0)

    lane = lax.broadcasted_iota(jnp.int32, (FEEDS, width), 1)
    sign = jnp.where(lane < chans, 1.0, -1.0)
    rows_each = BEAMS // (pairs * grp_count)
    half = BEAMS // pairs
    low = iota((half, width), 1) < chans
    owned = rows_each // mem_count

    def arrived(q, at):
        others = recv_ref.at[(at[0], pl.ds(0, peers - 1)) + at[1:]]
        return load(others, others, recv_sem.at[q])

    def left(q, at):
        others = send_ref.at[(at[0], pl.ds(0, peers - 1)) + at[1:]]
        return load(others, others, send_sem.at[q])

    others_count = pairs * grp_count - 1

    def power_copy(q, src, dst, p, g):
        return pltpu.make_async_remote_copy(
            src_ref=src,
            dst_ref=dst,
            send_sem=psend_sem.at[q],
            recv_sem=precv_sem.at[q],
            device_id={"pair": p, "grp": g},
            device_id_type=MESH,
        )

    def power_from(q, d, u, single):
        size = rows_each // 2 if single else rows_each
        at = u * (half if single else 0) + d * size
        return psend_ref.at[q, pl.ds(pl.multiple_of(at, size), size)]

    def power_to(q, src, u, single):
        size = rows_each // 2 if single else rows_each
        return precv_ref.at[q, src, pl.ds(u * size, size)]

    def power_own(q, u, single):
        src, dst = power_from(q, across, u, single), power_to(q, across, u, single)
        return load(src, dst, pown_sem.at[q + u])

    def power_arrived(q, u, single):
        others = power_to(q, pl.ds(0, others_count), u, single)
        return load(others, others, precv_sem.at[q + u])

    def power_left(q, u, single):
        others = power_to(q, pl.ds(0, others_count), u, single)
        return load(others, others, psend_sem.at[q + u])

    def calibrate(q, u, col):
        volt = recv_ref[q, :, u].reshape(FEEDS, width).astype(jnp.float32)
        cal = volt * gains_ref[:, :width] + pltpu.roll(volt, chans, 1) * gains_ref[:, width:]
        turned = pltpu.roll(cal, chans, 1) * sign
        x_ref[0:FEEDS, col : col + width] = cal.astype(jnp.bfloat16)
        x_ref[FEEDS : 2 * FEEDS, col : col + width] = turned.astype(jnp.bfloat16)

    def send_powers(q, u, p, single):
        for dg in range(grp_count - 1, -1, -1):
            g = (grp + dg) % grp_count
            here = jnp.logical_and(p == pair, g == grp)

            def go():
                src = power_from(q, p * grp_count + g, u, single)
                power_copy(q + u, src, power_to(q, across, u, single), p, g).start()

            if dg:
                go()
            else:
                pl.when(jnp.logical_not(here))(go)

                @pl.when(here)
                def _():
                    power_own(q, u, single).start()

    def beams(q):
        arrived(q, (q,)).wait()
        own_copy(q, (q,)).wait()
        for u in range(STEP):
            calibrate(q, u, u * width)

        def some(h, carry):
            p = (pair + 1 + h) % pairs
            rows = pl.ds(pl.multiple_of(p * half, half), half)
            formed = jnp.dot(w_ref[rows, :], x_ref[...], preferred_element_type=jnp.float32)
            squares = formed * formed
            one, two = squares[:, :width], squares[:, width:]
            first = one + pltpu.roll(one, chans, 1)
            second = two + pltpu.roll(two, chans, 1)
            power = jnp.where(low, first, second) * (1.0 / FEEDS)
            psend_ref[q, rows, :] = power.astype(jnp.bfloat16)
            send_powers(q, 0, p, False)
            return carry

        lax.fori_loop(0, pairs, some, 0)

    def beams_single(u):
        arrived(last + u, (last, u)).wait()
        own_copy(last + u, (last, u)).wait()
        calibrate(last, u, 0)

        def some(h, carry):
            p = (pair + 1 + h) % pairs
            rows = pl.ds(pl.multiple_of(p * half, half), half)
            formed = jnp.dot(
                w_ref[rows, :], x_ref[:, :width], preferred_element_type=jnp.float32
            )
            squares = formed * formed
            power = (squares + pltpu.roll(squares, chans, 1)) * (1.0 / FEEDS)
            power = power.reshape(grp_count, 2, rows_each // 2, width)
            lower = low[: rows_each // 2][None]
            power = jnp.where(lower, power[:, 0], power[:, 1]).reshape(half // 2, width)
            at = u * half + p * (half // 2)
            psend_ref[last, pl.ds(pl.multiple_of(at, half // 2), half // 2), :] = power.astype(
                jnp.bfloat16
            )
            send_powers(last, u, p, True)
            return carry

        lax.fori_loop(0, pairs, some, 0)

    def summed(q, s, rows):
        both = precv_ref[q, s, rows].astype(jnp.float32)
        for p in range(1, pairs):
            both = both + precv_ref[q, p * grp_count + s, rows].astype(jnp.float32)
        return both

    def dedisperse(q):
        for s in range(grp_count):
            for u in range(STEP):
                frame = (q * STEP + u).astype(jnp.float32)
                hit = shift_ref[s * chans : (s + 1) * chans, :] == frame
                at = (s * STEP + u) * chans
                t_ref[at : at + chans, :] = jnp.where(hit, HIT, MISS).astype(jnp.bfloat16)
        power_arrived(q, 0, False).wait()
        power_own(q, 0, False).wait()
        for s in range(grp_count):
            both = summed(q, s, slice(None))
            lhs_ref[:, s * width : (s + 1) * width] = both.astype(jnp.bfloat16)
        acc_ref[...] += jnp.dot(lhs_ref[...], t_ref[...], preferred_element_type=jnp.float32)

    def gather_single(u, into_ref):
        power_arrived(last, u, True).wait()
        power_own(last, u, True).wait()
        size = rows_each // 2
        lower = low[:size]
        for s in range(0, grp_count, 2):
            a, b = (summed(last, v, slice(u * size, (u + 1) * size)) for v in (s, s + 1))
            top = jnp.where(lower, a, pltpu.roll(b, chans, 1))
            bottom = jnp.where(lower, pltpu.roll(a, chans, 1), b)
            cols = slice(s * chans, (s + 2) * chans)
            into_ref[0:size, cols] = top.astype(jnp.bfloat16)
            into_ref[size : 2 * size, cols] = bottom.astype(jnp.bfloat16)

    def body(i, carry):
        j = i - AHEAD * steps
        ready = j + WINDOW

        @pl.when(jnp.logical_and(i % steps == 0, i // steps < chunks))
        def _():
            dft(i // steps)

        @pl.when(jnp.logical_and(ready >= steps, ready < last))
        def _():
            post_all(ready, (ready,))

        @pl.when(jnp.logical_and(ready >= last, ready < last + STEP))
        def _():
            post_all(ready, (last, ready - last))

        @pl.when(j == 0)
        def _():
            fill_gains(gains_ref, gain_table_ref, gain_index_ref, grp, pair)
            fill_weights(w_ref, hit_ref, upper_ref, cylinder_ref)
            fill_shifts(shift_ref, hit_ref, delays_ref, chan_map_ref, mem)

        @pl.when(j >= 2)
        def _():
            dedisperse(j - 2)

        @pl.when(jnp.logical_and(j >= 0, j < last))
        def _():
            beams(j)

        @pl.when(jnp.logical_and(j >= last, j < last + STEP - 1))
        def _():
            beams_single(j - last)

        return carry

    def owned_rows(m):
        return pl.ds(pl.multiple_of(m * owned, owned), owned)

    def z_copy(d):
        m = (mem + d) % mem_count
        return pltpu.make_async_remote_copy(
            src_ref=zsend_ref.at[owned_rows(m)],
            dst_ref=zrecv_ref.at[d - 1],
            send_sem=zsend_sem.at[d - 1],
            recv_sem=zrecv_sem.at[d - 1],
            device_id={"mem": m},
            device_id_type=MESH,
        )

    def part_copy(u, d):
        m = (mem + d) % mem_count
        at = u * (mem_count - 1) + d - 1
        return pltpu.make_async_remote_copy(
            src_ref=part_ref.at[u, owned_rows(m)],
            dst_ref=parts_ref.at[u, mem],
            send_sem=lsend_sem.at[at],
            recv_sem=lrecv_sem.at[at],
            device_id={"mem": m},
            device_id_type=MESH,
        )

    order = sorted(range(1, mem_count), key=lambda d: abs(d - mem_count // 2))

    def share(u):
        gather_single(u, part_ref.at[u])
        for d in order:
            part_copy(u, d).start()
        parts_ref[u, mem] = part_ref[u, owned_rows(mem), :]

    def finish(u):
        held = CHANS // mem_count
        done = None
        for d in (0, *order):
            if d:
                part_copy(u, d).wait()
            m = (mem + mem_count - d) % mem_count
            rows = pl.ds(pl.multiple_of(m * held, held), held)
            more = jnp.dot(
                parts_ref[u, m], hit_ref[rows, :], preferred_element_type=jnp.float32
            )
            done = more if done is None else done + more
        return done

    def drain(q, carry):
        left(q, (q,)).wait()
        power_left(q, 0, False).wait()
        return carry

    lax.fori_loop(0, AHEAD * steps + last + STEP - 1, body, 0)
    for q in range(last - 1, last):
        dedisperse(jnp.int32(q))
    zsend_ref[...] = acc_ref[...].astype(jnp.bfloat16)
    for d in order:
        z_copy(d).start()
    beams_single(STEP - 1)
    share(0)
    lax.fori_loop(0, last, drain, 0)
    share(1)
    for u in range(STEP):
        left(last + u, (last, u)).wait()
        power_left(last, u, True).wait()
    total = acc_ref[owned_rows(mem), :]
    for d in order:
        z_copy(d).wait()
        total = total + zrecv_ref[d - 1].astype(jnp.float32)
    before = finish(0)
    series = before.shape[1]
    time = iota(before.shape, 1) % TIMES
    wrapped = pltpu.roll(before, TIMES - 1, 1)
    total = total + jnp.where(time == TIMES - 1, wrapped, pltpu.roll(before, series - 1, 1))
    total = total + finish(1)
    out_ref[...] = total


def fused_stage(sizes, gain_table, gain_index, cylinder_map, delays, chan_map, voltages):
    grp_count, mem_count, pairs, cores = sizes
    peers = grp_count * mem_count
    chips = peers // cores
    feeds, samples = voltages.shape
    series = TRIALS * TIMES
    count = TIMES // STEP
    groups = pairs * grp_count
    rows_each = BEAMS // groups
    owned = rows_each // mem_count
    bf16, f32 = jnp.bfloat16, jnp.float32
    dma = pltpu.SemaphoreType.DMA
    vmem = pl.BlockSpec(memory_space=pltpu.VMEM)
    return pl.pallas_call(
        functools.partial(fused_kernel, sizes),
        out_shape=jax.ShapeDtypeStruct((owned, series), f32),
        in_specs=[vmem] * 5 + [pl.BlockSpec(memory_space=pl.ANY)],
        out_specs=vmem,
        scratch_shapes=[
            pltpu.VMEM((feeds, samples), bf16),
            pltpu.VMEM((chips, NFFT, cores * LANES), bf16),
            pltpu.VMEM((BEAMS, 2 * FEEDS), bf16),
            pltpu.VMEM((GROUP * feeds, NFFT), bf16),
            pltpu.VMEM((count, peers, STEP, feeds, LANES), bf16),
            pltpu.VMEM((count, peers, STEP, feeds, LANES), bf16),
            pltpu.VMEM((2 * FEEDS, STEP * LANES), bf16),
            pltpu.VMEM((count, BEAMS, LANES), bf16),
            pltpu.VMEM((count, groups, rows_each, LANES), bf16),
            pltpu.VMEM((grp_count * LANES, series), bf16),
            pltpu.VMEM((rows_each, grp_count * LANES), bf16),
            pltpu.VMEM((rows_each, series), f32),
            pltpu.VMEM((rows_each, series), bf16),
            pltpu.VMEM((mem_count - 1, owned, series), bf16),
            pltpu.VMEM((TAPS, NFFT), f32),
            pltpu.VMEM((2, NFFT, cores * LANES), f32),
            pltpu.VMEM((FEEDS, 2 * LANES), f32),
            pltpu.VMEM((CHANS // mem_count, series), f32),
            pltpu.VMEM((FEEDS, FEEDS), bf16),
            pltpu.VMEM((2, CYL * 16, FEEDS), f32),
            pltpu.VMEM((STEP, rows_each, CHANS // mem_count), bf16),
            pltpu.VMEM((STEP, mem_count, owned, CHANS // mem_count), bf16),
            dma,
            dma((TIMES // GROUP,)),
            *[dma((count - 1 + STEP,))] * 6,
            *[dma((mem_count - 1,))] * 2,
            *[dma((STEP * (mem_count - 1),))] * 2,
        ],
        compiler_params=pltpu.CompilerParams(
            collective_id=0, has_side_effects=True, vmem_limit_bytes=FUSED_VMEM * 1024 * 1024
        ),
    )(gain_table, gain_index, cylinder_map, delays, chan_map, voltages)


def local_fused(voltages, gain_table, gain_index, cylinder_map, delays, chan_map):
    feeds, _, samples = voltages.shape
    sizes = (lax.axis_size("grp"), lax.axis_size("mem"), lax.axis_size("pair"), 2)
    series = fused_stage(
        sizes,
        gain_table,
        gain_index.T,
        cylinder_map.reshape(1, FEEDS),
        delays,
        chan_map.reshape(1, CHANS),
        voltages.reshape(feeds, samples),
    )
    return series.reshape(1, -1, TRIALS, TIMES)


def solution(mesh):
    shape = (mesh.shape["grp"], mesh.shape["mem"], mesh.shape["pair"])
    return jax.shard_map(
        local_fused if shape == (4, 4, 2) else local,
        mesh=mesh,
        in_specs=(P(PEERS, "pair", None), P(None, None, "mem"), P(), P(), P(), P()),
        out_specs=P("pair", PEERS, None, None),
        check_vma=False,
    )
```
